256 devices in a mesh: inst: 16 (over x, y), page: 8 (over z), head: 2 (over core).
Axes of the slice: x: 4, y: 4, z: 8, core: 2. Of those that a mesh axis runs over, the one named last changes fastest.
Arguments:
- queries: bfloat16 [32, 8192], P('inst', 'head'), may hold values from -21 to 21
- fresh_key_value: bfloat16 [2, 32, 1024], P(None, 'inst', 'head'), may hold values from -8 to 8
- key_value_pool: bfloat16 [2, 16384, 16, 1024], P(None, ('inst', 'page'), None, 'head'), may hold values from -21 to 21
- block_table: int32 [32, 768], P('inst'), may hold values from -1 to 16383, as said below
- lengths: int32 [32], P('inst'), may hold values from 17 to 12288, as said below
Outputs:
- attn: bfloat16 [32, 8192], P('inst', 'head')
The draws below stay inside these ranges and needn't reach their ends.
Inputs may be any that keep to these rules, and one draw needn't show every extreme that they name: `block_table`: request r is owned by instance r // 2. Entries 0 to ceil(lengths[r] / 16) - 1 of row r are pool page numbers below 16384, distinct over all requests; every other entry is -1. `lengths`: every request has two or more pages; some request has exactly 768 full pages.
All inputs are finite; a program needn't handle non-finite values.
Results may differ from the reference program's by a relative error of at most 0.001.
Values may be sent and summed in bfloat16 or wider, within the bound.
No kernel may reach another device: no remote copies, remote signals or barrier semaphores. Data moves between devices by JAX's collectives and lax.ppermute only.
A program may use at most 192 MiB of HBM per device.

```python
import math
import jax
import jax.numpy as jnp
from jax import lax

QUERY_HEADS = 64
KEY_VALUE_HEADS = 8
HEAD_SIZE = 128
PAGE_TOKENS = 16
REQUEST_COUNT = 32
POOL_PAGES = 16384
REQUEST_PAGES = 768


def draw_plan(key):
    plan_key = jax.random.fold_in(key, 11)
    count_key = jax.random.fold_in(plan_key, 1)
    pick_key = jax.random.fold_in(plan_key, 2)
    fill_key = jax.random.fold_in(plan_key, 3)
    shuffle_key = jax.random.fold_in(plan_key, 4)
    request_ids = jnp.arange(REQUEST_COUNT, dtype=jnp.int32)
    page_count = jax.random.randint(count_key, (REQUEST_COUNT,), REQUEST_PAGES // 4, REQUEST_PAGES // 2 + 1)
    longest = jax.random.randint(pick_key, (), 0, REQUEST_COUNT)
    page_count = jnp.where(request_ids == longest, REQUEST_PAGES, page_count)
    last_fill = jax.random.randint(fill_key, (REQUEST_COUNT,), 1, PAGE_TOKENS + 1)
    last_fill = jnp.where(request_ids == longest, PAGE_TOKENS, last_fill)
    token_count = (page_count - 1) * PAGE_TOKENS + last_fill
    shuffled = jax.random.permutation(shuffle_key, POOL_PAGES).astype(jnp.int32)
    first_slot = jnp.cumsum(page_count) - page_count
    column = jnp.arange(REQUEST_PAGES, dtype=jnp.int32)
    position = jnp.minimum(first_slot[:, None] + column[None, :], POOL_PAGES - 1)
    page_table = jnp.where(column[None, :] < page_count[:, None], shuffled[position], -1)
    return (token_count.astype(jnp.int32), page_table.astype(jnp.int32))


def query_outputs(key):
    query_key = jax.random.fold_in(key, 23)
    return jnp.clip(3.0 * jax.random.normal(query_key, (REQUEST_COUNT, QUERY_HEADS, HEAD_SIZE), jnp.float32), -18.0, 18.0)


def draw_lengths(key, part):
    token_count, _ = draw_plan(key)
    return token_count


def draw_block_table(key, part):
    _, page_table = draw_plan(key)
    return page_table


def draw_queries(key, part):
    return query_outputs(key).reshape(REQUEST_COUNT, QUERY_HEADS * HEAD_SIZE).astype(jnp.bfloat16)


def draw_key_value_pool(key, part):
    pool_key = jax.random.fold_in(key, 37)
    pool_dimensions = (2, POOL_PAGES, PAGE_TOKENS, KEY_VALUE_HEADS * HEAD_SIZE)
    value_rows = jnp.clip(jax.random.normal(pool_key, pool_dimensions, jnp.float32), -6.0, 6.0)
    return value_rows.astype(jnp.bfloat16)


def level_of(key, dims, pieces, least, top_value):
    def one(dim, blocks):
        steps = jax.random.uniform(jax.random.fold_in(jax.random.fold_in(key, 6), dim), (blocks,), jnp.float32, least / len(pieces), top_value / len(pieces))
        return jnp.repeat(jnp.exp(steps), dims[dim] // blocks).reshape((-1,) + (1,) * (len(dims) - dim - 1))

    factor_of = one(*pieces[0])
    for cut in pieces[1:]:
        factor_of = factor_of * one(*cut)
    return factor_of


def centred(own_key, dims, scale, limit, cuts=(), kind=jnp.bfloat16):
    values = scale * jax.random.normal(own_key, dims, jnp.float32)
    if cuts:
        values = values * level_of(own_key, dims, cuts, -0.22, 0.18)
    return jnp.clip(values, -limit, limit).astype(kind)


def setup_inputs(seed: int = 0) -> dict:
    splits = jax.random.split(jax.random.key(seed), 6)
    queries = draw_queries(jax.random.fold_in(splits[5], 71), 0)
    fresh_key_value = centred(splits[1], (2, REQUEST_COUNT, KEY_VALUE_HEADS * HEAD_SIZE), 2.0, 8.0, ((1, 16), (2, 2)))
    key_value_pool = draw_key_value_pool(jax.random.fold_in(splits[5], 71), 0)
    block_table = draw_block_table(jax.random.fold_in(splits[5], 71), 0)
    lengths = draw_lengths(jax.random.fold_in(splits[5], 71), 0)
    return dict(queries=queries, fresh_key_value=fresh_key_value, key_value_pool=key_value_pool, block_table=block_table, lengths=lengths)


LOWEST_SCORE = -1e+30

def reference(queries, fresh_key_value, key_value_pool, block_table, lengths):
    inverse_sqrt_scale = 1.0 / math.sqrt(HEAD_SIZE)
    columns = jnp.arange(REQUEST_PAGES, dtype=jnp.int32)
    offsets = jnp.arange(PAGE_TOKENS, dtype=jnp.int32)

    def one_request(inputs):
        single_query, fresh_key, fresh_value, table_row, length = inputs
        live_page = columns * PAGE_TOKENS < length
        page_indices = jnp.where(live_page, table_row, 0).astype(jnp.int32)
        paged_keys = key_value_pool[0, page_indices].astype(jnp.float32).reshape(REQUEST_PAGES, PAGE_TOKENS, KEY_VALUE_HEADS, HEAD_SIZE)
        paged_values = key_value_pool[1, page_indices].astype(jnp.float32).reshape(REQUEST_PAGES, PAGE_TOKENS, KEY_VALUE_HEADS, HEAD_SIZE)
        grouped_queries = single_query.astype(jnp.float32).reshape(KEY_VALUE_HEADS, QUERY_HEADS // KEY_VALUE_HEADS, HEAD_SIZE)
        scores = jnp.einsum('gqd,stgd->sgqt', grouped_queries, paged_keys) * inverse_sqrt_scale
        valid = columns[:, None] * PAGE_TOKENS + offsets[None, :] < length
        valid = valid[:, None, None, :]
        masked = jnp.where(valid, scores, LOWEST_SCORE)
        page_max = lax.optimization_barrier(jnp.max(masked, axis=3))
        raw_weight = jnp.where(valid, jnp.exp(masked - page_max[..., None]), 0.0)
        page_sum = lax.optimization_barrier(jnp.sum(raw_weight, axis=3))
        rounded = lax.optimization_barrier(raw_weight.astype(jnp.bfloat16))
        page_out = jnp.einsum('sgqt,stgd->sgqd', rounded.astype(jnp.float32), paged_values)
        fresh_score = jnp.einsum('sxh,sh->sx', grouped_queries, fresh_key.astype(jnp.float32).reshape(KEY_VALUE_HEADS, HEAD_SIZE)) * inverse_sqrt_scale
        top_score = jnp.maximum(lax.optimization_barrier(jnp.max(page_max, axis=0)), fresh_score)
        factor = jnp.exp(page_max - top_score[None])
        own_weight = jnp.exp(fresh_score - top_score)
        denominator = own_weight + lax.optimization_barrier(jnp.sum(factor * page_sum, axis=0))
        self_value = fresh_value.astype(jnp.float32).reshape(KEY_VALUE_HEADS, 1, HEAD_SIZE)
        weighted = own_weight[..., None] * self_value + lax.optimization_barrier(jnp.sum(factor[..., None] * page_out, axis=0))
        return (weighted / denominator[..., None]).reshape(QUERY_HEADS * HEAD_SIZE).astype(jnp.bfloat16)
    return lax.map(one_request, (queries, fresh_key_value[0], fresh_key_value[1], block_table, lengths))
```

```python
import functools
import math

import jax
import jax.numpy as jnp
from jax import lax
from jax.experimental import pallas as pl
from jax.experimental.pallas import tpu as pltpu
from jax.sharding import PartitionSpec as P

HEAD_SIZE = 128
LOWEST_SCORE = -1e30
SCALE = 1.0 / math.sqrt(HEAD_SIZE)
VMEM = pltpu.MemorySpace.VMEM
SMEM = pltpu.MemorySpace.SMEM
f32 = jnp.float32
bf16 = jnp.bfloat16


def nt_dot(a, b):
    return lax.dot_general(a, b, (((1,), (1,)), ((), ())), preferred_element_type=f32)


def vmem_specs(n):
    return [pl.BlockSpec(memory_space=VMEM)] * n


def send_kernel(slots, pages, page_ref, lengths_ref, queries_ref, table_ref, out_ref):
    peers = out_ref.shape[0]
    own_rows, most_pages = table_ref.shape
    page_tok = 16
    column = lax.broadcasted_iota(jnp.int32, (1, most_pages), 1)
    fills = []
    for row in range(own_rows):
        entry = table_ref[row : row + 1, :]
        fill = jnp.clip(lengths_ref[row] - column * page_tok, 0, page_tok)
        here = (entry // slots) % pages == page_ref[0]
        fill = jnp.where(here & (entry >= 0), fill, 0)
        lender = entry // (slots * pages)
        slot = entry % slots
        lender_rows = lax.broadcasted_iota(jnp.int32, (peers, most_pages), 0)
        slot_rows = lax.broadcasted_iota(jnp.int32, (slots, most_pages), 0)
        a = jnp.where(lender_rows == lender, fill, 0).astype(f32).astype(bf16)
        b = jnp.where(slot_rows == slot, 1.0, 0.0).astype(bf16)
        fills.append(nt_dot(a, b))
    sub = lax.broadcasted_iota(jnp.int32, (16, slots), 0)
    rows = queries_ref.shape[0]
    queries = queries_ref[...]
    for peer in range(peers):
        out_ref[peer, 0:rows, :] = queries
        tile = jnp.zeros((16, slots), f32)
        for row in range(own_rows):
            tile = jnp.where(sub == row, fills[row][peer : peer + 1, :], tile)
        out_ref[peer, rows : rows + 16, :] = tile.astype(bf16)


def token_major_kernel(pool_ref, out_ref):
    pages, page_tok, width = pool_ref.shape[1:]
    block = page_tok * 16
    i = lax.broadcasted_iota(jnp.int32, (block, block), 0)
    j = lax.broadcasted_iota(jnp.int32, (block, block), 1)
    perm = jnp.where((i % 16) * page_tok + i // 16 == j, 1.0, 0.0).astype(bf16)
    for b in range(pages // 16):
        rows = pool_ref[0, b * 16 : (b + 1) * 16].reshape(block, width)
        moved = jnp.dot(perm, rows, preferred_element_type=f32).astype(bf16)
        out_ref[0, :, b * 16 : (b + 1) * 16, :] = moved.reshape(page_tok, 16, width)


def attend_kernel(recv_ref, kv_ref, out_ref, score_ref, weight_ref):
    peers = recv_ref.shape[0]
    page_tok, slots, width = kv_ref.shape[1:]
    groups = width // HEAD_SIZE
    requests = 2 * peers
    heads = groups * 8
    rows = groups * 16
    sub8 = lax.broadcasted_iota(jnp.int32, (8, slots), 0)
    fill = jnp.zeros((8, slots), f32)
    code = jnp.zeros((8, slots), f32)
    for peer in range(peers):
        tile = recv_ref[peer, rows : rows + 16, :].astype(f32)[0:8]
        fill = fill + tile
        code = code + jnp.where(tile > 0.0, (sub8 + (2 * peer + 1)).astype(f32), 0.0)
    fill = jnp.broadcast_to(jnp.sum(fill, axis=0, keepdims=True), (8, slots))
    owner = jnp.broadcast_to(jnp.sum(code, axis=0, keepdims=True), (8, slots))

    def score_step(t, carry):
        live = fill > t.astype(f32)
        for g in range(groups):
            q = recv_ref[:, g * 16 : (g + 1) * 16, :].reshape(requests * 8, HEAD_SIZE)
            k = kv_ref[0, t, :, g * HEAD_SIZE : (g + 1) * HEAD_SIZE]
            s = nt_dot(q, k)
            picked = jnp.zeros((8, slots), f32)
            for r in range(requests):
                picked = jnp.where(owner == float(r + 1), s[r * 8 : (r + 1) * 8], picked)
            score_ref[t, g * 8 : (g + 1) * 8, :] = jnp.where(live, picked * SCALE, LOWEST_SCORE)
        return carry

    lax.fori_loop(0, page_tok, score_step, 0)

    owner_h = jnp.broadcast_to(owner[0:1], (heads, slots))
    fill_h = jnp.broadcast_to(fill[0:1], (heads, slots))
    page_max = score_ref[0]
    for t in range(1, page_tok):
        page_max = jnp.maximum(page_max, score_ref[t])
    maxima = []
    owner_max = jnp.zeros((heads, slots), f32)
    for r in range(requests):
        mine = owner_h == float(r + 1)
        top = jnp.max(jnp.where(mine, page_max, LOWEST_SCORE), axis=1, keepdims=True)
        maxima.append(top)
        owner_max = jnp.where(mine, top, owner_max)
    factor = jnp.exp(page_max - owner_max)
    page_sum = jnp.zeros((heads, slots), f32)
    sub16 = lax.broadcasted_iota(jnp.int32, (16, slots), 0)
    owner_16 = jnp.broadcast_to(owner[0:1], (16, slots))
    for t in range(page_tok):
        w = jnp.where(fill_h > float(t), jnp.exp(score_ref[t] - page_max), 0.0)
        page_sum = page_sum + w
        scaled = w.astype(bf16).astype(f32) * factor
        high = scaled.astype(bf16).astype(f32)
        score_ref[t] = high
        weight_ref[t] = scaled - high
    page_sum = page_sum * factor
    masks = [
        jnp.where(owner_16 == (2 * k + 1 + sub16 // 8).astype(f32), 1.0, 0.0).astype(bf16)
        for k in range(peers)
    ]
    totals = [
        jnp.sum(jnp.where(owner_h == float(r + 1), page_sum, 0.0), axis=1, keepdims=True)
        for r in range(requests)
    ]
    lane = lax.broadcasted_iota(jnp.int32, (8, HEAD_SIZE), 1)
    for peer in range(peers):
        tile = jnp.zeros((8, HEAD_SIZE), f32)
        for g in range(groups):
            for row in range(2):
                r = 2 * peer + row
                c = g * 2 + row
                tile = jnp.where(lane == c, maxima[r][g * 8 : (g + 1) * 8], tile)
                tile = jnp.where(lane == 2 * groups + c, totals[r][g * 8 : (g + 1) * 8], tile)
        out_ref[peer, rows : rows + 8, :] = tile
    for g in range(groups):
        acc = jnp.zeros((requests * 8, HEAD_SIZE), f32)
        for t0 in range(0, page_tok, 2):
            v = kv_ref[1, t0 : t0 + 2, :, g * HEAD_SIZE : (g + 1) * HEAD_SIZE].reshape(
                2 * slots, HEAD_SIZE
            )
            for ref in (score_ref, weight_ref):
                cols = []
                for t in (t0, t0 + 1):
                    w8 = ref[t, g * 8 : (g + 1) * 8, :]
                    w16 = jnp.concatenate([w8, w8], axis=0).astype(bf16)
                    cols.append(jnp.concatenate([w16 * m for m in masks], axis=0))
                acc = acc + jnp.dot(
                    jnp.concatenate(cols, axis=1), v, preferred_element_type=f32
                )
        out_ref[:, g * 16 : (g + 1) * 16, :] = acc.reshape(peers, 16, HEAD_SIZE)


def merge(parts_ref, groups):
    tiles = 2 * groups
    count = parts_ref.shape[0]
    stats = [parts_ref[i, tiles * 8 : tiles * 8 + 8, :] for i in range(count)]
    top = stats[0]
    for s in stats[1:]:
        top = jnp.maximum(top, s)
    scales = [jnp.exp(s - top) for s in stats]
    total = jnp.zeros_like(top)
    for s, e in zip(stats, scales):
        total = total + pltpu.roll(s, HEAD_SIZE - tiles, axis=1) * e
    sums = []
    for c in range(tiles):
        acc = jnp.zeros((8, HEAD_SIZE), f32)
        for i in range(count):
            acc = acc + parts_ref[i, c * 8 : (c + 1) * 8, :] * scales[i][:, c : c + 1]
        sums.append(acc)
    return top, total, sums


def combine_kernel(groups, parts_ref, out_ref):
    tiles = 2 * groups
    top, total, sums = merge(parts_ref, groups)
    lane = lax.broadcasted_iota(jnp.int32, (8, HEAD_SIZE), 1)
    stat = jnp.where(lane < tiles, top, pltpu.roll(total, tiles, axis=1))
    for i in range(out_ref.shape[0]):
        for c in range(tiles):
            out_ref[i, c * 8 : (c + 1) * 8, :] = sums[c]
        out_ref[i, tiles * 8 : tiles * 8 + 8, :] = stat


def finish_kernel(groups, parts_ref, queries_ref, fresh_ref, out_ref):
    top, total, sums = merge(parts_ref, groups)
    fresh_k = fresh_ref[0].astype(f32)
    fresh_v = fresh_ref[1].astype(f32)
    for g in range(groups):
        outs = []
        q2 = queries_ref[g * 16 : (g + 1) * 16, :].astype(f32)
        for row in range(2):
            c = g * 2 + row
            k = fresh_k[row : row + 1, g * HEAD_SIZE : (g + 1) * HEAD_SIZE]
            v = fresh_v[row : row + 1, g * HEAD_SIZE : (g + 1) * HEAD_SIZE]
            new = jnp.sum(q2[row * 8 : row * 8 + 8] * k, axis=1, keepdims=True) * SCALE
            cache = top[:, c : c + 1]
            best = jnp.maximum(cache, new)
            carried = jnp.exp(cache - best)
            own = jnp.exp(new - best)
            denominator = own + total[:, c : c + 1] * carried
            outs.append((own * v + sums[c] * carried) / denominator)
        out_ref[g * 16 : (g + 1) * 16, :] = jnp.concatenate(outs, axis=0).astype(bf16)


def shards(queries, fresh_key_value, key_value_pool, block_table, lengths):
    lenders = lax.axis_size("inst")
    pages = lax.axis_size("page")
    own_rows = queries.shape[0]
    slots, page_tok, width = key_value_pool.shape[1:]
    groups = width // HEAD_SIZE
    rows = groups * 16
    q = (
        queries.reshape(own_rows, groups, 8, HEAD_SIZE)
        .transpose(1, 0, 2, 3)
        .reshape(rows, HEAD_SIZE)
    )
    page_index = lax.axis_index("page").reshape(1).astype(jnp.int32)

    to_send = pl.pallas_call(
        functools.partial(send_kernel, slots, pages),
        out_shape=jax.ShapeDtypeStruct((lenders, rows + 16, HEAD_SIZE), bf16),
        in_specs=[pl.BlockSpec(memory_space=SMEM)] * 2 + vmem_specs(2),
        out_specs=pl.BlockSpec(memory_space=VMEM),
        name="send",
    )(page_index, lengths, q, block_table)
    received = lax.all_to_all(to_send, "inst", 0, 0)

    kv = pl.pallas_call(
        token_major_kernel,
        grid=(2, 2),
        out_shape=jax.ShapeDtypeStruct((2, page_tok, slots, width), bf16),
        in_specs=[pl.BlockSpec((1, slots // 2, page_tok, width), lambda i, j: (i, j, 0, 0))],
        out_specs=pl.BlockSpec((1, page_tok, slots // 2, width), lambda i, j: (i, 0, j, 0)),
        cost_estimate=pl.CostEstimate(flops=10**9, bytes_accessed=2 * 4 * 2**20, transcendentals=0),
        name="token_major",
    )(key_value_pool)

    partial = pl.pallas_call(
        attend_kernel,
        out_shape=jax.ShapeDtypeStruct((lenders, rows + 8, HEAD_SIZE), f32),
        in_specs=vmem_specs(2),
        out_specs=pl.BlockSpec(memory_space=VMEM),
        scratch_shapes=[
            pltpu.VMEM((page_tok, groups * 8, slots), f32),
            pltpu.VMEM((page_tok, groups * 8, slots), f32),
        ],
        name="attend",
    )(received, kv)
    parts = lax.all_to_all(partial, "inst", 0, 0)

    combined = pl.pallas_call(
        functools.partial(combine_kernel, groups),
        out_shape=jax.ShapeDtypeStruct((pages, rows + 8, HEAD_SIZE), f32),
        in_specs=vmem_specs(1),
        out_specs=pl.BlockSpec(memory_space=VMEM),
        name="combine",
    )(parts)
    page_parts = lax.all_to_all(combined, "page", 0, 0)

    out = pl.pallas_call(
        functools.partial(finish_kernel, groups),
        out_shape=jax.ShapeDtypeStruct((rows, HEAD_SIZE), bf16),
        in_specs=vmem_specs(3),
        out_specs=pl.BlockSpec(memory_space=VMEM),
        name="finish",
    )(page_parts, q, fresh_key_value)
    return (
        out.reshape(groups, own_rows, 8, HEAD_SIZE)
        .transpose(1, 0, 2, 3)
        .reshape(own_rows, groups * 8 * HEAD_SIZE)
    )


def solution(mesh):
    return jax.shard_map(
        shards,
        mesh=mesh,
        in_specs=(
            P("inst", "head"),
            P(None, "inst", "head"),
            P(None, ("inst", "page"), None, "head"),
            P("inst", None),
            P("inst"),
        ),
        out_specs=P("inst", "head"),
        check_vma=False,
    )
```

```python
import functools
import math

import jax
import jax.numpy as jnp
from jax import lax
from jax.experimental import pallas as pl
from jax.experimental.pallas import tpu as pltpu
from jax.sharding import PartitionSpec as P

HEAD_SIZE = 128
LOWEST_SCORE = -1e30
SCALE = 1.0 / math.sqrt(HEAD_SIZE)
VMEM = pltpu.MemorySpace.VMEM
SMEM = pltpu.MemorySpace.SMEM
f32 = jnp.float32
bf16 = jnp.bfloat16


def nt_dot(a, b):
    return lax.dot_general(a, b, (((1,), (1,)), ((), ())), preferred_element_type=f32)


def vmem_specs(n):
    return [pl.BlockSpec(memory_space=VMEM)] * n


def send_kernel(slots, pages, page_ref, lengths_ref, queries_ref, table_ref, out_ref):
    peers = out_ref.shape[0]
    own_rows, most_pages = table_ref.shape
    heads = queries_ref.shape[1] // HEAD_SIZE
    page_tok = 16
    slot_bits = slots.bit_length() - 1
    page_bits = pages.bit_length() - 1
    column = lax.broadcasted_iota(jnp.int32, (1, most_pages), 1)
    lender_rows = lax.broadcasted_iota(jnp.int32, (peers, most_pages), 0)
    slot_rows = lax.broadcasted_iota(jnp.int32, (slots, most_pages), 0)
    fills = []
    for row in range(own_rows):
        entry = table_ref[row : row + 1, :]
        fill = jnp.clip(lengths_ref[row] - column * page_tok, 0, page_tok)
        here = ((entry >> slot_bits) & (pages - 1)) == page_ref[0]
        lender = jnp.where(here & (entry >= 0), entry >> (slot_bits + page_bits), -1)
        slot = entry & (slots - 1)
        a = jnp.where(lender_rows == lender, fill.astype(f32), 0.0).astype(bf16)
        b = jnp.where(slot_rows == slot, 1.0, 0.0).astype(bf16)
        fills.append(nt_dot(a, b))
    sub = lax.broadcasted_iota(jnp.int32, (8, HEAD_SIZE), 0)
    pieces = []
    for g in range(heads // 8):
        pair = [jnp.zeros((8, HEAD_SIZE), f32)] * own_rows
        for head in range(8):
            at = (g * 8 + head) * HEAD_SIZE
            both = queries_ref[:, at : at + HEAD_SIZE].astype(f32)
            pair = [
                jnp.where(sub == head, both[row : row + 1, :], pair[row]) for row in range(own_rows)
            ]
        pieces += pair
    queries = jnp.concatenate(pieces, axis=0).astype(bf16)
    rows = own_rows * heads
    sub = lax.broadcasted_iota(jnp.int32, (16, slots), 0)
    for peer in range(peers):
        out_ref[peer, 0:rows, :] = queries
        tile = jnp.zeros((16, slots), f32)
        for row in range(own_rows):
            tile = jnp.where(sub == row, fills[row][peer : peer + 1, :], tile)
        out_ref[peer, rows : rows + 16, :] = tile.astype(bf16)


def token_major_kernel(pool_ref, out_ref):
    pages, page_tok, width = pool_ref.shape[1:]
    block = page_tok * 16
    i = lax.broadcasted_iota(jnp.int32, (block, block), 0)
    j = lax.broadcasted_iota(jnp.int32, (block, block), 1)
    perm = jnp.where((i % 16) * page_tok + i // 16 == j, 1.0, 0.0).astype(bf16)
    for b in range(pages // 16):
        rows = pool_ref[0, b * 16 : (b + 1) * 16].reshape(block, width)
        moved = jnp.dot(perm, rows, preferred_element_type=f32).astype(bf16)
        out_ref[0, :, b * 16 : (b + 1) * 16, :] = moved.reshape(page_tok, 16, width)


CHUNKS = 4


def attend_kernel(recv_ref, kv_hbm, out_ref, kv_ref, score_ref, weight_ref, sems):
    peers = recv_ref.shape[0]
    page_tok, slots, width = kv_ref.shape[1:]
    step = page_tok // CHUNKS
    loads = [
        [
            pltpu.make_async_copy(
                kv_hbm.at[kind, pl.ds(c * step, step)],
                kv_ref.at[kind, pl.ds(c * step, step)],
                sems.at[kind, c],
            )
            for c in range(CHUNKS)
        ]
        for kind in range(2)
    ]
    for kind in range(2):
        for c in range(CHUNKS):
            loads[kind][c].start()
    groups = width // HEAD_SIZE
    requests = 2 * peers
    heads = groups * 8
    rows = groups * 16
    sub8 = lax.broadcasted_iota(jnp.int32, (8, slots), 0)
    fill = jnp.zeros((8, slots), f32)
    code = jnp.zeros((8, slots), f32)
    for peer in range(peers):
        tile = recv_ref[peer, rows : rows + 16, :].astype(f32)[0:8]
        fill = fill + tile
        code = code + jnp.where(tile > 0.0, (sub8 + (2 * peer + 1)).astype(f32), 0.0)
    fill = jnp.broadcast_to(jnp.sum(fill, axis=0, keepdims=True), (8, slots))
    owner = jnp.broadcast_to(jnp.sum(code, axis=0, keepdims=True), (8, slots))

    def score_step(t, carry):
        live = fill > jnp.asarray(t, f32)
        for g in range(groups):
            q = recv_ref[:, g * 16 : (g + 1) * 16, :].reshape(requests * 8, HEAD_SIZE)
            k = kv_ref[0, t, :, g * HEAD_SIZE : (g + 1) * HEAD_SIZE]
            s = nt_dot(q, k)
            picked = jnp.zeros((8, slots), f32)
            for r in range(requests):
                picked = jnp.where(owner == float(r + 1), s[r * 8 : (r + 1) * 8], picked)
            score_ref[t, g * 8 : (g + 1) * 8, :] = jnp.where(live, picked * SCALE, LOWEST_SCORE)
        return carry

    for c in range(CHUNKS):
        loads[0][c].wait()
        lax.fori_loop(c * step, (c + 1) * step, score_step, 0, unroll=True)

    owner_h = jnp.broadcast_to(owner[0:1], (heads, slots))
    fill_h = jnp.broadcast_to(fill[0:1], (heads, slots))
    page_max = score_ref[0]
    for t in range(1, page_tok):
        page_max = jnp.maximum(page_max, score_ref[t])
    maxima = []
    owner_max = jnp.zeros((heads, slots), f32)
    for r in range(requests):
        mine = owner_h == float(r + 1)
        top = jnp.max(jnp.where(mine, page_max, LOWEST_SCORE), axis=1, keepdims=True)
        maxima.append(top)
        owner_max = jnp.where(mine, top, owner_max)
    factor = jnp.exp(page_max - owner_max)
    page_sum = jnp.zeros((heads, slots), f32)
    sub16 = lax.broadcasted_iota(jnp.int32, (16, slots), 0)
    owner_16 = jnp.broadcast_to(owner[0:1], (16, slots))
    for t in range(page_tok):
        w = jnp.where(fill_h > float(t), jnp.exp(score_ref[t] - page_max), 0.0)
        page_sum = page_sum + w
        scaled = w.astype(bf16).astype(f32) * factor
        high = scaled.astype(bf16).astype(f32)
        score_ref[t] = high
        weight_ref[t] = scaled - high
    page_sum = page_sum * factor
    masks = [
        jnp.where(owner_16 == (2 * k + 1 + sub16 // 8).astype(f32), 1.0, 0.0).astype(bf16)
        for k in range(peers)
    ]
    totals = [
        jnp.sum(jnp.where(owner_h == float(r + 1), page_sum, 0.0), axis=1, keepdims=True)
        for r in range(requests)
    ]
    lane = lax.broadcasted_iota(jnp.int32, (8, HEAD_SIZE), 1)
    for peer in range(peers):
        tile = jnp.zeros((8, HEAD_SIZE), f32)
        for g in range(groups):
            for row in range(2):
                r = 2 * peer + row
                c = g * 2 + row
                tile = jnp.where(lane == c, maxima[r][g * 8 : (g + 1) * 8], tile)
                tile = jnp.where(lane == 2 * groups + c, totals[r][g * 8 : (g + 1) * 8], tile)
        out_ref[peer, rows : rows + 8, :] = tile
    for c in range(CHUNKS):
        loads[1][c].wait()
    for g in range(groups):
        acc = jnp.zeros((requests * 8, HEAD_SIZE), f32)
        for t0 in range(0, page_tok, 2):
            v = kv_ref[1, t0 : t0 + 2, :, g * HEAD_SIZE : (g + 1) * HEAD_SIZE].reshape(
                2 * slots, HEAD_SIZE
            )
            for ref in (score_ref, weight_ref):
                cols = []
                for t in (t0, t0 + 1):
                    w8 = ref[t, g * 8 : (g + 1) * 8, :]
                    w16 = jnp.concatenate([w8, w8], axis=0).astype(bf16)
                    cols.append(jnp.concatenate([w16 * m for m in masks], axis=0))
                acc = acc + jnp.dot(
                    jnp.concatenate(cols, axis=1), v, preferred_element_type=f32
                )
        out_ref[:, g * 16 : (g + 1) * 16, :] = acc.reshape(peers, 16, HEAD_SIZE)


def merge(parts_ref, groups):
    tiles = 2 * groups
    count = parts_ref.shape[0]
    stats = [parts_ref[i, tiles * 8 : tiles * 8 + 8, :] for i in range(count)]
    top = stats[0]
    for s in stats[1:]:
        top = jnp.maximum(top, s)
    scales = [jnp.exp(s - top) for s in stats]
    total = jnp.zeros_like(top)
    for s, e in zip(stats, scales):
        total = total + pltpu.roll(s, HEAD_SIZE - tiles, axis=1) * e
    sums = []
    for c in range(tiles):
        acc = jnp.zeros((8, HEAD_SIZE), f32)
        for i in range(count):
            acc = acc + parts_ref[i, c * 8 : (c + 1) * 8, :] * scales[i][:, c : c + 1]
        sums.append(acc)
    return top, total, sums


def combine_kernel(groups, parts_ref, out_ref):
    tiles = 2 * groups
    top, total, sums = merge(parts_ref, groups)
    lane = lax.broadcasted_iota(jnp.int32, (8, HEAD_SIZE), 1)
    stat = jnp.where(lane < tiles, top, pltpu.roll(total, tiles, axis=1))
    for i in range(out_ref.shape[0]):
        for c in range(tiles):
            out_ref[i, c * 8 : (c + 1) * 8, :] = sums[c]
        out_ref[i, tiles * 8 : tiles * 8 + 8, :] = stat


def finish_kernel(groups, parts_ref, queries_ref, fresh_ref, out_ref):
    top, total, sums = merge(parts_ref, groups)
    fresh_k = fresh_ref[0].astype(f32)
    fresh_v = fresh_ref[1].astype(f32)
    sub = lax.broadcasted_iota(jnp.int32, (8, HEAD_SIZE), 0)
    for g in range(groups):
        both = [
            queries_ref[:, (g * 8 + h) * HEAD_SIZE : (g * 8 + h + 1) * HEAD_SIZE].astype(f32)
            for h in range(8)
        ]
        outs = []
        for row in range(2):
            c = g * 2 + row
            q = jnp.zeros((8, HEAD_SIZE), f32)
            for h in range(8):
                q = jnp.where(sub == h, both[h][row : row + 1, :], q)
            k = fresh_k[row : row + 1, g * HEAD_SIZE : (g + 1) * HEAD_SIZE]
            v = fresh_v[row : row + 1, g * HEAD_SIZE : (g + 1) * HEAD_SIZE]
            new = jnp.sum(q * k, axis=1, keepdims=True) * SCALE
            cache = top[:, c : c + 1]
            best = jnp.maximum(cache, new)
            carried = jnp.exp(cache - best)
            own = jnp.exp(new - best)
            denominator = own + total[:, c : c + 1] * carried
            outs.append((own * v + sums[c] * carried) / denominator)
        for h in range(8):
            at = (g * 8 + h) * HEAD_SIZE
            out_ref[:, at : at + HEAD_SIZE] = jnp.concatenate(
                [outs[0][h : h + 1], outs[1][h : h + 1]], axis=0
            ).astype(bf16)


def shards(queries, fresh_key_value, key_value_pool, block_table, lengths):
    lenders = lax.axis_size("inst")
    pages = lax.axis_size("page")
    own_rows = queries.shape[0]
    slots, page_tok, width = key_value_pool.shape[1:]
    groups = width // HEAD_SIZE
    rows = groups * 16
    page_index = lax.axis_index("page").reshape(1).astype(jnp.int32)

    to_send = pl.pallas_call(
        functools.partial(send_kernel, slots, pages),
        out_shape=jax.ShapeDtypeStruct((lenders, rows + 16, HEAD_SIZE), bf16),
        in_specs=[pl.BlockSpec(memory_space=SMEM)] * 2 + vmem_specs(2),
        out_specs=pl.BlockSpec(memory_space=VMEM),
        compiler_params=pltpu.CompilerParams(vmem_limit_bytes=16 * 2**20),
        name="send",
    )(page_index, lengths, queries, block_table)
    received = lax.all_to_all(to_send, "inst", 0, 0)

    kv = pl.pallas_call(
        token_major_kernel,
        grid=(2, 2),
        out_shape=jax.ShapeDtypeStruct((2, page_tok, slots, width), bf16),
        in_specs=[pl.BlockSpec((1, slots // 2, page_tok, width), lambda i, j: (i, j, 0, 0))],
        out_specs=pl.BlockSpec((1, page_tok, slots // 2, width), lambda i, j: (i, 0, j, 0)),
        cost_estimate=pl.CostEstimate(flops=10**9, bytes_accessed=2 * 4 * 2**20, transcendentals=0),
        name="token_major",
    )(key_value_pool)

    partial = pl.pallas_call(
        attend_kernel,
        out_shape=jax.ShapeDtypeStruct((lenders, rows + 8, HEAD_SIZE), f32),
        in_specs=vmem_specs(1) + [pl.BlockSpec(memory_space=pltpu.MemorySpace.HBM)],
        out_specs=pl.BlockSpec(memory_space=VMEM),
        scratch_shapes=[
            pltpu.VMEM(kv.shape, bf16),
            pltpu.VMEM((page_tok, groups * 8, slots), f32),
            pltpu.VMEM((page_tok, groups * 8, slots), f32),
            pltpu.SemaphoreType.DMA((2, CHUNKS)),
        ],
        compiler_params=pltpu.CompilerParams(vmem_limit_bytes=52 * 2**20),
        name="attend",
    )(received, kv)
    parts = lax.all_to_all(partial, "inst", 0, 0)

    combined = pl.pallas_call(
        functools.partial(combine_kernel, groups),
        out_shape=jax.ShapeDtypeStruct((pages, rows + 8, HEAD_SIZE), f32),
        in_specs=vmem_specs(1),
        out_specs=pl.BlockSpec(memory_space=VMEM),
        compiler_params=pltpu.CompilerParams(vmem_limit_bytes=16 * 2**20),
        name="combine",
    )(parts)
    page_parts = lax.all_to_all(combined, "page", 0, 0)

    return pl.pallas_call(
        functools.partial(finish_kernel, groups),
        out_shape=jax.ShapeDtypeStruct(queries.shape, bf16),
        in_specs=vmem_specs(3),
        out_specs=pl.BlockSpec(memory_space=VMEM),
        compiler_params=pltpu.CompilerParams(vmem_limit_bytes=16 * 2**20),
        name="finish",
    )(page_parts, queries, fresh_key_value)


def solution(mesh):
    return jax.shard_map(
        shards,
        mesh=mesh,
        in_specs=(
            P("inst", "head"),
            P(None, "inst", "head"),
            P(None, ("inst", "page"), None, "head"),
            P("inst", None),
            P("inst"),
        ),
        out_specs=P("inst", "head"),
        check_vma=False,
    )
```

```python
import functools
import math

import jax
import jax.numpy as jnp
from jax import lax
from jax.experimental import pallas as pl
from jax.experimental.pallas import tpu as pltpu
from jax.sharding import PartitionSpec as P

HEAD_SIZE = 128
LOWEST_SCORE = -1e30
SCALE = 1.0 / math.sqrt(HEAD_SIZE)
VMEM = pltpu.MemorySpace.VMEM
SMEM = pltpu.MemorySpace.SMEM
f32 = jnp.float32
bf16 = jnp.bfloat16


def nt_dot(a, b):
    return lax.dot_general(a, b, (((1,), (1,)), ((), ())), preferred_element_type=f32)


STEPS = 16.0
FULL = 32700.0
LOWEST_TOP = -32000.0
PART = 32767.0


def encode_rows(x):
    top = jnp.max(jnp.abs(x), axis=1, keepdims=True)
    k = jnp.ceil(jnp.log2(jnp.maximum(top, 2.0**-120)) * STEPS)
    code = jnp.round((x * jnp.exp2(k * (-1.0 / STEPS))) * FULL)
    return k, code.astype(jnp.int32).astype(jnp.int16)


def vmem_specs(n):
    return [pl.BlockSpec(memory_space=VMEM)] * n


def send_kernel(slots, pages, page_ref, lengths_ref, queries_ref, table_ref, out_ref):
    peers = out_ref.shape[0]
    own_rows, most_pages = table_ref.shape
    heads = queries_ref.shape[1] // HEAD_SIZE
    page_tok = 16
    slot_bits = slots.bit_length() - 1
    page_bits = pages.bit_length() - 1
    column = lax.broadcasted_iota(jnp.int32, (1, most_pages), 1)
    lender_rows = lax.broadcasted_iota(jnp.int32, (peers, most_pages), 0)
    slot_rows = lax.broadcasted_iota(jnp.int32, (slots, most_pages), 0)
    fills = []
    for row in range(own_rows):
        entry = table_ref[row : row + 1, :]
        fill = jnp.clip(lengths_ref[row] - column * page_tok, 0, page_tok)
        here = ((entry >> slot_bits) & (pages - 1)) == page_ref[0]
        lender = jnp.where(here & (entry >= 0), entry >> (slot_bits + page_bits), -1)
        slot = entry & (slots - 1)
        a = jnp.where(lender_rows == lender, fill.astype(f32), 0.0).astype(bf16)
        b = jnp.where(slot_rows == slot, 1.0, 0.0).astype(bf16)
        fills.append(nt_dot(a, b))
    sub = lax.broadcasted_iota(jnp.int32, (8, HEAD_SIZE), 0)
    pieces = []
    for g in range(heads // 8):
        pair = [jnp.zeros((8, HEAD_SIZE), f32)] * own_rows
        for head in range(8):
            at = (g * 8 + head) * HEAD_SIZE
            both = queries_ref[:, at : at + HEAD_SIZE].astype(f32)
            pair = [
                jnp.where(sub == head, both[row : row + 1, :], pair[row]) for row in range(own_rows)
            ]
        pieces += pair
    queries = jnp.concatenate(pieces, axis=0).astype(bf16)
    rows = own_rows * heads
    sub = lax.broadcasted_iota(jnp.int32, (16, slots), 0)
    for peer in range(peers):
        out_ref[peer, 0:rows, :] = queries
        tile = jnp.zeros((16, slots), f32)
        for row in range(own_rows):
            tile = jnp.where(sub == row, fills[row][peer : peer + 1, :], tile)
        out_ref[peer, rows : rows + 16, :] = tile.astype(bf16)


def token_major_kernel(pool_ref, out_ref):
    pages, page_tok, width = pool_ref.shape[1:]
    block = page_tok * 16
    i = lax.broadcasted_iota(jnp.int32, (block, block), 0)
    j = lax.broadcasted_iota(jnp.int32, (block, block), 1)
    perm = jnp.where((i % 16) * page_tok + i // 16 == j, 1.0, 0.0).astype(bf16)
    for b in range(pages // 16):
        rows = pool_ref[0, b * 16 : (b + 1) * 16].reshape(block, width)
        moved = jnp.dot(perm, rows, preferred_element_type=f32).astype(bf16)
        out_ref[0, :, b * 16 : (b + 1) * 16, :] = moved.reshape(page_tok, 16, width)


CHUNKS = 4


def attend_kernel(recv_ref, kv_hbm, out_ref, kv_ref, score_ref, weight_ref, sems):
    peers = recv_ref.shape[0]
    page_tok, slots, width = kv_ref.shape[1:]
    step = page_tok // CHUNKS
    loads = [
        [
            pltpu.make_async_copy(
                kv_hbm.at[kind, pl.ds(c * step, step)],
                kv_ref.at[kind, pl.ds(c * step, step)],
                sems.at[kind, c],
            )
            for c in range(CHUNKS)
        ]
        for kind in range(2)
    ]
    for kind in range(2):
        for c in range(CHUNKS):
            loads[kind][c].start()
    groups = width // HEAD_SIZE
    requests = 2 * peers
    heads = groups * 8
    rows = groups * 16
    sub8 = lax.broadcasted_iota(jnp.int32, (8, slots), 0)
    fill = jnp.zeros((8, slots), f32)
    code = jnp.zeros((8, slots), f32)
    for peer in range(peers):
        tile = recv_ref[peer, rows : rows + 16, :].astype(f32)[0:8]
        fill = fill + tile
        code = code + jnp.where(tile > 0.0, (sub8 + (2 * peer + 1)).astype(f32), 0.0)
    fill = jnp.broadcast_to(jnp.sum(fill, axis=0, keepdims=True), (8, slots))
    owner = jnp.broadcast_to(jnp.sum(code, axis=0, keepdims=True), (8, slots))

    def score_step(t, carry):
        live = fill > jnp.asarray(t, f32)
        for g in range(groups):
            q = recv_ref[:, g * 16 : (g + 1) * 16, :].reshape(requests * 8, HEAD_SIZE)
            k = kv_ref[0, t, :, g * HEAD_SIZE : (g + 1) * HEAD_SIZE]
            s = nt_dot(q, k)
            picked = jnp.zeros((8, slots), f32)
            for r in range(requests):
                picked = jnp.where(owner == float(r + 1), s[r * 8 : (r + 1) * 8], picked)
            score_ref[t, g * 8 : (g + 1) * 8, :] = jnp.where(live, picked * SCALE, LOWEST_SCORE)
        return carry

    for c in range(CHUNKS):
        loads[0][c].wait()
        lax.fori_loop(c * step, (c + 1) * step, score_step, 0, unroll=True)

    owner_h = jnp.broadcast_to(owner[0:1], (heads, slots))
    fill_h = jnp.broadcast_to(fill[0:1], (heads, slots))
    page_max = score_ref[0]
    for t in range(1, page_tok):
        page_max = jnp.maximum(page_max, score_ref[t])
    maxima = []
    owner_max = jnp.zeros((heads, slots), f32)
    for r in range(requests):
        mine = owner_h == float(r + 1)
        top = jnp.max(jnp.where(mine, page_max, LOWEST_TOP), axis=1, keepdims=True)
        top = jnp.round(jnp.maximum(top, LOWEST_TOP))
        maxima.append(top)
        owner_max = jnp.where(mine, top, owner_max)
    factor = jnp.exp(page_max - owner_max)
    page_sum = jnp.zeros((heads, slots), f32)
    sub16 = lax.broadcasted_iota(jnp.int32, (16, slots), 0)
    owner_16 = jnp.broadcast_to(owner[0:1], (16, slots))
    for t in range(page_tok):
        w = jnp.where(fill_h > float(t), jnp.exp(score_ref[t] - page_max), 0.0)
        page_sum = page_sum + w
        scaled = w.astype(bf16).astype(f32) * factor
        high = scaled.astype(bf16).astype(f32)
        score_ref[t] = high
        weight_ref[t] = scaled - high
    page_sum = page_sum * factor
    masks = [
        jnp.where(owner_16 == (2 * k + 1 + sub16 // 8).astype(f32), 1.0, 0.0).astype(bf16)
        for k in range(peers)
    ]
    totals = [
        jnp.sum(jnp.where(owner_h == float(r + 1), page_sum, 0.0), axis=1, keepdims=True)
        for r in range(requests)
    ]
    for c in range(CHUNKS):
        loads[1][c].wait()
    scales = []
    for g in range(groups):
        acc = jnp.zeros((requests * 8, HEAD_SIZE), f32)
        for t0 in range(0, page_tok, 2):
            v = kv_ref[1, t0 : t0 + 2, :, g * HEAD_SIZE : (g + 1) * HEAD_SIZE].reshape(
                2 * slots, HEAD_SIZE
            )
            for ref in (score_ref, weight_ref):
                cols = []
                for t in (t0, t0 + 1):
                    w8 = ref[t, g * 8 : (g + 1) * 8, :]
                    w16 = jnp.concatenate([w8, w8], axis=0).astype(bf16)
                    cols.append(jnp.concatenate([w16 * m for m in masks], axis=0))
                acc = acc + jnp.dot(
                    jnp.concatenate(cols, axis=1), v, preferred_element_type=f32
                )
        k, code = encode_rows(acc)
        scales.append(k)
        out_ref[:, g * 16 : (g + 1) * 16, :] = code.reshape(peers, 16, HEAD_SIZE)
    for peer in range(peers):
        columns = []
        for g in range(groups):
            for row in range(2):
                r = 2 * peer + row
                at = slice(g * 8, (g + 1) * 8)
                columns.append((maxima[r][at], totals[r][at], scales[g][r * 8 : (r + 1) * 8]))
        out_ref[peer, rows : rows + 16, :] = stat_tile(columns, LENDER_UNIT)


LENDER_UNIT = 8.0
OWNER_UNIT = 1.0


def stat_tile(columns, unit):
    tiles = len(columns)
    lane = lax.broadcasted_iota(jnp.int32, (8, HEAD_SIZE), 1)
    top = jnp.zeros((8, HEAD_SIZE), f32)
    total = top
    scale = top
    for c, (m, l, k) in enumerate(columns):
        top = jnp.where(lane == c, m, top)
        total = jnp.where((lane == tiles + c) | (lane == 2 * tiles + c), l, total)
        scale = jnp.where(lane == 3 * tiles + c, k, scale)
    total = total * unit
    whole = jnp.floor(total)
    part = jnp.round((total - whole) * PART)
    tile = jnp.where(lane < tiles, top, jnp.where(lane < 2 * tiles, whole, part))
    tile = jnp.where(lane < 3 * tiles, tile, scale)
    tile = tile.astype(jnp.int32)
    return jnp.concatenate([tile, jnp.zeros_like(tile)], axis=0).astype(jnp.int16)


def merge(parts_ref, groups, unit):
    tiles = 2 * groups
    count = parts_ref.shape[0]
    stats = [
        parts_ref[i, tiles * 8 : tiles * 8 + 16, :].astype(jnp.int32).astype(f32)[0:8]
        for i in range(count)
    ]
    top = stats[0]
    for s in stats[1:]:
        top = jnp.maximum(top, s)
    total = jnp.zeros_like(top)
    scales = []
    for s in stats:
        shifted = [pltpu.roll(s, HEAD_SIZE - n * tiles, axis=1) for n in (1, 2, 3)]
        e = jnp.exp(s - top)
        total = total + (shifted[0] + shifted[1] * (1.0 / PART)) * e
        scales.append(e * (jnp.exp2(shifted[2] * (1.0 / STEPS)) * (1.0 / FULL)))
    sums = []
    for g in range(groups):
        pair = [jnp.zeros((8, HEAD_SIZE), f32)] * 2
        for i in range(count):
            both = parts_ref[i, g * 16 : (g + 1) * 16, :].astype(jnp.int32).astype(f32)
            pair = [
                pair[n] + both[n * 8 : (n + 1) * 8] * scales[i][:, g * 2 + n : g * 2 + n + 1]
                for n in range(2)
            ]
        sums += pair
    return top, total * (1.0 / unit), sums


def combine_kernel(groups, parts_ref, out_ref):
    tiles = 2 * groups
    top, total, sums = merge(parts_ref, groups, LENDER_UNIT)
    coded = [encode_rows(jnp.concatenate(sums[2 * g : 2 * g + 2], axis=0)) for g in range(groups)]
    columns = [
        (top[:, c : c + 1], total[:, c : c + 1], coded[c // 2][0][c % 2 * 8 : c % 2 * 8 + 8])
        for c in range(tiles)
    ]
    stat = stat_tile(columns, OWNER_UNIT)
    for i in range(out_ref.shape[0]):
        for g in range(groups):
            out_ref[i, g * 16 : (g + 1) * 16, :] = coded[g][1]
        out_ref[i, tiles * 8 : tiles * 8 + 16, :] = stat


def finish_kernel(groups, parts_ref, queries_ref, fresh_ref, out_ref):
    top, total, sums = merge(parts_ref, groups, OWNER_UNIT)
    fresh_k = fresh_ref[0].astype(f32)
    fresh_v = fresh_ref[1].astype(f32)
    sub = lax.broadcasted_iota(jnp.int32, (8, HEAD_SIZE), 0)
    for g in range(groups):
        both = [
            queries_ref[:, (g * 8 + h) * HEAD_SIZE : (g * 8 + h + 1) * HEAD_SIZE].astype(f32)
            for h in range(8)
        ]
        outs = []
        for row in range(2):
            c = g * 2 + row
            q = jnp.zeros((8, HEAD_SIZE), f32)
            for h in range(8):
                q = jnp.where(sub == h, both[h][row : row + 1, :], q)
            k = fresh_k[row : row + 1, g * HEAD_SIZE : (g + 1) * HEAD_SIZE]
            v = fresh_v[row : row + 1, g * HEAD_SIZE : (g + 1) * HEAD_SIZE]
            new = jnp.sum(q * k, axis=1, keepdims=True) * SCALE
            cache = top[:, c : c + 1]
            best = jnp.maximum(cache, new)
            carried = jnp.exp(cache - best)
            own = jnp.exp(new - best)
            denominator = own + total[:, c : c + 1] * carried
            outs.append((own * v + sums[c] * carried) / denominator)
        for h in range(8):
            at = (g * 8 + h) * HEAD_SIZE
            out_ref[:, at : at + HEAD_SIZE] = jnp.concatenate(
                [outs[0][h : h + 1], outs[1][h : h + 1]], axis=0
            ).astype(bf16)


def shards(queries, fresh_key_value, key_value_pool, block_table, lengths):
    lenders = lax.axis_size("inst")
    pages = lax.axis_size("page")
    own_rows = queries.shape[0]
    slots, page_tok, width = key_value_pool.shape[1:]
    groups = width // HEAD_SIZE
    rows = groups * 16
    page_index = lax.axis_index("page").reshape(1).astype(jnp.int32)

    to_send = pl.pallas_call(
        functools.partial(send_kernel, slots, pages),
        out_shape=jax.ShapeDtypeStruct((lenders, rows + 16, HEAD_SIZE), bf16),
        in_specs=[pl.BlockSpec(memory_space=SMEM)] * 2 + vmem_specs(2),
        out_specs=pl.BlockSpec(memory_space=VMEM),
        name="send",
    )(page_index, lengths, queries, block_table)
    received = lax.all_to_all(to_send, "inst", 0, 0)

    kv = pl.pallas_call(
        token_major_kernel,
        grid=(2, 2),
        out_shape=jax.ShapeDtypeStruct((2, page_tok, slots, width), bf16),
        in_specs=[pl.BlockSpec((1, slots // 2, page_tok, width), lambda i, j: (i, j, 0, 0))],
        out_specs=pl.BlockSpec((1, page_tok, slots // 2, width), lambda i, j: (i, 0, j, 0)),
        cost_estimate=pl.CostEstimate(flops=10**9, bytes_accessed=2 * 4 * 2**20, transcendentals=0),
        name="token_major",
    )(key_value_pool)

    partial = pl.pallas_call(
        attend_kernel,
        out_shape=jax.ShapeDtypeStruct((lenders, rows + 16, HEAD_SIZE), jnp.int16),
        in_specs=vmem_specs(1) + [pl.BlockSpec(memory_space=pltpu.MemorySpace.HBM)],
        out_specs=pl.BlockSpec(memory_space=VMEM),
        scratch_shapes=[
            pltpu.VMEM(kv.shape, bf16),
            pltpu.VMEM((page_tok, groups * 8, slots), f32),
            pltpu.VMEM((page_tok, groups * 8, slots), f32),
            pltpu.SemaphoreType.DMA((2, CHUNKS)),
        ],
        compiler_params=pltpu.CompilerParams(vmem_limit_bytes=52 * 2**20),
        name="attend",
    )(received, kv)
    parts = lax.all_to_all(partial, "inst", 0, 0)

    combined = pl.pallas_call(
        functools.partial(combine_kernel, groups),
        out_shape=jax.ShapeDtypeStruct((pages, rows + 16, HEAD_SIZE), jnp.int16),
        in_specs=vmem_specs(1),
        out_specs=pl.BlockSpec(memory_space=VMEM),
        compiler_params=pltpu.CompilerParams(vmem_limit_bytes=16 * 2**20),
        name="combine",
    )(parts)
    page_parts = lax.all_to_all(combined, "page", 0, 0)

    return pl.pallas_call(
        functools.partial(finish_kernel, groups),
        out_shape=jax.ShapeDtypeStruct(queries.shape, bf16),
        in_specs=vmem_specs(3),
        out_specs=pl.BlockSpec(memory_space=VMEM),
        compiler_params=pltpu.CompilerParams(vmem_limit_bytes=16 * 2**20),
        name="finish",
    )(page_parts, queries, fresh_key_value)


def solution(mesh):
    return jax.shard_map(
        shards,
        mesh=mesh,
        in_specs=(
            P("inst", "head"),
            P(None, "inst", "head"),
            P(None, ("inst", "page"), None, "head"),
            P("inst", None),
            P("inst"),
        ),
        out_specs=P("inst", "head"),
        check_vma=False,
    )
```

```python
import functools
import math

import jax
import jax.numpy as jnp
from jax import lax
from jax.experimental import pallas as pl
from jax.experimental.pallas import tpu as pltpu
from jax.sharding import PartitionSpec as P

HEAD_SIZE = 128
LOWEST_SCORE = -1e30
SCALE = 1.0 / math.sqrt(HEAD_SIZE)
VMEM = pltpu.MemorySpace.VMEM
SMEM = pltpu.MemorySpace.SMEM
f32 = jnp.float32
bf16 = jnp.bfloat16


def nt_dot(a, b):
    return lax.dot_general(a, b, (((1,), (1,)), ((), ())), preferred_element_type=f32)


STEPS = 16.0
FULL = 32700.0
LOWEST_TOP = -32000.0
PART = 32767.0


def encode_rows(x):
    top = jnp.max(jnp.abs(x), axis=1, keepdims=True)
    k = jnp.ceil(jnp.log2(jnp.maximum(top, 2.0**-120)) * STEPS)
    code = jnp.round((x * jnp.exp2(k * (-1.0 / STEPS))) * FULL)
    return k, code.astype(jnp.int32).astype(jnp.int16)


def vmem_specs(n):
    return [pl.BlockSpec(memory_space=VMEM)] * n


def send_kernel(slots, pages, page_ref, lengths_ref, queries_ref, table_ref, out_ref):
    peers = out_ref.shape[0]
    own_rows, most_pages = table_ref.shape
    heads = queries_ref.shape[1] // HEAD_SIZE
    page_tok = 16
    slot_bits = slots.bit_length() - 1
    page_bits = pages.bit_length() - 1
    column = lax.broadcasted_iota(jnp.int32, (1, most_pages), 1)
    lender_rows = lax.broadcasted_iota(jnp.int32, (peers, most_pages), 0)
    slot_rows = lax.broadcasted_iota(jnp.int32, (slots, most_pages), 0)
    fills = []
    for row in range(own_rows):
        entry = table_ref[row : row + 1, :]
        fill = jnp.clip(lengths_ref[row] - column * page_tok, 0, page_tok)
        here = ((entry >> slot_bits) & (pages - 1)) == page_ref[0]
        lender = jnp.where(here & (entry >= 0), entry >> (slot_bits + page_bits), -1)
        slot = entry & (slots - 1)
        a = jnp.where(lender_rows == lender, fill.astype(f32), 0.0).astype(bf16)
        b = jnp.where(slot_rows == slot, 1.0, 0.0).astype(bf16)
        fills.append(nt_dot(a, b))
    sub = lax.broadcasted_iota(jnp.int32, (8, HEAD_SIZE), 0)
    pieces = []
    for g in range(heads // 8):
        pair = [jnp.zeros((8, HEAD_SIZE), f32)] * own_rows
        for head in range(8):
            at = (g * 8 + head) * HEAD_SIZE
            both = queries_ref[:, at : at + HEAD_SIZE].astype(f32)
            pair = [
                jnp.where(sub == head, both[row : row + 1, :], pair[row]) for row in range(own_rows)
            ]
        pieces += pair
    queries = jnp.concatenate(pieces, axis=0).astype(bf16)
    rows = own_rows * heads
    sub = lax.broadcasted_iota(jnp.int32, (16, slots), 0)
    for peer in range(peers):
        out_ref[peer, 0:rows, :] = queries
        tile = jnp.zeros((16, slots), f32)
        for row in range(own_rows):
            tile = jnp.where(sub == row, fills[row][peer : peer + 1, :], tile)
        out_ref[peer, rows : rows + 16, :] = tile.astype(bf16)


PARTS = 2


def token_major_kernel(pool_hbm, out_hbm, pool_ref, out_ref, load_sems, store_sems):
    pages, page_tok, width = pool_hbm.shape[1:]
    chunk = pages // PARTS
    block = page_tok * 16
    loads = []
    stores = []
    for kind in range(2):
        for c in range(PARTS):
            at = pl.ds(c * chunk, chunk)
            loads.append(
                pltpu.make_async_copy(
                    pool_hbm.at[kind, at], pool_ref.at[kind, at], load_sems.at[kind, c]
                )
            )
            stores.append(
                pltpu.make_async_copy(
                    out_ref.at[kind, :, at], out_hbm.at[kind, :, at], store_sems.at[kind, c]
                )
            )
    for load in loads:
        load.start()
    i = lax.broadcasted_iota(jnp.int32, (block, block), 0)
    j = lax.broadcasted_iota(jnp.int32, (block, block), 1)
    perm = jnp.where((i % 16) * page_tok + i // 16 == j, 1.0, 0.0).astype(bf16)
    for kind in range(2):
        for c in range(PARTS):
            loads[kind * PARTS + c].wait()
            for b in range(chunk // 16):
                first = c * chunk + b * 16
                rows = pool_ref[kind, first : first + 16].reshape(block, width)
                moved = jnp.dot(perm, rows, preferred_element_type=f32).astype(bf16)
                out_ref[kind, :, first : first + 16, :] = moved.reshape(page_tok, 16, width)
            stores[kind * PARTS + c].start()
    for store in stores:
        store.wait()


CHUNKS = 4


def attend_kernel(recv_ref, kv_hbm, out_ref, kv_ref, score_ref, weight_ref, sems):
    peers = recv_ref.shape[0]
    page_tok, slots, width = kv_ref.shape[1:]
    step = page_tok // CHUNKS
    loads = [
        [
            pltpu.make_async_copy(
                kv_hbm.at[kind, pl.ds(c * step, step)],
                kv_ref.at[kind, pl.ds(c * step, step)],
                sems.at[kind, c],
            )
            for c in range(CHUNKS)
        ]
        for kind in range(2)
    ]
    for kind in range(2):
        for c in range(CHUNKS):
            loads[kind][c].start()
    groups = width // HEAD_SIZE
    requests = 2 * peers
    heads = groups * 8
    rows = groups * 16
    sub8 = lax.broadcasted_iota(jnp.int32, (8, slots), 0)
    fill = jnp.zeros((8, slots), f32)
    code = jnp.zeros((8, slots), f32)
    for peer in range(peers):
        tile = recv_ref[peer, rows : rows + 16, :].astype(f32)[0:8]
        fill = fill + tile
        code = code + jnp.where(tile > 0.0, (sub8 + (2 * peer + 1)).astype(f32), 0.0)
    fill = jnp.broadcast_to(jnp.sum(fill, axis=0, keepdims=True), (8, slots))
    owner = jnp.broadcast_to(jnp.sum(code, axis=0, keepdims=True), (8, slots))

    def score_step(t, carry):
        live = fill > jnp.asarray(t, f32)
        for g in range(groups):
            q = recv_ref[:, g * 16 : (g + 1) * 16, :].reshape(requests * 8, HEAD_SIZE)
            k = kv_ref[0, t, :, g * HEAD_SIZE : (g + 1) * HEAD_SIZE]
            s = nt_dot(q, k)
            picked = jnp.zeros((8, slots), f32)
            for r in range(requests):
                picked = jnp.where(owner == float(r + 1), s[r * 8 : (r + 1) * 8], picked)
            score_ref[t, g * 8 : (g + 1) * 8, :] = jnp.where(live, picked * SCALE, LOWEST_SCORE)
        return carry

    for c in range(CHUNKS):
        loads[0][c].wait()
        lax.fori_loop(c * step, (c + 1) * step, score_step, 0, unroll=True)

    owner_h = jnp.broadcast_to(owner[0:1], (heads, slots))
    fill_h = jnp.broadcast_to(fill[0:1], (heads, slots))
    page_max = score_ref[0]
    for t in range(1, page_tok):
        page_max = jnp.maximum(page_max, score_ref[t])
    maxima = []
    owner_max = jnp.zeros((heads, slots), f32)
    for r in range(requests):
        mine = owner_h == float(r + 1)
        top = jnp.max(jnp.where(mine, page_max, LOWEST_TOP), axis=1, keepdims=True)
        top = jnp.round(jnp.maximum(top, LOWEST_TOP))
        maxima.append(top)
        owner_max = jnp.where(mine, top, owner_max)
    factor = jnp.exp(page_max - owner_max)
    page_sum = jnp.zeros((heads, slots), f32)
    sub16 = lax.broadcasted_iota(jnp.int32, (16, slots), 0)
    owner_16 = jnp.broadcast_to(owner[0:1], (16, slots))
    for t in range(page_tok):
        w = jnp.where(fill_h > float(t), jnp.exp(score_ref[t] - page_max), 0.0)
        page_sum = page_sum + w
        scaled = w.astype(bf16).astype(f32) * factor
        high = scaled.astype(bf16).astype(f32)
        score_ref[t] = high
        weight_ref[t] = scaled - high
    page_sum = page_sum * factor
    masks = [
        jnp.where(owner_16 == (2 * k + 1 + sub16 // 8).astype(f32), 1.0, 0.0).astype(bf16)
        for k in range(peers)
    ]
    totals = [
        jnp.sum(jnp.where(owner_h == float(r + 1), page_sum, 0.0), axis=1, keepdims=True)
        for r in range(requests)
    ]
    for c in range(CHUNKS):
        loads[1][c].wait()
    scales = []
    for g in range(groups):
        acc = jnp.zeros((requests * 8, HEAD_SIZE), f32)
        for t0 in range(0, page_tok, 2):
            v = kv_ref[1, t0 : t0 + 2, :, g * HEAD_SIZE : (g + 1) * HEAD_SIZE].reshape(
                2 * slots, HEAD_SIZE
            )
            for ref in (score_ref, weight_ref):
                cols = []
                for t in (t0, t0 + 1):
                    w8 = ref[t, g * 8 : (g + 1) * 8, :]
                    w16 = jnp.concatenate([w8, w8], axis=0).astype(bf16)
                    cols.append(jnp.concatenate([w16 * m for m in masks], axis=0))
                acc = acc + jnp.dot(
                    jnp.concatenate(cols, axis=1), v, preferred_element_type=f32
                )
        k, code = encode_rows(acc)
        scales.append(k)
        out_ref[:, g * 16 : (g + 1) * 16, :] = code.reshape(peers, 16, HEAD_SIZE)
    for peer in range(peers):
        columns = []
        for g in range(groups):
            for row in range(2):
                r = 2 * peer + row
                at = slice(g * 8, (g + 1) * 8)
                columns.append((maxima[r][at], totals[r][at], scales[g][r * 8 : (r + 1) * 8]))
        out_ref[peer, rows : rows + 16, :] = stat_tile(columns, LENDER_UNIT)


LENDER_UNIT = 8.0
OWNER_UNIT = 1.0


def stat_tile(columns, unit):
    tiles = len(columns)
    lane = lax.broadcasted_iota(jnp.int32, (8, HEAD_SIZE), 1)
    top = jnp.zeros((8, HEAD_SIZE), f32)
    total = top
    scale = top
    for c, (m, l, k) in enumerate(columns):
        top = jnp.where(lane == c, m, top)
        total = jnp.where((lane == tiles + c) | (lane == 2 * tiles + c), l, total)
        scale = jnp.where(lane == 3 * tiles + c, k, scale)
    total = total * unit
    whole = jnp.floor(total)
    part = jnp.round((total - whole) * PART)
    tile = jnp.where(lane < tiles, top, jnp.where(lane < 2 * tiles, whole, part))
    tile = jnp.where(lane < 3 * tiles, tile, scale)
    tile = tile.astype(jnp.int32)
    return jnp.concatenate([tile, jnp.zeros_like(tile)], axis=0).astype(jnp.int16)


def merge(parts_ref, groups, unit):
    tiles = 2 * groups
    count = parts_ref.shape[0]
    stats = [
        parts_ref[i, tiles * 8 : tiles * 8 + 16, :].astype(jnp.int32).astype(f32)[0:8]
        for i in range(count)
    ]
    top = stats[0]
    for s in stats[1:]:
        top = jnp.maximum(top, s)
    total = jnp.zeros_like(top)
    scales = []
    for s in stats:
        shifted = [pltpu.roll(s, HEAD_SIZE - n * tiles, axis=1) for n in (1, 2, 3)]
        e = jnp.exp(s - top)
        total = total + (shifted[0] + shifted[1] * (1.0 / PART)) * e
        scales.append(e * (jnp.exp2(shifted[2] * (1.0 / STEPS)) * (1.0 / FULL)))
    sums = []
    for g in range(groups):
        pair = [jnp.zeros((8, HEAD_SIZE), f32)] * 2
        for i in range(count):
            both = parts_ref[i, g * 16 : (g + 1) * 16, :].astype(jnp.int32).astype(f32)
            pair = [
                pair[n] + both[n * 8 : (n + 1) * 8] * scales[i][:, g * 2 + n : g * 2 + n + 1]
                for n in range(2)
            ]
        sums += pair
    return top, total * (1.0 / unit), sums


def combine_kernel(groups, parts_ref, out_ref):
    tiles = 2 * groups
    top, total, sums = merge(parts_ref, groups, LENDER_UNIT)
    coded = [encode_rows(jnp.concatenate(sums[2 * g : 2 * g + 2], axis=0)) for g in range(groups)]
    columns = [
        (top[:, c : c + 1], total[:, c : c + 1], coded[c // 2][0][c % 2 * 8 : c % 2 * 8 + 8])
        for c in range(tiles)
    ]
    stat = stat_tile(columns, OWNER_UNIT)
    for i in range(out_ref.shape[0]):
        for g in range(groups):
            out_ref[i, g * 16 : (g + 1) * 16, :] = coded[g][1]
        out_ref[i, tiles * 8 : tiles * 8 + 16, :] = stat


def finish_kernel(groups, parts_ref, queries_ref, fresh_ref, out_ref):
    top, total, sums = merge(parts_ref, groups, OWNER_UNIT)
    fresh_k = fresh_ref[0].astype(f32)
    fresh_v = fresh_ref[1].astype(f32)
    sub = lax.broadcasted_iota(jnp.int32, (8, HEAD_SIZE), 0)
    for g in range(groups):
        both = [
            queries_ref[:, (g * 8 + h) * HEAD_SIZE : (g * 8 + h + 1) * HEAD_SIZE].astype(f32)
            for h in range(8)
        ]
        outs = []
        for row in range(2):
            c = g * 2 + row
            q = jnp.zeros((8, HEAD_SIZE), f32)
            for h in range(8):
                q = jnp.where(sub == h, both[h][row : row + 1, :], q)
            k = fresh_k[row : row + 1, g * HEAD_SIZE : (g + 1) * HEAD_SIZE]
            v = fresh_v[row : row + 1, g * HEAD_SIZE : (g + 1) * HEAD_SIZE]
            new = jnp.sum(q * k, axis=1, keepdims=True) * SCALE
            cache = top[:, c : c + 1]
            best = jnp.maximum(cache, new)
            carried = jnp.exp(cache - best)
            own = jnp.exp(new - best)
            denominator = own + total[:, c : c + 1] * carried
            outs.append((own * v + sums[c] * carried) / denominator)
        for h in range(8):
            at = (g * 8 + h) * HEAD_SIZE
            out_ref[:, at : at + HEAD_SIZE] = jnp.concatenate(
                [outs[0][h : h + 1], outs[1][h : h + 1]], axis=0
            ).astype(bf16)


def shards(queries, fresh_key_value, key_value_pool, block_table, lengths):
    lenders = lax.axis_size("inst")
    pages = lax.axis_size("page")
    own_rows = queries.shape[0]
    slots, page_tok, width = key_value_pool.shape[1:]
    groups = width // HEAD_SIZE
    rows = groups * 16
    page_index = lax.axis_index("page").reshape(1).astype(jnp.int32)

    to_send = pl.pallas_call(
        functools.partial(send_kernel, slots, pages),
        out_shape=jax.ShapeDtypeStruct((lenders, rows + 16, HEAD_SIZE), bf16),
        in_specs=[pl.BlockSpec(memory_space=SMEM)] * 2 + vmem_specs(2),
        out_specs=pl.BlockSpec(memory_space=VMEM),
        name="send",
    )(page_index, lengths, queries, block_table)
    received = lax.all_to_all(to_send, "inst", 0, 0)

    kv = pl.pallas_call(
        token_major_kernel,
        out_shape=jax.ShapeDtypeStruct((2, page_tok, slots, width), bf16),
        in_specs=[pl.BlockSpec(memory_space=pl.ANY)],
        out_specs=pl.BlockSpec(memory_space=pl.ANY),
        scratch_shapes=[
            pltpu.VMEM(key_value_pool.shape, bf16),
            pltpu.VMEM((2, page_tok, slots, width), bf16),
            pltpu.SemaphoreType.DMA((2, PARTS)),
            pltpu.SemaphoreType.DMA((2, PARTS)),
        ],
        cost_estimate=pl.CostEstimate(flops=10**9, bytes_accessed=2 * 4 * 2**20, transcendentals=0),
        name="token_major",
    )(key_value_pool)

    partial = pl.pallas_call(
        attend_kernel,
        out_shape=jax.ShapeDtypeStruct((lenders, rows + 16, HEAD_SIZE), jnp.int16),
        in_specs=vmem_specs(1) + [pl.BlockSpec(memory_space=pltpu.MemorySpace.HBM)],
        out_specs=pl.BlockSpec(memory_space=VMEM),
        scratch_shapes=[
            pltpu.VMEM(kv.shape, bf16),
            pltpu.VMEM((page_tok, groups * 8, slots), f32),
            pltpu.VMEM((page_tok, groups * 8, slots), f32),
            pltpu.SemaphoreType.DMA((2, CHUNKS)),
        ],
        compiler_params=pltpu.CompilerParams(vmem_limit_bytes=52 * 2**20),
        name="attend",
    )(received, kv)
    parts = lax.all_to_all(partial, "inst", 0, 0)

    combined = pl.pallas_call(
        functools.partial(combine_kernel, groups),
        out_shape=jax.ShapeDtypeStruct((pages, rows + 16, HEAD_SIZE), jnp.int16),
        in_specs=vmem_specs(1),
        out_specs=pl.BlockSpec(memory_space=VMEM),
        compiler_params=pltpu.CompilerParams(vmem_limit_bytes=16 * 2**20),
        name="combine",
    )(parts)
    page_parts = lax.all_to_all(combined, "page", 0, 0)

    return pl.pallas_call(
        functools.partial(finish_kernel, groups),
        out_shape=jax.ShapeDtypeStruct(queries.shape, bf16),
        in_specs=vmem_specs(3),
        out_specs=pl.BlockSpec(memory_space=VMEM),
        compiler_params=pltpu.CompilerParams(vmem_limit_bytes=16 * 2**20),
        name="finish",
    )(page_parts, queries, fresh_key_value)


def solution(mesh):
    return jax.shard_map(
        shards,
        mesh=mesh,
        in_specs=(
            P("inst", "head"),
            P(None, "inst", "head"),
            P(None, ("inst", "page"), None, "head"),
            P("inst", None),
            P("inst"),
        ),
        out_specs=P("inst", "head"),
        check_vma=False,
    )
```

```python
import functools
import math

import jax
import jax.numpy as jnp
from jax import lax
from jax.experimental import pallas as pl
from jax.experimental.pallas import tpu as pltpu
from jax.sharding import PartitionSpec as P

HEAD_SIZE = 128
LOWEST_SCORE = -1e30
SCALE = 1.0 / math.sqrt(HEAD_SIZE)
VMEM = pltpu.MemorySpace.VMEM
SMEM = pltpu.MemorySpace.SMEM
f32 = jnp.float32
bf16 = jnp.bfloat16


def nt_dot(a, b):
    return lax.dot_general(a, b, (((1,), (1,)), ((), ())), preferred_element_type=f32)


STEPS = 16.0
FULL = 32700.0
LOWEST_TOP = -32000.0
PART = 32767.0


def encode_rows(x):
    top = jnp.max(jnp.abs(x), axis=1, keepdims=True)
    k = jnp.ceil(jnp.log2(jnp.maximum(top, 2.0**-120)) * STEPS)
    code = jnp.round((x * jnp.exp2(k * (-1.0 / STEPS))) * FULL)
    return k, code.astype(jnp.int32).astype(jnp.int16)


def vmem_specs(n):
    return [pl.BlockSpec(memory_space=VMEM)] * n


def send_kernel(slots, pages, page_ref, lengths_ref, queries_ref, table_ref, out_ref):
    peers = out_ref.shape[0]
    own_rows, most_pages = table_ref.shape
    heads = queries_ref.shape[1] // HEAD_SIZE
    page_tok = 16
    slot_bits = slots.bit_length() - 1
    page_bits = pages.bit_length() - 1
    column = lax.broadcasted_iota(jnp.int32, (1, most_pages), 1)
    lender_rows = lax.broadcasted_iota(jnp.int32, (peers, most_pages), 0)
    slot_rows = lax.broadcasted_iota(jnp.int32, (slots, most_pages), 0)
    fills = []
    for row in range(own_rows):
        entry = table_ref[row : row + 1, :]
        fill = jnp.clip(lengths_ref[row] - column * page_tok, 0, page_tok)
        here = ((entry >> slot_bits) & (pages - 1)) == page_ref[0]
        lender = jnp.where(here & (entry >= 0), entry >> (slot_bits + page_bits), -1)
        slot = entry & (slots - 1)
        a = jnp.where(lender_rows == lender, fill.astype(f32), 0.0).astype(bf16)
        b = jnp.where(slot_rows == slot, 1.0, 0.0).astype(bf16)
        fills.append(nt_dot(a, b))
    sub = lax.broadcasted_iota(jnp.int32, (8, HEAD_SIZE), 0)
    pieces = []
    for g in range(heads // 8):
        pair = [jnp.zeros((8, HEAD_SIZE), f32)] * own_rows
        for head in range(8):
            at = (g * 8 + head) * HEAD_SIZE
            both = queries_ref[:, at : at + HEAD_SIZE].astype(f32)
            pair = [
                jnp.where(sub == head, both[row : row + 1, :], pair[row]) for row in range(own_rows)
            ]
        pieces += pair
    queries = jnp.concatenate(pieces, axis=0).astype(bf16)
    rows = own_rows * heads
    sub = lax.broadcasted_iota(jnp.int32, (16, slots), 0)
    for peer in range(peers):
        out_ref[peer, 0:rows, :] = queries
        tile = jnp.zeros((16, slots), f32)
        for row in range(own_rows):
            tile = jnp.where(sub == row, fills[row][peer : peer + 1, :], tile)
        out_ref[peer, rows : rows + 16, :] = tile.astype(bf16)


PARTS = 2


def token_major_kernel(pool_hbm, out_hbm, pool_ref, out_ref, load_sems, store_sems):
    pages, page_tok, width = pool_hbm.shape[1:]
    chunk = pages // PARTS
    block = page_tok * 16
    loads = []
    stores = []
    for kind in range(2):
        for c in range(PARTS):
            at = pl.ds(c * chunk, chunk)
            loads.append(
                pltpu.make_async_copy(
                    pool_hbm.at[kind, at], pool_ref.at[kind, at], load_sems.at[kind, c]
                )
            )
            stores.append(
                pltpu.make_async_copy(
                    out_ref.at[kind, :, at], out_hbm.at[kind, :, at], store_sems.at[kind, c]
                )
            )
    for load in loads:
        load.start()
    i = lax.broadcasted_iota(jnp.int32, (block, block), 0)
    j = lax.broadcasted_iota(jnp.int32, (block, block), 1)
    perm = jnp.where((i % 16) * page_tok + i // 16 == j, 1.0, 0.0).astype(bf16)
    for kind in range(2):
        for c in range(PARTS):
            loads[kind * PARTS + c].wait()
            for b in range(chunk // 16):
                first = c * chunk + b * 16
                rows = pool_ref[kind, first : first + 16].reshape(block, width)
                moved = jnp.dot(perm, rows, preferred_element_type=f32).astype(bf16)
                out_ref[kind, :, first : first + 16, :] = moved.reshape(page_tok, 16, width)
            stores[kind * PARTS + c].start()
    for store in stores:
        store.wait()


CHUNKS = 4


def attend_kernel(recv_ref, kv_hbm, out_ref, kv_ref, score_ref, weight_ref, sems):
    peers = recv_ref.shape[0]
    page_tok, slots, width = kv_ref.shape[1:]
    step = page_tok // CHUNKS
    loads = [
        [
            pltpu.make_async_copy(
                kv_hbm.at[kind, pl.ds(c * step, step)],
                kv_ref.at[kind, pl.ds(c * step, step)],
                sems.at[kind, c],
            )
            for c in range(CHUNKS)
        ]
        for kind in range(2)
    ]
    for kind in range(2):
        for c in range(CHUNKS):
            loads[kind][c].start()
    groups = width // HEAD_SIZE
    requests = 2 * peers
    heads = groups * 8
    rows = groups * 16
    sub8 = lax.broadcasted_iota(jnp.int32, (8, slots), 0)
    fill = jnp.zeros((8, slots), f32)
    code = jnp.zeros((8, slots), f32)
    for peer in range(peers):
        tile = recv_ref[peer, rows : rows + 16, :].astype(f32)[0:8]
        fill = fill + tile
        code = code + jnp.where(tile > 0.0, (sub8 + (2 * peer + 1)).astype(f32), 0.0)
    fill = jnp.broadcast_to(jnp.sum(fill, axis=0, keepdims=True), (8, slots))
    owner = jnp.broadcast_to(jnp.sum(code, axis=0, keepdims=True), (8, slots))

    def score_step(t, carry):
        live = fill > jnp.asarray(t, f32)
        for g in range(groups):
            q = recv_ref[:, g * 16 : (g + 1) * 16, :].reshape(requests * 8, HEAD_SIZE)
            k = kv_ref[0, t, :, g * HEAD_SIZE : (g + 1) * HEAD_SIZE]
            s = nt_dot(q, k)
            picked = jnp.zeros((8, slots), f32)
            for r in range(requests):
                picked = jnp.where(owner == float(r + 1), s[r * 8 : (r + 1) * 8], picked)
            score_ref[t, g * 8 : (g + 1) * 8, :] = jnp.where(live, picked * SCALE, LOWEST_SCORE)
        return carry

    for c in range(CHUNKS):
        loads[0][c].wait()
        lax.fori_loop(c * step, (c + 1) * step, score_step, 0, unroll=True)

    owner_h = jnp.broadcast_to(owner[0:1], (heads, slots))
    fill_h = jnp.broadcast_to(fill[0:1], (heads, slots))
    page_max = score_ref[0]
    for t in range(1, page_tok):
        page_max = jnp.maximum(page_max, score_ref[t])
    maxima = []
    owner_max = jnp.zeros((heads, slots), f32)
    for r in range(requests):
        mine = owner_h == float(r + 1)
        top = jnp.max(jnp.where(mine, page_max, LOWEST_TOP), axis=1, keepdims=True)
        top = jnp.round(jnp.maximum(top, LOWEST_TOP))
        maxima.append(top)
        owner_max = jnp.where(mine, top, owner_max)
    factor = jnp.exp(page_max - owner_max)
    page_sum = jnp.zeros((heads, slots), f32)
    sub16 = lax.broadcasted_iota(jnp.int32, (16, slots), 0)
    owner_16 = jnp.broadcast_to(owner[0:1], (16, slots))
    for t in range(page_tok):
        w = jnp.where(fill_h > float(t), jnp.exp(score_ref[t] - page_max), 0.0)
        page_sum = page_sum + w
        scaled = w.astype(bf16).astype(f32) * factor
        high = scaled.astype(bf16).astype(f32)
        score_ref[t] = high
        weight_ref[t] = scaled - high
    page_sum = page_sum * factor
    masks = [
        jnp.where(owner_16 == (2 * k + 1 + sub16 // 8).astype(f32), 1.0, 0.0).astype(bf16)
        for k in range(peers)
    ]
    totals = [
        jnp.sum(jnp.where(owner_h == float(r + 1), page_sum, 0.0), axis=1, keepdims=True)
        for r in range(requests)
    ]
    for c in range(CHUNKS):
        loads[1][c].wait()
    scales = []
    for g in range(groups):
        acc = jnp.zeros((requests * 8, HEAD_SIZE), f32)
        for t0 in range(0, page_tok, 2):
            v = kv_ref[1, t0 : t0 + 2, :, g * HEAD_SIZE : (g + 1) * HEAD_SIZE].reshape(
                2 * slots, HEAD_SIZE
            )
            for ref in (score_ref, weight_ref):
                cols = []
                for t in (t0, t0 + 1):
                    w8 = ref[t, g * 8 : (g + 1) * 8, :]
                    w16 = jnp.concatenate([w8, w8], axis=0).astype(bf16)
                    cols.append(jnp.concatenate([w16 * m for m in masks], axis=0))
                acc = acc + jnp.dot(
                    jnp.concatenate(cols, axis=1), v, preferred_element_type=f32
                )
        k, code = encode_rows(acc)
        scales.append(k)
        out_ref[:, g * 16 : (g + 1) * 16, :] = code.reshape(peers, 16, HEAD_SIZE)
    for peer in range(peers):
        columns = []
        for g in range(groups):
            for row in range(2):
                r = 2 * peer + row
                at = slice(g * 8, (g + 1) * 8)
                columns.append((maxima[r][at], totals[r][at], scales[g][r * 8 : (r + 1) * 8]))
        out_ref[peer, rows : rows + 16, :] = stat_tile(columns, LENDER_UNIT)


LENDER_UNIT = 8.0
OWNER_UNIT = 1.0


def stat_tile(columns, unit):
    tiles = len(columns)
    lane = lax.broadcasted_iota(jnp.int32, (8, HEAD_SIZE), 1)
    top = jnp.zeros((8, HEAD_SIZE), f32)
    total = top
    scale = top
    for c, (m, l, k) in enumerate(columns):
        top = jnp.where(lane == c, m, top)
        total = jnp.where((lane == tiles + c) | (lane == 2 * tiles + c), l, total)
        scale = jnp.where(lane == 3 * tiles + c, k, scale)
    total = total * unit
    whole = jnp.floor(total)
    part = jnp.round((total - whole) * PART)
    tile = jnp.where(lane < tiles, top, jnp.where(lane < 2 * tiles, whole, part))
    tile = jnp.where(lane < 3 * tiles, tile, scale)
    tile = tile.astype(jnp.int32)
    return jnp.concatenate([tile, jnp.zeros_like(tile)], axis=0).astype(jnp.int16)


def merge(parts_ref, groups, unit):
    tiles = 2 * groups
    count = parts_ref.shape[0]
    stats = [
        parts_ref[i, tiles * 8 : tiles * 8 + 16, :].astype(jnp.int32).astype(f32)[0:8]
        for i in range(count)
    ]
    top = stats[0]
    for s in stats[1:]:
        top = jnp.maximum(top, s)
    total = jnp.zeros_like(top)
    scales = []
    for s in stats:
        shifted = [pltpu.roll(s, HEAD_SIZE - n * tiles, axis=1) for n in (1, 2, 3)]
        e = jnp.exp(s - top)
        total = total + (shifted[0] + shifted[1] * (1.0 / PART)) * e
        scales.append(e * (jnp.exp2(shifted[2] * (1.0 / STEPS)) * (1.0 / FULL)))
    sums = []
    for g in range(groups):
        pair = [jnp.zeros((8, HEAD_SIZE), f32)] * 2
        for i in range(count):
            both = parts_ref[i, g * 16 : (g + 1) * 16, :].astype(jnp.int32).astype(f32)
            pair = [
                pair[n] + both[n * 8 : (n + 1) * 8] * scales[i][:, g * 2 + n : g * 2 + n + 1]
                for n in range(2)
            ]
        sums += pair
    return top, total * (1.0 / unit), sums


def combine_kernel(groups, parts_ref, out_ref):
    tiles = 2 * groups
    top, total, sums = merge(parts_ref, groups, LENDER_UNIT)
    coded = [encode_rows(jnp.concatenate(sums[2 * g : 2 * g + 2], axis=0)) for g in range(groups)]
    columns = [
        (top[:, c : c + 1], total[:, c : c + 1], coded[c // 2][0][c % 2 * 8 : c % 2 * 8 + 8])
        for c in range(tiles)
    ]
    stat = stat_tile(columns, OWNER_UNIT)
    for i in range(out_ref.shape[0]):
        for g in range(groups):
            out_ref[i, g * 16 : (g + 1) * 16, :] = coded[g][1]
        out_ref[i, tiles * 8 : tiles * 8 + 16, :] = stat


def new_token_kernel(groups, queries_ref, fresh_ref, out_ref):
    sub = lax.broadcasted_iota(jnp.int32, (8, HEAD_SIZE), 0)
    lane = lax.broadcasted_iota(jnp.int32, (8, HEAD_SIZE), 1)
    fresh_k = fresh_ref[0].astype(f32)
    fresh_v = fresh_ref[1].astype(f32)
    values = jnp.zeros((8, HEAD_SIZE), f32)
    tile = jnp.zeros((8, HEAD_SIZE), f32)
    for g in range(groups):
        both = [
            queries_ref[:, (g * 8 + h) * HEAD_SIZE : (g * 8 + h + 1) * HEAD_SIZE].astype(f32)
            for h in range(8)
        ]
        for row in range(2):
            q = jnp.zeros((8, HEAD_SIZE), f32)
            for h in range(8):
                q = jnp.where(sub == h, both[h][row : row + 1, :], q)
            k = fresh_k[row : row + 1, g * HEAD_SIZE : (g + 1) * HEAD_SIZE]
            new = jnp.sum(q * k, axis=1, keepdims=True) * SCALE
            tile = jnp.where(lane == g * 2 + row, new, tile)
            v = fresh_v[row : row + 1, g * HEAD_SIZE : (g + 1) * HEAD_SIZE]
            values = jnp.where(sub == g * 2 + row, v, values)
    out_ref[0:8, :] = tile
    out_ref[8:16, :] = values


def finish_kernel(groups, parts_ref, token_ref, out_ref):
    top, total, sums = merge(parts_ref, groups, OWNER_UNIT)
    new = token_ref[0:8, :]
    best = jnp.maximum(top, new)
    carried = jnp.exp(top - best)
    own = jnp.exp(new - best)
    denominator = own + total * carried
    for g in range(groups):
        outs = []
        for row in range(2):
            c = g * 2 + row
            at = slice(c, c + 1)
            outs.append(
                (own[:, at] * token_ref[8 + c : 9 + c, :] + sums[c] * carried[:, at])
                / denominator[:, at]
            )
        for h in range(8):
            at = (g * 8 + h) * HEAD_SIZE
            out_ref[:, at : at + HEAD_SIZE] = jnp.concatenate(
                [outs[0][h : h + 1], outs[1][h : h + 1]], axis=0
            ).astype(bf16)


def shards(queries, fresh_key_value, key_value_pool, block_table, lengths):
    lenders = lax.axis_size("inst")
    pages = lax.axis_size("page")
    own_rows = queries.shape[0]
    slots, page_tok, width = key_value_pool.shape[1:]
    groups = width // HEAD_SIZE
    rows = groups * 16
    page_index = lax.axis_index("page").reshape(1).astype(jnp.int32)

    to_send = pl.pallas_call(
        functools.partial(send_kernel, slots, pages),
        out_shape=jax.ShapeDtypeStruct((lenders, rows + 16, HEAD_SIZE), bf16),
        in_specs=[pl.BlockSpec(memory_space=SMEM)] * 2 + vmem_specs(2),
        out_specs=pl.BlockSpec(memory_space=VMEM),
        name="send",
    )(page_index, lengths, queries, block_table)
    received = lax.all_to_all(to_send, "inst", 0, 0)

    kv = pl.pallas_call(
        token_major_kernel,
        out_shape=jax.ShapeDtypeStruct((2, page_tok, slots, width), bf16),
        in_specs=[pl.BlockSpec(memory_space=pl.ANY)],
        out_specs=pl.BlockSpec(memory_space=pl.ANY),
        scratch_shapes=[
            pltpu.VMEM(key_value_pool.shape, bf16),
            pltpu.VMEM((2, page_tok, slots, width), bf16),
            pltpu.SemaphoreType.DMA((2, PARTS)),
            pltpu.SemaphoreType.DMA((2, PARTS)),
        ],
        cost_estimate=pl.CostEstimate(flops=10**9, bytes_accessed=2 * 4 * 2**20, transcendentals=0),
        name="token_major",
    )(key_value_pool)

    partial = pl.pallas_call(
        attend_kernel,
        out_shape=jax.ShapeDtypeStruct((lenders, rows + 16, HEAD_SIZE), jnp.int16),
        in_specs=vmem_specs(1) + [pl.BlockSpec(memory_space=pltpu.MemorySpace.HBM)],
        out_specs=pl.BlockSpec(memory_space=VMEM),
        scratch_shapes=[
            pltpu.VMEM(kv.shape, bf16),
            pltpu.VMEM((page_tok, groups * 8, slots), f32),
            pltpu.VMEM((page_tok, groups * 8, slots), f32),
            pltpu.SemaphoreType.DMA((2, CHUNKS)),
        ],
        compiler_params=pltpu.CompilerParams(vmem_limit_bytes=52 * 2**20),
        name="attend",
    )(received, kv)
    parts = lax.all_to_all(partial, "inst", 0, 0)

    combined = pl.pallas_call(
        functools.partial(combine_kernel, groups),
        out_shape=jax.ShapeDtypeStruct((pages, rows + 16, HEAD_SIZE), jnp.int16),
        in_specs=vmem_specs(1),
        out_specs=pl.BlockSpec(memory_space=VMEM),
        compiler_params=pltpu.CompilerParams(vmem_limit_bytes=16 * 2**20),
        name="combine",
    )(parts)
    combined, last_queries, last_fresh = lax.optimization_barrier(
        (combined, queries, fresh_key_value)
    )
    page_parts = lax.all_to_all(combined, "page", 0, 0)
    token = pl.pallas_call(
        functools.partial(new_token_kernel, groups),
        out_shape=jax.ShapeDtypeStruct((16, HEAD_SIZE), f32),
        in_specs=vmem_specs(2),
        out_specs=pl.BlockSpec(memory_space=VMEM),
        cost_estimate=pl.CostEstimate(flops=10**6, bytes_accessed=2**16, transcendentals=0),
        name="new_token",
    )(last_queries, last_fresh)

    return pl.pallas_call(
        functools.partial(finish_kernel, groups),
        out_shape=jax.ShapeDtypeStruct(queries.shape, bf16),
        in_specs=vmem_specs(2),
        out_specs=pl.BlockSpec(memory_space=VMEM),
        compiler_params=pltpu.CompilerParams(vmem_limit_bytes=16 * 2**20),
        name="finish",
    )(page_parts, token)


def solution(mesh):
    return jax.shard_map(
        shards,
        mesh=mesh,
        in_specs=(
            P("inst", "head"),
            P(None, "inst", "head"),
            P(None, ("inst", "page"), None, "head"),
            P("inst", None),
            P("inst"),
        ),
        out_specs=P("inst", "head"),
        check_vma=False,
    )
```

```python
import functools
import math

import jax
import jax.numpy as jnp
from jax import lax
from jax.experimental import pallas as pl
from jax.experimental.pallas import tpu as pltpu
from jax.sharding import PartitionSpec as P

HEAD_SIZE = 128
LOWEST_SCORE = -1e30
SCALE = 1.0 / math.sqrt(HEAD_SIZE)
VMEM = pltpu.MemorySpace.VMEM
SMEM = pltpu.MemorySpace.SMEM
f32 = jnp.float32
bf16 = jnp.bfloat16


def nt_dot(a, b):
    return lax.dot_general(a, b, (((1,), (1,)), ((), ())), preferred_element_type=f32)


STEPS = 16.0
FULL = 32700.0
LOWEST_TOP = -32000.0
PART = 32767.0


def encode_rows(x):
    top = jnp.max(jnp.abs(x), axis=1, keepdims=True)
    k = jnp.ceil(jnp.log2(jnp.maximum(top, 2.0**-120)) * STEPS)
    code = jnp.round((x * jnp.exp2(k * (-1.0 / STEPS))) * FULL)
    return k, code.astype(jnp.int32).astype(jnp.int16)


def vmem_specs(n):
    return [pl.BlockSpec(memory_space=VMEM)] * n


def send_kernel(slots, pages, page_ref, lengths_ref, queries_ref, table_ref, out_ref):
    peers = out_ref.shape[0]
    own_rows, most_pages = table_ref.shape
    heads = queries_ref.shape[1] // HEAD_SIZE
    page_tok = 16
    slot_bits = slots.bit_length() - 1
    page_bits = pages.bit_length() - 1
    column = lax.broadcasted_iota(jnp.int32, (1, most_pages), 1)
    lender_rows = lax.broadcasted_iota(jnp.int32, (peers, most_pages), 0)
    slot_rows = lax.broadcasted_iota(jnp.int32, (slots, most_pages), 0)
    fills = []
    for row in range(own_rows):
        entry = table_ref[row : row + 1, :]
        fill = jnp.clip(lengths_ref[row] - column * page_tok, 0, page_tok)
        here = ((entry >> slot_bits) & (pages - 1)) == page_ref[0]
        lender = jnp.where(here & (entry >= 0), entry >> (slot_bits + page_bits), -1)
        slot = entry & (slots - 1)
        a = jnp.where(lender_rows == lender, fill.astype(f32), 0.0).astype(bf16)
        b = jnp.where(slot_rows == slot, 1.0, 0.0).astype(bf16)
        fills.append(nt_dot(a, b))
    sub = lax.broadcasted_iota(jnp.int32, (8, HEAD_SIZE), 0)
    pieces = []
    for g in range(heads // 8):
        pair = [jnp.zeros((8, HEAD_SIZE), f32)] * own_rows
        for head in range(8):
            at = (g * 8 + head) * HEAD_SIZE
            both = queries_ref[:, at : at + HEAD_SIZE].astype(f32)
            pair = [
                jnp.where(sub == head, both[row : row + 1, :], pair[row]) for row in range(own_rows)
            ]
        pieces += pair
    queries = jnp.concatenate(pieces, axis=0).astype(bf16)
    rows = own_rows * heads
    sub = lax.broadcasted_iota(jnp.int32, (8, slots), 0)
    for peer in range(peers):
        out_ref[peer, 0:rows, :] = queries
        tile = jnp.zeros((8, slots), f32)
        for row in range(own_rows):
            tile = jnp.where(sub == row, fills[row][peer : peer + 1, :], tile)
        out_ref[peer, rows : rows + 8, :] = tile.astype(bf16)


def new_token(queries_ref, fresh_ref, token_ref):
    groups = fresh_ref.shape[2] // HEAD_SIZE
    sub = lax.broadcasted_iota(jnp.int32, (8, HEAD_SIZE), 0)
    lane = lax.broadcasted_iota(jnp.int32, (8, HEAD_SIZE), 1)
    fresh_k = fresh_ref[0].astype(f32)
    fresh_v = fresh_ref[1].astype(f32)
    scores = jnp.zeros((8, HEAD_SIZE), f32)
    values = jnp.zeros((8, HEAD_SIZE), f32)
    for g in range(groups):
        both = [
            queries_ref[:, (g * 8 + h) * HEAD_SIZE : (g * 8 + h + 1) * HEAD_SIZE].astype(f32)
            for h in range(8)
        ]
        for row in range(2):
            q = jnp.zeros((8, HEAD_SIZE), f32)
            for h in range(8):
                q = jnp.where(sub == h, both[h][row : row + 1, :], q)
            k = fresh_k[row : row + 1, g * HEAD_SIZE : (g + 1) * HEAD_SIZE]
            new = jnp.sum(q * k, axis=1, keepdims=True) * SCALE
            scores = jnp.where(lane == g * 2 + row, new, scores)
            v = fresh_v[row : row + 1, g * HEAD_SIZE : (g + 1) * HEAD_SIZE]
            values = jnp.where(sub == g * 2 + row, v, values)
    token_ref[0:8, :] = scores
    token_ref[8:16, :] = values


PARTS = 2


def token_major_kernel(
    pool_hbm, queries_ref, fresh_ref, out_hbm, token_ref, pool_ref, out_ref, load_sems, store_sems
):
    pages, page_tok, width = pool_hbm.shape[1:]
    chunk = pages // PARTS
    block = page_tok * 16
    loads = []
    stores = []
    for kind in range(2):
        for c in range(PARTS):
            at = pl.ds(c * chunk, chunk)
            loads.append(
                pltpu.make_async_copy(
                    pool_hbm.at[kind, at], pool_ref.at[kind, at], load_sems.at[kind, c]
                )
            )
            stores.append(
                pltpu.make_async_copy(
                    out_ref.at[kind, :, at], out_hbm.at[kind, :, at], store_sems.at[kind, c]
                )
            )
    for load in loads:
        load.start()
    i = lax.broadcasted_iota(jnp.int32, (block, block), 0)
    j = lax.broadcasted_iota(jnp.int32, (block, block), 1)
    new_token(queries_ref, fresh_ref, token_ref)
    perm = jnp.where((i % 16) * page_tok + i // 16 == j, 1.0, 0.0).astype(bf16)
    for kind in range(2):
        for c in range(PARTS):
            loads[kind * PARTS + c].wait()
            for b in range(chunk // 16):
                first = c * chunk + b * 16
                rows = pool_ref[kind, first : first + 16].reshape(block, width)
                moved = jnp.dot(perm, rows, preferred_element_type=f32).astype(bf16)
                out_ref[kind, :, first : first + 16, :] = moved.reshape(page_tok, 16, width)
            stores[kind * PARTS + c].start()
    for store in stores:
        store.wait()


KEY_LOADS = (4, 12)
VALUE_LOADS = (16,)
UNROLL = True


def attend_kernel(recv_ref, kv_hbm, out_ref, kv_ref, score_ref, weight_ref, sems):
    peers = recv_ref.shape[0]
    page_tok, slots, width = kv_ref.shape[1:]
    loads = []
    for kind, sizes in enumerate((KEY_LOADS, VALUE_LOADS)):
        first = 0
        for size in sizes:
            at = pl.ds(first, size)
            copy = pltpu.make_async_copy(
                kv_hbm.at[kind, at], kv_ref.at[kind, at], sems.at[len(loads)]
            )
            copy.start()
            loads.append((first, size, copy))
            first += size
    key_loads = loads[: len(KEY_LOADS)]
    value_loads = loads[len(KEY_LOADS) :]
    groups = width // HEAD_SIZE
    requests = 2 * peers
    heads = groups * 8
    rows = groups * 16
    sub8 = lax.broadcasted_iota(jnp.int32, (8, slots), 0)
    fill = jnp.zeros((8, slots), f32)
    code = jnp.zeros((8, slots), f32)
    for peer in range(peers):
        tile = recv_ref[peer, rows : rows + 8, :].astype(f32)
        fill = fill + tile
        code = code + jnp.where(tile > 0.0, (sub8 + (2 * peer + 1)).astype(f32), 0.0)
    fill = jnp.broadcast_to(jnp.sum(fill, axis=0, keepdims=True), (8, slots))
    owner = jnp.broadcast_to(jnp.sum(code, axis=0, keepdims=True), (8, slots))

    def score_step(t, carry):
        live = fill > jnp.asarray(t, f32)
        for g in range(groups):
            q = recv_ref[:, g * 16 : (g + 1) * 16, :].reshape(requests * 8, HEAD_SIZE)
            k = kv_ref[0, t, :, g * HEAD_SIZE : (g + 1) * HEAD_SIZE]
            s = nt_dot(q, k)
            picked = jnp.zeros((8, slots), f32)
            for r in range(requests):
                picked = jnp.where(owner == float(r + 1), s[r * 8 : (r + 1) * 8], picked)
            score_ref[t, g * 8 : (g + 1) * 8, :] = jnp.where(live, picked * SCALE, LOWEST_SCORE)
        return carry

    for first, size, copy in key_loads:
        copy.wait()
        lax.fori_loop(first, first + size, score_step, 0, unroll=UNROLL)

    owner_h = jnp.broadcast_to(owner[0:1], (heads, slots))
    fill_h = jnp.broadcast_to(fill[0:1], (heads, slots))
    page_max = score_ref[0]
    for t in range(1, page_tok):
        page_max = jnp.maximum(page_max, score_ref[t])
    maxima = []
    owner_max = jnp.zeros((heads, slots), f32)
    for r in range(requests):
        mine = owner_h == float(r + 1)
        top = jnp.max(jnp.where(mine, page_max, LOWEST_TOP), axis=1, keepdims=True)
        top = jnp.round(jnp.maximum(top, LOWEST_TOP))
        maxima.append(top)
        owner_max = jnp.where(mine, top, owner_max)
    factor = jnp.exp(page_max - owner_max)
    page_sum = jnp.zeros((heads, slots), f32)
    sub16 = lax.broadcasted_iota(jnp.int32, (16, slots), 0)
    owner_16 = jnp.broadcast_to(owner[0:1], (16, slots))
    for t in range(page_tok):
        w = jnp.where(fill_h > float(t), jnp.exp(score_ref[t] - page_max), 0.0)
        page_sum = page_sum + w
        scaled = w.astype(bf16).astype(f32) * factor
        high = scaled.astype(bf16).astype(f32)
        score_ref[t] = high
        weight_ref[t] = scaled - high
    page_sum = page_sum * factor
    masks = [
        jnp.where(owner_16 == (2 * k + 1 + sub16 // 8).astype(f32), 1.0, 0.0).astype(bf16)
        for k in range(peers)
    ]
    totals = [
        jnp.sum(jnp.where(owner_h == float(r + 1), page_sum, 0.0), axis=1, keepdims=True)
        for r in range(requests)
    ]
    for _, _, copy in value_loads:
        copy.wait()
    scales = []
    for g in range(groups):
        acc = jnp.zeros((requests * 8, HEAD_SIZE), f32)
        for t0 in range(0, page_tok, 2):
            v = kv_ref[1, t0 : t0 + 2, :, g * HEAD_SIZE : (g + 1) * HEAD_SIZE].reshape(
                2 * slots, HEAD_SIZE
            )
            for ref in (score_ref, weight_ref):
                cols = []
                for t in (t0, t0 + 1):
                    w8 = ref[t, g * 8 : (g + 1) * 8, :]
                    w16 = jnp.concatenate([w8, w8], axis=0).astype(bf16)
                    cols.append(jnp.concatenate([w16 * m for m in masks], axis=0))
                acc = acc + jnp.dot(
                    jnp.concatenate(cols, axis=1), v, preferred_element_type=f32
                )
        k, code = encode_rows(acc)
        scales.append(k)
        out_ref[:, g * 16 : (g + 1) * 16, :] = code.reshape(peers, 16, HEAD_SIZE)
    for peer in range(peers):
        columns = []
        for g in range(groups):
            for row in range(2):
                r = 2 * peer + row
                at = slice(g * 8, (g + 1) * 8)
                columns.append((maxima[r][at], totals[r][at], scales[g][r * 8 : (r + 1) * 8]))
        out_ref[peer, rows : rows + 8, :] = stat_tile(columns, LENDER_UNIT)


LENDER_UNIT = 8.0
OWNER_UNIT = 1.0


def stat_tile(columns, unit):
    tiles = len(columns)
    lane = lax.broadcasted_iota(jnp.int32, (8, HEAD_SIZE), 1)
    top = jnp.zeros((8, HEAD_SIZE), f32)
    total = top
    scale = top
    for c, (m, l, k) in enumerate(columns):
        top = jnp.where(lane == c, m, top)
        total = jnp.where((lane == tiles + c) | (lane == 2 * tiles + c), l, total)
        scale = jnp.where(lane == 3 * tiles + c, k, scale)
    total = total * unit
    whole = jnp.floor(total)
    part = jnp.round((total - whole) * PART)
    tile = jnp.where(lane < tiles, top, jnp.where(lane < 2 * tiles, whole, part))
    tile = jnp.where(lane < 3 * tiles, tile, scale)
    return tile.astype(jnp.int32).astype(jnp.int16)


def merge(parts_ref, groups, unit):
    tiles = 2 * groups
    count = parts_ref.shape[0]
    stats = [
        parts_ref[i, tiles * 8 : tiles * 8 + 8, :].astype(jnp.int32).astype(f32)
        for i in range(count)
    ]
    top = stats[0]
    for s in stats[1:]:
        top = jnp.maximum(top, s)
    total = jnp.zeros_like(top)
    scales = []
    for s in stats:
        shifted = [pltpu.roll(s, HEAD_SIZE - n * tiles, axis=1) for n in (1, 2, 3)]
        e = jnp.exp(s - top)
        total = total + (shifted[0] + shifted[1] * (1.0 / PART)) * e
        scales.append(e * (jnp.exp2(shifted[2] * (1.0 / STEPS)) * (1.0 / FULL)))
    sums = []
    for g in range(groups):
        pair = [jnp.zeros((8, HEAD_SIZE), f32)] * 2
        for i in range(count):
            both = parts_ref[i, g * 16 : (g + 1) * 16, :].astype(jnp.int32).astype(f32)
            pair = [
                pair[n] + both[n * 8 : (n + 1) * 8] * scales[i][:, g * 2 + n : g * 2 + n + 1]
                for n in range(2)
            ]
        sums += pair
    return top, total * (1.0 / unit), sums


def combine_kernel(groups, parts_ref, out_ref):
    tiles = 2 * groups
    top, total, sums = merge(parts_ref, groups, LENDER_UNIT)
    coded = [encode_rows(jnp.concatenate(sums[2 * g : 2 * g + 2], axis=0)) for g in range(groups)]
    columns = [
        (top[:, c : c + 1], total[:, c : c + 1], coded[c // 2][0][c % 2 * 8 : c % 2 * 8 + 8])
        for c in range(tiles)
    ]
    stat = stat_tile(columns, OWNER_UNIT)
    for i in range(out_ref.shape[0]):
        for g in range(groups):
            out_ref[i, g * 16 : (g + 1) * 16, :] = coded[g][1]
        out_ref[i, tiles * 8 : tiles * 8 + 8, :] = stat


def finish_kernel(groups, parts_ref, token_ref, out_ref):
    top, total, sums = merge(parts_ref, groups, OWNER_UNIT)
    new = token_ref[0:8, :]
    best = jnp.maximum(top, new)
    carried = jnp.exp(top - best)
    own = jnp.exp(new - best)
    denominator = own + total * carried
    for g in range(groups):
        outs = []
        for row in range(2):
            c = g * 2 + row
            at = slice(c, c + 1)
            outs.append(
                (own[:, at] * token_ref[8 + c : 9 + c, :] + sums[c] * carried[:, at])
                / denominator[:, at]
            )
        for h in range(8):
            at = (g * 8 + h) * HEAD_SIZE
            out_ref[:, at : at + HEAD_SIZE] = jnp.concatenate(
                [outs[0][h : h + 1], outs[1][h : h + 1]], axis=0
            ).astype(bf16)


def shards(queries, fresh_key_value, key_value_pool, block_table, lengths):
    lenders = lax.axis_size("inst")
    pages = lax.axis_size("page")
    own_rows = queries.shape[0]
    slots, page_tok, width = key_value_pool.shape[1:]
    groups = width // HEAD_SIZE
    rows = groups * 16
    page_index = lax.axis_index("page").reshape(1).astype(jnp.int32)

    to_send = pl.pallas_call(
        functools.partial(send_kernel, slots, pages),
        out_shape=jax.ShapeDtypeStruct((lenders, rows + 8, HEAD_SIZE), bf16),
        in_specs=[pl.BlockSpec(memory_space=SMEM)] * 2 + vmem_specs(2),
        out_specs=pl.BlockSpec(memory_space=VMEM),
        name="send",
    )(page_index, lengths, queries, block_table)
    received = lax.all_to_all(to_send, "inst", 0, 0)

    kv, token = pl.pallas_call(
        token_major_kernel,
        out_shape=(
            jax.ShapeDtypeStruct((2, page_tok, slots, width), bf16),
            jax.ShapeDtypeStruct((16, HEAD_SIZE), f32),
        ),
        in_specs=[pl.BlockSpec(memory_space=pl.ANY)] + vmem_specs(2),
        out_specs=(pl.BlockSpec(memory_space=pl.ANY), pl.BlockSpec(memory_space=VMEM)),
        scratch_shapes=[
            pltpu.VMEM(key_value_pool.shape, bf16),
            pltpu.VMEM((2, page_tok, slots, width), bf16),
            pltpu.SemaphoreType.DMA((2, PARTS)),
            pltpu.SemaphoreType.DMA((2, PARTS)),
        ],
        cost_estimate=pl.CostEstimate(flops=10**9, bytes_accessed=2 * 4 * 2**20, transcendentals=0),
        name="token_major",
    )(key_value_pool, queries, fresh_key_value)

    partial = pl.pallas_call(
        attend_kernel,
        out_shape=jax.ShapeDtypeStruct((lenders, rows + 8, HEAD_SIZE), jnp.int16),
        in_specs=vmem_specs(1) + [pl.BlockSpec(memory_space=pltpu.MemorySpace.HBM)],
        out_specs=pl.BlockSpec(memory_space=VMEM),
        scratch_shapes=[
            pltpu.VMEM(kv.shape, bf16),
            pltpu.VMEM((page_tok, groups * 8, slots), f32),
            pltpu.VMEM((page_tok, groups * 8, slots), f32),
            pltpu.SemaphoreType.DMA((len(KEY_LOADS) + len(VALUE_LOADS),)),
        ],
        compiler_params=pltpu.CompilerParams(vmem_limit_bytes=52 * 2**20),
        name="attend",
    )(received, kv)
    parts = lax.all_to_all(partial, "inst", 0, 0)

    combined = pl.pallas_call(
        functools.partial(combine_kernel, groups),
        out_shape=jax.ShapeDtypeStruct((pages, rows + 8, HEAD_SIZE), jnp.int16),
        in_specs=vmem_specs(1),
        out_specs=pl.BlockSpec(memory_space=VMEM),
        compiler_params=pltpu.CompilerParams(vmem_limit_bytes=16 * 2**20),
        name="combine",
    )(parts)
    page_parts = lax.all_to_all(combined, "page", 0, 0)

    return pl.pallas_call(
        functools.partial(finish_kernel, groups),
        out_shape=jax.ShapeDtypeStruct(queries.shape, bf16),
        in_specs=vmem_specs(2),
        out_specs=pl.BlockSpec(memory_space=VMEM),
        compiler_params=pltpu.CompilerParams(vmem_limit_bytes=16 * 2**20),
        name="finish",
    )(page_parts, token)


def solution(mesh):
    return jax.shard_map(
        shards,
        mesh=mesh,
        in_specs=(
            P("inst", "head"),
            P(None, "inst", "head"),
            P(None, ("inst", "page"), None, "head"),
            P("inst", None),
            P("inst"),
        ),
        out_specs=P("inst", "head"),
        check_vma=False,
    )
```

```python
import functools
import math

import jax
import jax.numpy as jnp
from jax import lax
from jax.experimental import pallas as pl
from jax.experimental.pallas import tpu as pltpu
from jax.sharding import PartitionSpec as P

HEAD_SIZE = 128
LOWEST_SCORE = -1e30
SCALE = 1.0 / math.sqrt(HEAD_SIZE)
VMEM = pltpu.MemorySpace.VMEM
SMEM = pltpu.MemorySpace.SMEM
f32 = jnp.float32
bf16 = jnp.bfloat16


def nt_dot(a, b):
    return lax.dot_general(a, b, (((1,), (1,)), ((), ())), preferred_element_type=f32)


STEPS = 16.0
FULL = 32700.0
LOWEST_TOP = -32000.0
PART = 32767.0


def encode_rows(x):
    top = jnp.max(jnp.abs(x), axis=1, keepdims=True)
    k = jnp.ceil(jnp.log2(jnp.maximum(top, 2.0**-120)) * STEPS)
    code = jnp.round((x * jnp.exp2(k * (-1.0 / STEPS))) * FULL)
    return k, code.astype(jnp.int32).astype(jnp.int16)


def vmem_specs(n):
    return [pl.BlockSpec(memory_space=VMEM)] * n


def send_kernel(slots, pages, page_ref, lengths_ref, queries_ref, table_ref, out_ref):
    peers = out_ref.shape[0]
    own_rows, most_pages = table_ref.shape
    heads = queries_ref.shape[1] // HEAD_SIZE
    page_tok = 16
    slot_bits = slots.bit_length() - 1
    page_bits = pages.bit_length() - 1
    column = lax.broadcasted_iota(jnp.int32, (1, most_pages), 1)
    lender_rows = lax.broadcasted_iota(jnp.int32, (peers, most_pages), 0)
    slot_rows = lax.broadcasted_iota(jnp.int32, (slots, most_pages), 0)
    fills = []
    for row in range(own_rows):
        entry = table_ref[row : row + 1, :]
        fill = jnp.clip(lengths_ref[row] - column * page_tok, 0, page_tok)
        here = ((entry >> slot_bits) & (pages - 1)) == page_ref[0]
        lender = jnp.where(here & (entry >= 0), entry >> (slot_bits + page_bits), -1)
        slot = entry & (slots - 1)
        a = jnp.where(lender_rows == lender, fill.astype(f32), 0.0).astype(bf16)
        b = jnp.where(slot_rows == slot, 1.0, 0.0).astype(bf16)
        fills.append(nt_dot(a, b))
    sub = lax.broadcasted_iota(jnp.int32, (8, HEAD_SIZE), 0)
    pieces = []
    for g in range(heads // 8):
        pair = [jnp.zeros((8, HEAD_SIZE), f32)] * own_rows
        for head in range(8):
            at = (g * 8 + head) * HEAD_SIZE
            both = queries_ref[:, at : at + HEAD_SIZE].astype(f32)
            pair = [
                jnp.where(sub == head, both[row : row + 1, :], pair[row]) for row in range(own_rows)
            ]
        pieces += pair
    queries = jnp.concatenate(pieces, axis=0).astype(bf16)
    rows = own_rows * heads
    sub = lax.broadcasted_iota(jnp.int32, (8, slots), 0)
    for peer in range(peers):
        out_ref[peer, 0:rows, :] = queries
        tile = jnp.zeros((8, slots), f32)
        for row in range(own_rows):
            tile = jnp.where(sub == row, fills[row][peer : peer + 1, :], tile)
        out_ref[peer, rows : rows + 8, :] = tile.astype(bf16)


def new_token(queries_ref, fresh_ref, token_ref):
    groups = fresh_ref.shape[2] // HEAD_SIZE
    sub = lax.broadcasted_iota(jnp.int32, (8, HEAD_SIZE), 0)
    lane = lax.broadcasted_iota(jnp.int32, (8, HEAD_SIZE), 1)
    fresh_k = fresh_ref[0].astype(f32)
    fresh_v = fresh_ref[1].astype(f32)
    scores = jnp.zeros((8, HEAD_SIZE), f32)
    values = jnp.zeros((8, HEAD_SIZE), f32)
    for g in range(groups):
        both = [
            queries_ref[:, (g * 8 + h) * HEAD_SIZE : (g * 8 + h + 1) * HEAD_SIZE].astype(f32)
            for h in range(8)
        ]
        for row in range(2):
            q = jnp.zeros((8, HEAD_SIZE), f32)
            for h in range(8):
                q = jnp.where(sub == h, both[h][row : row + 1, :], q)
            k = fresh_k[row : row + 1, g * HEAD_SIZE : (g + 1) * HEAD_SIZE]
            new = jnp.sum(q * k, axis=1, keepdims=True) * SCALE
            scores = jnp.where(lane == g * 2 + row, new, scores)
            v = fresh_v[row : row + 1, g * HEAD_SIZE : (g + 1) * HEAD_SIZE]
            values = jnp.where(sub == g * 2 + row, v, values)
    token_ref[0:8, :] = scores
    token_ref[8:16, :] = values


PARTS = 2


def token_major_kernel(
    pool_hbm,
    queries_hbm,
    fresh_hbm,
    out_hbm,
    token_hbm,
    pool_ref,
    queries_ref,
    fresh_ref,
    out_ref,
    token_ref,
    load_sems,
    store_sems,
    token_sems,
):
    pages, page_tok, width = pool_hbm.shape[1:]
    chunk = pages // PARTS
    block = page_tok * 16
    loads = []
    stores = []
    for kind in range(2):
        for c in range(PARTS):
            at = pl.ds(c * chunk, chunk)
            loads.append(
                pltpu.make_async_copy(
                    pool_hbm.at[kind, at], pool_ref.at[kind, at], load_sems.at[kind, c]
                )
            )
            stores.append(
                pltpu.make_async_copy(
                    out_ref.at[kind, :, at], out_hbm.at[kind, :, at], store_sems.at[kind, c]
                )
            )
    for load in loads:
        load.start()
    small = [
        pltpu.make_async_copy(queries_hbm, queries_ref, token_sems.at[0]),
        pltpu.make_async_copy(fresh_hbm, fresh_ref, token_sems.at[1]),
    ]
    for load in small:
        load.start()
    i = lax.broadcasted_iota(jnp.int32, (block, block), 0)
    j = lax.broadcasted_iota(jnp.int32, (block, block), 1)
    perm = jnp.where((i % 16) * page_tok + i // 16 == j, 1.0, 0.0).astype(bf16)
    for kind in range(2):
        for c in range(PARTS):
            loads[kind * PARTS + c].wait()
            if kind == 1 and c == PARTS - 1:
                for load in small:
                    load.wait()
                new_token(queries_ref, fresh_ref, token_ref)
                stores.append(pltpu.make_async_copy(token_ref, token_hbm, token_sems.at[2]))
                stores[-1].start()
            for b in range(chunk // 16):
                first = c * chunk + b * 16
                rows = pool_ref[kind, first : first + 16].reshape(block, width)
                moved = jnp.dot(perm, rows, preferred_element_type=f32).astype(bf16)
                out_ref[kind, :, first : first + 16, :] = moved.reshape(page_tok, 16, width)
            stores[kind * PARTS + c].start()
    for store in stores:
        store.wait()


KEY_LOADS = (4, 12)
VALUE_LOADS = (16,)
UNROLL = True


def attend_kernel(recv_ref, kv_hbm, out_ref, kv_ref, score_ref, weight_ref, sems):
    peers = recv_ref.shape[0]
    page_tok, slots, width = kv_ref.shape[1:]
    loads = []
    for kind, sizes in enumerate((KEY_LOADS, VALUE_LOADS)):
        first = 0
        for size in sizes:
            at = pl.ds(first, size)
            copy = pltpu.make_async_copy(
                kv_hbm.at[kind, at], kv_ref.at[kind, at], sems.at[len(loads)]
            )
            copy.start()
            loads.append((first, size, copy))
            first += size
    key_loads = loads[: len(KEY_LOADS)]
    value_loads = loads[len(KEY_LOADS) :]
    groups = width // HEAD_SIZE
    requests = 2 * peers
    heads = groups * 8
    rows = groups * 16
    sub8 = lax.broadcasted_iota(jnp.int32, (8, slots), 0)
    fill = jnp.zeros((8, slots), f32)
    code = jnp.zeros((8, slots), f32)
    for peer in range(peers):
        tile = recv_ref[peer, rows : rows + 8, :].astype(f32)
        fill = fill + tile
        code = code + jnp.where(tile > 0.0, (sub8 + (2 * peer + 1)).astype(f32), 0.0)
    fill = jnp.broadcast_to(jnp.sum(fill, axis=0, keepdims=True), (8, slots))
    owner = jnp.broadcast_to(jnp.sum(code, axis=0, keepdims=True), (8, slots))

    def score_step(t, carry):
        live = fill > jnp.asarray(t, f32)
        for g in range(groups):
            q = recv_ref[:, g * 16 : (g + 1) * 16, :].reshape(requests * 8, HEAD_SIZE)
            k = kv_ref[0, t, :, g * HEAD_SIZE : (g + 1) * HEAD_SIZE]
            s = nt_dot(q, k)
            picked = jnp.zeros((8, slots), f32)
            for r in range(requests):
                picked = jnp.where(owner == float(r + 1), s[r * 8 : (r + 1) * 8], picked)
            score_ref[t, g * 8 : (g + 1) * 8, :] = jnp.where(live, picked * SCALE, LOWEST_SCORE)
        return carry

    for first, size, copy in key_loads:
        copy.wait()
        lax.fori_loop(first, first + size, score_step, 0, unroll=UNROLL)

    for _, _, copy in value_loads:
        copy.wait()
    owner_h = jnp.broadcast_to(owner[0:1], (heads, slots))
    fill_h = jnp.broadcast_to(fill[0:1], (heads, slots))
    page_max = score_ref[0]
    for t in range(1, page_tok):
        page_max = jnp.maximum(page_max, score_ref[t])
    maxima = []
    owner_max = jnp.zeros((heads, slots), f32)
    for r in range(requests):
        mine = owner_h == float(r + 1)
        top = jnp.max(jnp.where(mine, page_max, LOWEST_TOP), axis=1, keepdims=True)
        top = jnp.round(jnp.maximum(top, LOWEST_TOP))
        maxima.append(top)
        owner_max = jnp.where(mine, top, owner_max)
    factor = jnp.exp(page_max - owner_max)
    page_sum = jnp.zeros((heads, slots), f32)
    sub16 = lax.broadcasted_iota(jnp.int32, (16, slots), 0)
    owner_16 = jnp.broadcast_to(owner[0:1], (16, slots))
    for t in range(page_tok):
        w = jnp.where(fill_h > float(t), jnp.exp(score_ref[t] - page_max), 0.0)
        page_sum = page_sum + w
        scaled = w.astype(bf16).astype(f32) * factor
        high = scaled.astype(bf16).astype(f32)
        score_ref[t] = high
        weight_ref[t] = scaled - high
    page_sum = page_sum * factor
    masks = [
        jnp.where(owner_16 == (2 * k + 1 + sub16 // 8).astype(f32), 1.0, 0.0).astype(bf16)
        for k in range(peers)
    ]
    totals = [
        jnp.sum(jnp.where(owner_h == float(r + 1), page_sum, 0.0), axis=1, keepdims=True)
        for r in range(requests)
    ]
    scales = []
    for g in range(groups):
        acc = jnp.zeros((requests * 8, HEAD_SIZE), f32)
        for t0 in range(0, page_tok, 2):
            v = kv_ref[1, t0 : t0 + 2, :, g * HEAD_SIZE : (g + 1) * HEAD_SIZE].reshape(
                2 * slots, HEAD_SIZE
            )
            for ref in (score_ref, weight_ref):
                cols = []
                for t in (t0, t0 + 1):
                    w8 = ref[t, g * 8 : (g + 1) * 8, :]
                    w16 = jnp.concatenate([w8, w8], axis=0).astype(bf16)
                    cols.append(jnp.concatenate([w16 * m for m in masks], axis=0))
                acc = acc + jnp.dot(
                    jnp.concatenate(cols, axis=1), v, preferred_element_type=f32
                )
        k, code = encode_rows(acc)
        scales.append(k)
        out_ref[:, g * 16 : (g + 1) * 16, :] = code.reshape(peers, 16, HEAD_SIZE)
    for peer in range(peers):
        columns = []
        for g in range(groups):
            for row in range(2):
                r = 2 * peer + row
                at = slice(g * 8, (g + 1) * 8)
                columns.append((maxima[r][at], totals[r][at], scales[g][r * 8 : (r + 1) * 8]))
        out_ref[peer, rows : rows + 8, :] = stat_tile(columns, LENDER_UNIT)


LENDER_UNIT = 8.0
OWNER_UNIT = 1.0


def stat_tile(columns, unit):
    tiles = len(columns)
    lane = lax.broadcasted_iota(jnp.int32, (8, HEAD_SIZE), 1)
    top = jnp.zeros((8, HEAD_SIZE), f32)
    total = top
    scale = top
    for c, (m, l, k) in enumerate(columns):
        top = jnp.where(lane == c, m, top)
        total = jnp.where((lane == tiles + c) | (lane == 2 * tiles + c), l, total)
        scale = jnp.where(lane == 3 * tiles + c, k, scale)
    total = total * unit
    whole = jnp.floor(total)
    part = jnp.round((total - whole) * PART)
    tile = jnp.where(lane < tiles, top, jnp.where(lane < 2 * tiles, whole, part))
    tile = jnp.where(lane < 3 * tiles, tile, scale)
    return tile.astype(jnp.int32).astype(jnp.int16)


def merge(parts_ref, groups, unit):
    tiles = 2 * groups
    count = parts_ref.shape[0]
    stats = [
        parts_ref[i, tiles * 8 : tiles * 8 + 8, :].astype(jnp.int32).astype(f32)
        for i in range(count)
    ]
    top = stats[0]
    for s in stats[1:]:
        top = jnp.maximum(top, s)
    total = jnp.zeros_like(top)
    scales = []
    for s in stats:
        shifted = [pltpu.roll(s, HEAD_SIZE - n * tiles, axis=1) for n in (1, 2, 3)]
        e = jnp.exp(s - top)
        total = total + (shifted[0] + shifted[1] * (1.0 / PART)) * e
        scales.append(e * (jnp.exp2(shifted[2] * (1.0 / STEPS)) * (1.0 / FULL)))
    sums = []
    for g in range(groups):
        pair = [jnp.zeros((8, HEAD_SIZE), f32)] * 2
        for i in range(count):
            both = parts_ref[i, g * 16 : (g + 1) * 16, :].astype(jnp.int32).astype(f32)
            pair = [
                pair[n] + both[n * 8 : (n + 1) * 8] * scales[i][:, g * 2 + n : g * 2 + n + 1]
                for n in range(2)
            ]
        sums += pair
    return top, total * (1.0 / unit), sums


def combine_kernel(groups, parts_ref, out_ref):
    tiles = 2 * groups
    top, total, sums = merge(parts_ref, groups, LENDER_UNIT)
    coded = [encode_rows(jnp.concatenate(sums[2 * g : 2 * g + 2], axis=0)) for g in range(groups)]
    columns = [
        (top[:, c : c + 1], total[:, c : c + 1], coded[c // 2][0][c % 2 * 8 : c % 2 * 8 + 8])
        for c in range(tiles)
    ]
    stat = stat_tile(columns, OWNER_UNIT)
    for i in range(out_ref.shape[0]):
        for g in range(groups):
            out_ref[i, g * 16 : (g + 1) * 16, :] = coded[g][1]
        out_ref[i, tiles * 8 : tiles * 8 + 8, :] = stat


def finish_kernel(groups, parts_ref, token_ref, out_ref):
    top, total, sums = merge(parts_ref, groups, OWNER_UNIT)
    new = token_ref[0:8, :]
    best = jnp.maximum(top, new)
    carried = jnp.exp(top - best)
    own = jnp.exp(new - best)
    denominator = own + total * carried
    for g in range(groups):
        outs = []
        for row in range(2):
            c = g * 2 + row
            at = slice(c, c + 1)
            outs.append(
                (own[:, at] * token_ref[8 + c : 9 + c, :] + sums[c] * carried[:, at])
                / denominator[:, at]
            )
        for h in range(8):
            at = (g * 8 + h) * HEAD_SIZE
            out_ref[:, at : at + HEAD_SIZE] = jnp.concatenate(
                [outs[0][h : h + 1], outs[1][h : h + 1]], axis=0
            ).astype(bf16)


def shards(queries, fresh_key_value, key_value_pool, block_table, lengths):
    lenders = lax.axis_size("inst")
    pages = lax.axis_size("page")
    own_rows = queries.shape[0]
    slots, page_tok, width = key_value_pool.shape[1:]
    groups = width // HEAD_SIZE
    rows = groups * 16
    page_index = lax.axis_index("page").reshape(1).astype(jnp.int32)

    to_send = pl.pallas_call(
        functools.partial(send_kernel, slots, pages),
        out_shape=jax.ShapeDtypeStruct((lenders, rows + 8, HEAD_SIZE), bf16),
        in_specs=[pl.BlockSpec(memory_space=SMEM)] * 2 + vmem_specs(2),
        out_specs=pl.BlockSpec(memory_space=VMEM),
        name="send",
    )(page_index, lengths, queries, block_table)
    received = lax.all_to_all(to_send, "inst", 0, 0)

    kv, token = pl.pallas_call(
        token_major_kernel,
        out_shape=(
            jax.ShapeDtypeStruct((2, page_tok, slots, width), bf16),
            jax.ShapeDtypeStruct((16, HEAD_SIZE), f32),
        ),
        in_specs=[pl.BlockSpec(memory_space=pl.ANY)] * 3,
        out_specs=(pl.BlockSpec(memory_space=pl.ANY),) * 2,
        scratch_shapes=[
            pltpu.VMEM(key_value_pool.shape, bf16),
            pltpu.VMEM(queries.shape, bf16),
            pltpu.VMEM(fresh_key_value.shape, bf16),
            pltpu.VMEM((2, page_tok, slots, width), bf16),
            pltpu.VMEM((16, HEAD_SIZE), f32),
            pltpu.SemaphoreType.DMA((2, PARTS)),
            pltpu.SemaphoreType.DMA((2, PARTS)),
            pltpu.SemaphoreType.DMA((3,)),
        ],
        cost_estimate=pl.CostEstimate(flops=10**9, bytes_accessed=2 * 4 * 2**20, transcendentals=0),
        name="token_major",
    )(key_value_pool, queries, fresh_key_value)

    partial = pl.pallas_call(
        attend_kernel,
        out_shape=jax.ShapeDtypeStruct((lenders, rows + 8, HEAD_SIZE), jnp.int16),
        in_specs=vmem_specs(1) + [pl.BlockSpec(memory_space=pltpu.MemorySpace.HBM)],
        out_specs=pl.BlockSpec(memory_space=VMEM),
        scratch_shapes=[
            pltpu.VMEM(kv.shape, bf16),
            pltpu.VMEM((page_tok, groups * 8, slots), f32),
            pltpu.VMEM((page_tok, groups * 8, slots), f32),
            pltpu.SemaphoreType.DMA((len(KEY_LOADS) + len(VALUE_LOADS),)),
        ],
        compiler_params=pltpu.CompilerParams(vmem_limit_bytes=52 * 2**20),
        name="attend",
    )(received, kv)
    parts = lax.all_to_all(partial, "inst", 0, 0)

    combined = pl.pallas_call(
        functools.partial(combine_kernel, groups),
        out_shape=jax.ShapeDtypeStruct((pages, rows + 8, HEAD_SIZE), jnp.int16),
        in_specs=vmem_specs(1),
        out_specs=pl.BlockSpec(memory_space=VMEM),
        compiler_params=pltpu.CompilerParams(vmem_limit_bytes=16 * 2**20),
        name="combine",
    )(parts)
    page_parts = lax.all_to_all(combined, "page", 0, 0)

    return pl.pallas_call(
        functools.partial(finish_kernel, groups),
        out_shape=jax.ShapeDtypeStruct(queries.shape, bf16),
        in_specs=vmem_specs(2),
        out_specs=pl.BlockSpec(memory_space=VMEM),
        compiler_params=pltpu.CompilerParams(vmem_limit_bytes=16 * 2**20),
        name="finish",
    )(page_parts, token)


def solution(mesh):
    return jax.shard_map(
        shards,
        mesh=mesh,
        in_specs=(
            P("inst", "head"),
            P(None, "inst", "head"),
            P(None, ("inst", "page"), None, "head"),
            P("inst", None),
            P("inst"),
        ),
        out_specs=P("inst", "head"),
        check_vma=False,
    )
```

```python
import functools
import math

import jax
import jax.numpy as jnp
from jax import lax
from jax.experimental import pallas as pl
from jax.experimental.pallas import tpu as pltpu
from jax.sharding import PartitionSpec as P

HEAD_SIZE = 128
LOWEST_SCORE = -1e30
SCALE = 1.0 / math.sqrt(HEAD_SIZE)
VMEM = pltpu.MemorySpace.VMEM
SMEM = pltpu.MemorySpace.SMEM
f32 = jnp.float32
bf16 = jnp.bfloat16


def nt_dot(a, b):
    return lax.dot_general(a, b, (((1,), (1,)), ((), ())), preferred_element_type=f32)


STEPS = 16.0
FULL = 32700.0
LOWEST_TOP = -32000.0
PART = 32767.0


def encode_rows(x):
    top = jnp.max(jnp.abs(x), axis=1, keepdims=True)
    k = jnp.ceil(jnp.log2(jnp.maximum(top, 2.0**-120)) * STEPS)
    code = jnp.round((x * jnp.exp2(k * (-1.0 / STEPS))) * FULL)
    return k, code.astype(jnp.int32).astype(jnp.int16)


def vmem_specs(n):
    return [pl.BlockSpec(memory_space=VMEM)] * n


def send_kernel(slots, pages, page_ref, lengths_ref, queries_ref, table_ref, out_ref):
    peers = out_ref.shape[0]
    own_rows, most_pages = table_ref.shape
    heads = queries_ref.shape[1] // HEAD_SIZE
    page_tok = 16
    slot_bits = slots.bit_length() - 1
    page_bits = pages.bit_length() - 1
    column = lax.broadcasted_iota(jnp.int32, (1, most_pages), 1)
    lender_rows = lax.broadcasted_iota(jnp.int32, (peers, most_pages), 0)
    slot_rows = lax.broadcasted_iota(jnp.int32, (slots, most_pages), 0)
    fills = []
    for row in range(own_rows):
        entry = table_ref[row : row + 1, :]
        fill = jnp.clip(lengths_ref[row] - column * page_tok, 0, page_tok)
        here = ((entry >> slot_bits) & (pages - 1)) == page_ref[0]
        lender = jnp.where(here & (entry >= 0), entry >> (slot_bits + page_bits), -1)
        slot = entry & (slots - 1)
        a = jnp.where(lender_rows == lender, fill.astype(f32), 0.0).astype(bf16)
        b = jnp.where(slot_rows == slot, 1.0, 0.0).astype(bf16)
        fills.append(nt_dot(a, b))
    sub = lax.broadcasted_iota(jnp.int32, (8, HEAD_SIZE), 0)
    pieces = []
    for g in range(heads // 8):
        pair = [jnp.zeros((8, HEAD_SIZE), f32)] * own_rows
        for head in range(8):
            at = (g * 8 + head) * HEAD_SIZE
            both = queries_ref[:, at : at + HEAD_SIZE].astype(f32)
            pair = [
                jnp.where(sub == head, both[row : row + 1, :], pair[row]) for row in range(own_rows)
            ]
        pieces += pair
    queries = jnp.concatenate(pieces, axis=0).astype(bf16)
    rows = own_rows * heads
    sub = lax.broadcasted_iota(jnp.int32, (8, slots), 0)
    for peer in range(peers):
        out_ref[peer, 0:rows, :] = queries
        tile = jnp.zeros((8, slots), f32)
        for row in range(own_rows):
            tile = jnp.where(sub == row, fills[row][peer : peer + 1, :], tile)
        out_ref[peer, rows : rows + 8, :] = tile.astype(bf16)


def new_token(queries_ref, fresh_ref, token_ref):
    groups = fresh_ref.shape[2] // HEAD_SIZE
    sub = lax.broadcasted_iota(jnp.int32, (8, HEAD_SIZE), 0)
    lane = lax.broadcasted_iota(jnp.int32, (8, HEAD_SIZE), 1)
    fresh_k = fresh_ref[0].astype(f32)
    fresh_v = fresh_ref[1].astype(f32)
    scores = jnp.zeros((8, HEAD_SIZE), f32)
    values = jnp.zeros((8, HEAD_SIZE), f32)
    for g in range(groups):
        both = [
            queries_ref[:, (g * 8 + h) * HEAD_SIZE : (g * 8 + h + 1) * HEAD_SIZE].astype(f32)
            for h in range(8)
        ]
        for row in range(2):
            q = jnp.zeros((8, HEAD_SIZE), f32)
            for h in range(8):
                q = jnp.where(sub == h, both[h][row : row + 1, :], q)
            k = fresh_k[row : row + 1, g * HEAD_SIZE : (g + 1) * HEAD_SIZE]
            new = jnp.sum(q * k, axis=1, keepdims=True) * SCALE
            scores = jnp.where(lane == g * 2 + row, new, scores)
            v = fresh_v[row : row + 1, g * HEAD_SIZE : (g + 1) * HEAD_SIZE]
            values = jnp.where(sub == g * 2 + row, v, values)
    token_ref[0:8, :] = scores
    token_ref[8:16, :] = values


PARTS = 2


def token_major_kernel(
    pool_hbm, keys_ref, values_hbm, pool_ref, values_ref, load_sems, store_sems
):
    pages, page_tok, width = pool_hbm.shape[1:]
    chunk = pages // PARTS
    block = page_tok * 16
    loads = []
    stores = []
    for kind in (1, 0):
        for c in range(PARTS):
            at = pl.ds(c * chunk, chunk)
            loads.append(
                pltpu.make_async_copy(
                    pool_hbm.at[kind, at], pool_ref.at[kind, at], load_sems.at[kind, c]
                )
            )
            if kind == 1:
                stores.append(
                    pltpu.make_async_copy(
                        values_ref.at[:, at], values_hbm.at[:, at], store_sems.at[c]
                    )
                )
    for load in loads:
        load.start()
    i = lax.broadcasted_iota(jnp.int32, (block, block), 0)
    j = lax.broadcasted_iota(jnp.int32, (block, block), 1)
    perm = jnp.where((i % 16) * page_tok + i // 16 == j, 1.0, 0.0).astype(bf16)
    for kind in (1, 0):
        out_ref = values_ref if kind == 1 else keys_ref
        for c in range(PARTS):
            loads[(1 - kind) * PARTS + c].wait()
            for b in range(chunk // 16):
                first = c * chunk + b * 16
                rows = pool_ref[kind, first : first + 16].reshape(block, width)
                moved = jnp.dot(perm, rows, preferred_element_type=f32).astype(bf16)
                out_ref[:, first : first + 16, :] = moved.reshape(page_tok, 16, width)
            if kind == 1:
                stores[c].start()
    for store in stores:
        store.wait()


def attend_kernel(
    recv_ref,
    keys_ref,
    queries_ref,
    fresh_ref,
    values_hbm,
    out_ref,
    token_ref,
    values_ref,
    score_ref,
    weight_ref,
    sem,
):
    peers = recv_ref.shape[0]
    page_tok, slots, width = keys_ref.shape
    load = pltpu.make_async_copy(values_hbm, values_ref, sem)
    load.start()
    groups = width // HEAD_SIZE
    requests = 2 * peers
    heads = groups * 8
    rows = groups * 16
    sub8 = lax.broadcasted_iota(jnp.int32, (8, slots), 0)
    fill = jnp.zeros((8, slots), f32)
    code = jnp.zeros((8, slots), f32)
    for peer in range(peers):
        tile = recv_ref[peer, rows : rows + 8, :].astype(f32)
        fill = fill + tile
        code = code + jnp.where(tile > 0.0, (sub8 + (2 * peer + 1)).astype(f32), 0.0)
    fill = jnp.broadcast_to(jnp.sum(fill, axis=0, keepdims=True), (8, slots))
    owner = jnp.broadcast_to(jnp.sum(code, axis=0, keepdims=True), (8, slots))

    def score_step(t, carry):
        live = fill > jnp.asarray(t, f32)
        for g in range(groups):
            q = recv_ref[:, g * 16 : (g + 1) * 16, :].reshape(requests * 8, HEAD_SIZE)
            k = keys_ref[t, :, g * HEAD_SIZE : (g + 1) * HEAD_SIZE]
            s = nt_dot(q, k)
            picked = jnp.zeros((8, slots), f32)
            for r in range(requests):
                picked = jnp.where(owner == float(r + 1), s[r * 8 : (r + 1) * 8], picked)
            score_ref[t, g * 8 : (g + 1) * 8, :] = jnp.where(live, picked * SCALE, LOWEST_SCORE)
        return carry

    lax.fori_loop(0, page_tok, score_step, 0, unroll=True)

    load.wait()
    new_token(queries_ref, fresh_ref, token_ref)
    owner_h = jnp.broadcast_to(owner[0:1], (heads, slots))
    fill_h = jnp.broadcast_to(fill[0:1], (heads, slots))
    page_max = score_ref[0]
    for t in range(1, page_tok):
        page_max = jnp.maximum(page_max, score_ref[t])
    maxima = []
    owner_max = jnp.zeros((heads, slots), f32)
    for r in range(requests):
        mine = owner_h == float(r + 1)
        top = jnp.max(jnp.where(mine, page_max, LOWEST_TOP), axis=1, keepdims=True)
        top = jnp.round(jnp.maximum(top, LOWEST_TOP))
        maxima.append(top)
        owner_max = jnp.where(mine, top, owner_max)
    factor = jnp.exp(page_max - owner_max)
    page_sum = jnp.zeros((heads, slots), f32)
    sub16 = lax.broadcasted_iota(jnp.int32, (16, slots), 0)
    owner_16 = jnp.broadcast_to(owner[0:1], (16, slots))
    for t in range(page_tok):
        w = jnp.where(fill_h > float(t), jnp.exp(score_ref[t] - page_max), 0.0)
        page_sum = page_sum + w
        scaled = w.astype(bf16).astype(f32) * factor
        high = scaled.astype(bf16).astype(f32)
        score_ref[t] = high
        weight_ref[t] = scaled - high
    page_sum = page_sum * factor
    masks = [
        jnp.where(owner_16 == (2 * k + 1 + sub16 // 8).astype(f32), 1.0, 0.0).astype(bf16)
        for k in range(peers)
    ]
    totals = [
        jnp.sum(jnp.where(owner_h == float(r + 1), page_sum, 0.0), axis=1, keepdims=True)
        for r in range(requests)
    ]
    scales = []
    for g in range(groups):
        acc = jnp.zeros((requests * 8, HEAD_SIZE), f32)
        for t0 in range(0, page_tok, 2):
            v = values_ref[t0 : t0 + 2, :, g * HEAD_SIZE : (g + 1) * HEAD_SIZE].reshape(
                2 * slots, HEAD_SIZE
            )
            for ref in (score_ref, weight_ref):
                cols = []
                for t in (t0, t0 + 1):
                    w8 = ref[t, g * 8 : (g + 1) * 8, :]
                    w16 = jnp.concatenate([w8, w8], axis=0).astype(bf16)
                    cols.append(jnp.concatenate([w16 * m for m in masks], axis=0))
                acc = acc + jnp.dot(
                    jnp.concatenate(cols, axis=1), v, preferred_element_type=f32
                )
        k, code = encode_rows(acc)
        scales.append(k)
        out_ref[:, g * 16 : (g + 1) * 16, :] = code.reshape(peers, 16, HEAD_SIZE)
    for peer in range(peers):
        columns = []
        for g in range(groups):
            for row in range(2):
                r = 2 * peer + row
                at = slice(g * 8, (g + 1) * 8)
                columns.append((maxima[r][at], totals[r][at], scales[g][r * 8 : (r + 1) * 8]))
        out_ref[peer, rows : rows + 8, :] = stat_tile(columns, LENDER_UNIT)


LENDER_UNIT = 8.0
OWNER_UNIT = 1.0


def stat_tile(columns, unit):
    tiles = len(columns)
    lane = lax.broadcasted_iota(jnp.int32, (8, HEAD_SIZE), 1)
    top = jnp.zeros((8, HEAD_SIZE), f32)
    total = top
    scale = top
    for c, (m, l, k) in enumerate(columns):
        top = jnp.where(lane == c, m, top)
        total = jnp.where((lane == tiles + c) | (lane == 2 * tiles + c), l, total)
        scale = jnp.where(lane == 3 * tiles + c, k, scale)
    total = total * unit
    whole = jnp.floor(total)
    part = jnp.round((total - whole) * PART)
    tile = jnp.where(lane < tiles, top, jnp.where(lane < 2 * tiles, whole, part))
    tile = jnp.where(lane < 3 * tiles, tile, scale)
    return tile.astype(jnp.int32).astype(jnp.int16)


def merge(parts_ref, groups, unit):
    tiles = 2 * groups
    count = parts_ref.shape[0]
    stats = [
        parts_ref[i, tiles * 8 : tiles * 8 + 8, :].astype(jnp.int32).astype(f32)
        for i in range(count)
    ]
    top = stats[0]
    for s in stats[1:]:
        top = jnp.maximum(top, s)
    total = jnp.zeros_like(top)
    scales = []
    for s in stats:
        shifted = [pltpu.roll(s, HEAD_SIZE - n * tiles, axis=1) for n in (1, 2, 3)]
        e = jnp.exp(s - top)
        total = total + (shifted[0] + shifted[1] * (1.0 / PART)) * e
        scales.append(e * (jnp.exp2(shifted[2] * (1.0 / STEPS)) * (1.0 / FULL)))
    sums = []
    for g in range(groups):
        pair = [jnp.zeros((8, HEAD_SIZE), f32)] * 2
        for i in range(count):
            both = parts_ref[i, g * 16 : (g + 1) * 16, :].astype(jnp.int32).astype(f32)
            pair = [
                pair[n] + both[n * 8 : (n + 1) * 8] * scales[i][:, g * 2 + n : g * 2 + n + 1]
                for n in range(2)
            ]
        sums += pair
    return top, total * (1.0 / unit), sums


def combine_kernel(groups, parts_ref, out_ref):
    tiles = 2 * groups
    top, total, sums = merge(parts_ref, groups, LENDER_UNIT)
    coded = [encode_rows(jnp.concatenate(sums[2 * g : 2 * g + 2], axis=0)) for g in range(groups)]
    columns = [
        (top[:, c : c + 1], total[:, c : c + 1], coded[c // 2][0][c % 2 * 8 : c % 2 * 8 + 8])
        for c in range(tiles)
    ]
    stat = stat_tile(columns, OWNER_UNIT)
    for i in range(out_ref.shape[0]):
        for g in range(groups):
            out_ref[i, g * 16 : (g + 1) * 16, :] = coded[g][1]
        out_ref[i, tiles * 8 : tiles * 8 + 8, :] = stat


def finish_kernel(groups, parts_ref, token_ref, out_ref):
    top, total, sums = merge(parts_ref, groups, OWNER_UNIT)
    new = token_ref[0:8, :]
    best = jnp.maximum(top, new)
    carried = jnp.exp(top - best)
    own = jnp.exp(new - best)
    denominator = own + total * carried
    for g in range(groups):
        outs = []
        for row in range(2):
            c = g * 2 + row
            at = slice(c, c + 1)
            outs.append(
                (own[:, at] * token_ref[8 + c : 9 + c, :] + sums[c] * carried[:, at])
                / denominator[:, at]
            )
        for h in range(8):
            at = (g * 8 + h) * HEAD_SIZE
            out_ref[:, at : at + HEAD_SIZE] = jnp.concatenate(
                [outs[0][h : h + 1], outs[1][h : h + 1]], axis=0
            ).astype(bf16)


def shards(queries, fresh_key_value, key_value_pool, block_table, lengths):
    lenders = lax.axis_size("inst")
    pages = lax.axis_size("page")
    own_rows = queries.shape[0]
    slots, page_tok, width = key_value_pool.shape[1:]
    groups = width // HEAD_SIZE
    rows = groups * 16
    page_index = lax.axis_index("page").reshape(1).astype(jnp.int32)

    to_send = pl.pallas_call(
        functools.partial(send_kernel, slots, pages),
        out_shape=jax.ShapeDtypeStruct((lenders, rows + 8, HEAD_SIZE), bf16),
        in_specs=[pl.BlockSpec(memory_space=SMEM)] * 2 + vmem_specs(2),
        out_specs=pl.BlockSpec(memory_space=VMEM),
        name="send",
    )(page_index, lengths, queries, block_table)
    received = lax.all_to_all(to_send, "inst", 0, 0)

    keys, values = pl.pallas_call(
        token_major_kernel,
        out_shape=(
            jax.ShapeDtypeStruct((page_tok, slots, width), bf16),
            jax.ShapeDtypeStruct((page_tok, slots, width), bf16),
        ),
        in_specs=[pl.BlockSpec(memory_space=pl.ANY)],
        out_specs=(pl.BlockSpec(memory_space=VMEM), pl.BlockSpec(memory_space=pl.ANY)),
        scratch_shapes=[
            pltpu.VMEM(key_value_pool.shape, bf16),
            pltpu.VMEM((page_tok, slots, width), bf16),
            pltpu.SemaphoreType.DMA((2, PARTS)),
            pltpu.SemaphoreType.DMA((PARTS,)),
        ],
        cost_estimate=pl.CostEstimate(flops=10**9, bytes_accessed=2 * 4 * 2**20, transcendentals=0),
        compiler_params=pltpu.CompilerParams(vmem_limit_bytes=50 * 2**20),
        name="token_major",
    )(key_value_pool)

    partial, token = pl.pallas_call(
        attend_kernel,
        out_shape=(
            jax.ShapeDtypeStruct((lenders, rows + 8, HEAD_SIZE), jnp.int16),
            jax.ShapeDtypeStruct((16, HEAD_SIZE), f32),
        ),
        in_specs=vmem_specs(4) + [pl.BlockSpec(memory_space=pl.ANY)],
        out_specs=tuple(vmem_specs(2)),
        scratch_shapes=[
            pltpu.VMEM(values.shape, bf16),
            pltpu.VMEM((page_tok, groups * 8, slots), f32),
            pltpu.VMEM((page_tok, groups * 8, slots), f32),
            pltpu.SemaphoreType.DMA,
        ],
        compiler_params=pltpu.CompilerParams(vmem_limit_bytes=51 * 2**20),
        name="attend",
    )(received, keys, queries, fresh_key_value, values)
    parts = lax.all_to_all(partial, "inst", 0, 0)

    combined = pl.pallas_call(
        functools.partial(combine_kernel, groups),
        out_shape=jax.ShapeDtypeStruct((pages, rows + 8, HEAD_SIZE), jnp.int16),
        in_specs=vmem_specs(1),
        out_specs=pl.BlockSpec(memory_space=VMEM),
        compiler_params=pltpu.CompilerParams(vmem_limit_bytes=16 * 2**20),
        name="combine",
    )(parts)
    page_parts = lax.all_to_all(combined, "page", 0, 0)

    return pl.pallas_call(
        functools.partial(finish_kernel, groups),
        out_shape=jax.ShapeDtypeStruct(queries.shape, bf16),
        in_specs=vmem_specs(2),
        out_specs=pl.BlockSpec(memory_space=VMEM),
        compiler_params=pltpu.CompilerParams(vmem_limit_bytes=16 * 2**20),
        name="finish",
    )(page_parts, token)


def solution(mesh):
    return jax.shard_map(
        shards,
        mesh=mesh,
        in_specs=(
            P("inst", "head"),
            P(None, "inst", "head"),
            P(None, ("inst", "page"), None, "head"),
            P("inst", None),
            P("inst"),
        ),
        out_specs=P("inst", "head"),
        check_vma=False,
    )
```

```python
import functools
import math

import jax
import jax.numpy as jnp
from jax import lax
from jax.experimental import pallas as pl
from jax.experimental.pallas import tpu as pltpu
from jax.sharding import PartitionSpec as P

HEAD_SIZE = 128
LOWEST_SCORE = -1e30
SCALE = 1.0 / math.sqrt(HEAD_SIZE)
VMEM = pltpu.MemorySpace.VMEM
SMEM = pltpu.MemorySpace.SMEM
f32 = jnp.float32
bf16 = jnp.bfloat16


def nt_dot(a, b):
    return lax.dot_general(a, b, (((1,), (1,)), ((), ())), preferred_element_type=f32)


STEPS = 16.0
FULL = 32700.0
LOWEST_TOP = -32000.0
PART = 32767.0


def encode_rows(x):
    top = jnp.max(jnp.abs(x), axis=1, keepdims=True)
    k = jnp.ceil(jnp.log2(jnp.maximum(top, 2.0**-120)) * STEPS)
    code = jnp.round((x * jnp.exp2(k * (-1.0 / STEPS))) * FULL)
    return k, code.astype(jnp.int32).astype(jnp.int16)


def vmem_specs(n):
    return [pl.BlockSpec(memory_space=VMEM)] * n


def send_kernel(slots, pages, page_ref, lengths_ref, queries_ref, table_ref, out_ref):
    peers = out_ref.shape[0]
    own_rows, most_pages = table_ref.shape
    heads = queries_ref.shape[1] // HEAD_SIZE
    page_tok = 16
    slot_bits = slots.bit_length() - 1
    page_bits = pages.bit_length() - 1
    column = lax.broadcasted_iota(jnp.int32, (1, most_pages), 1)
    lender_rows = lax.broadcasted_iota(jnp.int32, (peers, most_pages), 0)
    slot_rows = lax.broadcasted_iota(jnp.int32, (slots, most_pages), 0)
    fills = []
    for row in range(own_rows):
        entry = table_ref[row : row + 1, :]
        fill = jnp.clip(lengths_ref[row] - column * page_tok, 0, page_tok)
        here = ((entry >> slot_bits) & (pages - 1)) == page_ref[0]
        lender = jnp.where(here & (entry >= 0), entry >> (slot_bits + page_bits), -1)
        slot = entry & (slots - 1)
        a = jnp.where(lender_rows == lender, fill.astype(f32), 0.0).astype(bf16)
        b = jnp.where(slot_rows == slot, 1.0, 0.0).astype(bf16)
        fills.append(nt_dot(a, b))
    sub = lax.broadcasted_iota(jnp.int32, (8, HEAD_SIZE), 0)
    pieces = []
    for g in range(heads // 8):
        pair = [jnp.zeros((8, HEAD_SIZE), f32)] * own_rows
        for head in range(8):
            at = (g * 8 + head) * HEAD_SIZE
            both = queries_ref[:, at : at + HEAD_SIZE].astype(f32)
            pair = [
                jnp.where(sub == head, both[row : row + 1, :], pair[row]) for row in range(own_rows)
            ]
        pieces += pair
    queries = jnp.concatenate(pieces, axis=0).astype(bf16)
    rows = own_rows * heads
    sub = lax.broadcasted_iota(jnp.int32, (8, slots), 0)
    for peer in range(peers):
        out_ref[peer, 0:rows, :] = queries
        tile = jnp.zeros((8, slots), f32)
        for row in range(own_rows):
            tile = jnp.where(sub == row, fills[row][peer : peer + 1, :], tile)
        out_ref[peer, rows : rows + 8, :] = tile.astype(bf16)


def new_token(queries_ref, fresh_ref, token_ref):
    groups = fresh_ref.shape[2] // HEAD_SIZE
    sub = lax.broadcasted_iota(jnp.int32, (8, HEAD_SIZE), 0)
    lane = lax.broadcasted_iota(jnp.int32, (8, HEAD_SIZE), 1)
    fresh_k = fresh_ref[0].astype(f32)
    fresh_v = fresh_ref[1].astype(f32)
    scores = jnp.zeros((8, HEAD_SIZE), f32)
    values = jnp.zeros((8, HEAD_SIZE), f32)
    for g in range(groups):
        both = [
            queries_ref[:, (g * 8 + h) * HEAD_SIZE : (g * 8 + h + 1) * HEAD_SIZE].astype(f32)
            for h in range(8)
        ]
        for row in range(2):
            q = jnp.zeros((8, HEAD_SIZE), f32)
            for h in range(8):
                q = jnp.where(sub == h, both[h][row : row + 1, :], q)
            k = fresh_k[row : row + 1, g * HEAD_SIZE : (g + 1) * HEAD_SIZE]
            new = jnp.sum(q * k, axis=1, keepdims=True) * SCALE
            scores = jnp.where(lane == g * 2 + row, new, scores)
            v = fresh_v[row : row + 1, g * HEAD_SIZE : (g + 1) * HEAD_SIZE]
            values = jnp.where(sub == g * 2 + row, v, values)
    token_ref[0:8, :] = scores
    token_ref[8:16, :] = values


PARTS = 2


def token_major_kernel(
    pool_hbm, keys_ref, values_hbm, pool_ref, values_ref, load_sems, store_sems
):
    pages, page_tok, width = pool_hbm.shape[1:]
    chunk = pages // PARTS
    block = page_tok * 16
    loads = []
    stores = []
    for kind in (1, 0):
        for c in range(PARTS):
            at = pl.ds(c * chunk, chunk)
            loads.append(
                pltpu.make_async_copy(
                    pool_hbm.at[kind, at], pool_ref.at[kind, at], load_sems.at[kind, c]
                )
            )
            if kind == 1:
                stores.append(
                    pltpu.make_async_copy(
                        values_ref.at[:, at], values_hbm.at[:, at], store_sems.at[c]
                    )
                )
    for load in loads:
        load.start()
    i = lax.broadcasted_iota(jnp.int32, (block, block), 0)
    j = lax.broadcasted_iota(jnp.int32, (block, block), 1)
    perm = jnp.where((i % 16) * page_tok + i // 16 == j, 1.0, 0.0).astype(bf16)
    for kind in (1, 0):
        out_ref = values_ref if kind == 1 else keys_ref
        for c in range(PARTS):
            loads[(1 - kind) * PARTS + c].wait()
            for b in range(chunk // 16):
                first = c * chunk + b * 16
                rows = pool_ref[kind, first : first + 16].reshape(block, width)
                moved = jnp.dot(perm, rows, preferred_element_type=f32).astype(bf16)
                out_ref[:, first : first + 16, :] = moved.reshape(page_tok, 16, width)
            if kind == 1:
                stores[c].start()
    for store in stores:
        store.wait()


def attend_kernel(
    recv_ref,
    keys_ref,
    queries_ref,
    fresh_ref,
    values_hbm,
    out_ref,
    token_ref,
    values_ref,
    score_ref,
    weight_ref,
    sem,
):
    peers = recv_ref.shape[0]
    page_tok, slots, width = keys_ref.shape
    load = pltpu.make_async_copy(values_hbm, values_ref, sem)
    load.start()
    groups = width // HEAD_SIZE
    requests = 2 * peers
    heads = groups * 8
    rows = groups * 16
    sub8 = lax.broadcasted_iota(jnp.int32, (8, slots), 0)
    fill = jnp.zeros((8, slots), f32)
    code = jnp.zeros((8, slots), f32)
    for peer in range(peers):
        tile = recv_ref[peer, rows : rows + 8, :].astype(f32)
        fill = fill + tile
        code = code + jnp.where(tile > 0.0, (sub8 + (2 * peer + 1)).astype(f32), 0.0)
    fill = jnp.broadcast_to(jnp.sum(fill, axis=0, keepdims=True), (8, slots))
    owner = jnp.broadcast_to(jnp.sum(code, axis=0, keepdims=True), (8, slots))

    def score_step(t, carry):
        live = fill > jnp.asarray(t, f32)
        for g in range(groups):
            q = recv_ref[:, g * 16 : (g + 1) * 16, :].reshape(requests * 8, HEAD_SIZE)
            k = keys_ref[t, :, g * HEAD_SIZE : (g + 1) * HEAD_SIZE]
            s = nt_dot(q, k)
            picked = jnp.zeros((8, slots), f32)
            for r in range(requests):
                picked = jnp.where(owner == float(r + 1), s[r * 8 : (r + 1) * 8], picked)
            score_ref[t, g * 8 : (g + 1) * 8, :] = jnp.where(live, picked * SCALE, LOWEST_SCORE)
        return carry

    lax.fori_loop(0, page_tok, score_step, 0, unroll=8)

    load.wait()
    new_token(queries_ref, fresh_ref, token_ref)
    owner_h = jnp.broadcast_to(owner[0:1], (heads, slots))
    fill_h = jnp.broadcast_to(fill[0:1], (heads, slots))
    page_max = score_ref[0]
    for t in range(1, page_tok):
        page_max = jnp.maximum(page_max, score_ref[t])
    maxima = []
    owner_max = jnp.zeros((heads, slots), f32)
    for r in range(requests):
        mine = owner_h == float(r + 1)
        top = jnp.max(jnp.where(mine, page_max, LOWEST_TOP), axis=1, keepdims=True)
        top = jnp.round(jnp.maximum(top, LOWEST_TOP))
        maxima.append(top)
        owner_max = jnp.where(mine, top, owner_max)
    factor = jnp.exp(page_max - owner_max)
    page_sum = jnp.zeros((heads, slots), f32)
    sub16 = lax.broadcasted_iota(jnp.int32, (16, slots), 0)
    owner_16 = jnp.broadcast_to(owner[0:1], (16, slots))
    for t in range(page_tok):
        w = jnp.where(fill_h > float(t), jnp.exp(score_ref[t] - page_max), 0.0)
        page_sum = page_sum + w
        scaled = w.astype(bf16).astype(f32) * factor
        high = scaled.astype(bf16).astype(f32)
        score_ref[t] = high
        weight_ref[t] = scaled - high
    page_sum = page_sum * factor
    masks = [
        jnp.where(owner_16 == (2 * k + 1 + sub16 // 8).astype(f32), 1.0, 0.0).astype(bf16)
        for k in range(peers)
    ]
    totals = [
        jnp.sum(jnp.where(owner_h == float(r + 1), page_sum, 0.0), axis=1, keepdims=True)
        for r in range(requests)
    ]
    scales = []
    for g in range(groups):
        acc = jnp.zeros((requests * 8, HEAD_SIZE), f32)
        for t0 in range(0, page_tok, 2):
            v = values_ref[t0 : t0 + 2, :, g * HEAD_SIZE : (g + 1) * HEAD_SIZE].reshape(
                2 * slots, HEAD_SIZE
            )
            for ref in (score_ref, weight_ref):
                cols = []
                for t in (t0, t0 + 1):
                    w8 = ref[t, g * 8 : (g + 1) * 8, :]
                    w16 = jnp.concatenate([w8, w8], axis=0).astype(bf16)
                    cols.append(jnp.concatenate([w16 * m for m in masks], axis=0))
                acc = acc + jnp.dot(
                    jnp.concatenate(cols, axis=1), v, preferred_element_type=f32
                )
        k, code = encode_rows(acc)
        scales.append(k)
        out_ref[:, g * 16 : (g + 1) * 16, :] = code.reshape(peers, 16, HEAD_SIZE)
    for peer in range(peers):
        columns = []
        for g in range(groups):
            for row in range(2):
                r = 2 * peer + row
                at = slice(g * 8, (g + 1) * 8)
                columns.append((maxima[r][at], totals[r][at], scales[g][r * 8 : (r + 1) * 8]))
        out_ref[peer, rows : rows + 8, :] = stat_tile(columns, LENDER_UNIT)


LENDER_UNIT = 8.0
OWNER_UNIT = 1.0


def stat_tile(columns, unit):
    tiles = len(columns)
    lane = lax.broadcasted_iota(jnp.int32, (8, HEAD_SIZE), 1)
    top = jnp.zeros((8, HEAD_SIZE), f32)
    total = top
    scale = top
    for c, (m, l, k) in enumerate(columns):
        top = jnp.where(lane == c, m, top)
        total = jnp.where((lane == tiles + c) | (lane == 2 * tiles + c), l, total)
        scale = jnp.where(lane == 3 * tiles + c, k, scale)
    total = total * unit
    whole = jnp.floor(total)
    part = jnp.round((total - whole) * PART)
    tile = jnp.where(lane < tiles, top, jnp.where(lane < 2 * tiles, whole, part))
    tile = jnp.where(lane < 3 * tiles, tile, scale)
    return tile.astype(jnp.int32).astype(jnp.int16)


def merge(parts_ref, groups, unit):
    tiles = 2 * groups
    count = parts_ref.shape[0]
    stats = [
        parts_ref[i, tiles * 8 : tiles * 8 + 8, :].astype(jnp.int32).astype(f32)
        for i in range(count)
    ]
    top = stats[0]
    for s in stats[1:]:
        top = jnp.maximum(top, s)
    total = jnp.zeros_like(top)
    scales = []
    for s in stats:
        shifted = [pltpu.roll(s, HEAD_SIZE - n * tiles, axis=1) for n in (1, 2, 3)]
        e = jnp.exp(s - top)
        total = total + (shifted[0] + shifted[1] * (1.0 / PART)) * e
        scales.append(e * (jnp.exp2(shifted[2] * (1.0 / STEPS)) * (1.0 / FULL)))
    sums = []
    for g in range(groups):
        pair = [jnp.zeros((8, HEAD_SIZE), f32)] * 2
        for i in range(count):
            both = parts_ref[i, g * 16 : (g + 1) * 16, :].astype(jnp.int32).astype(f32)
            pair = [
                pair[n] + both[n * 8 : (n + 1) * 8] * scales[i][:, g * 2 + n : g * 2 + n + 1]
                for n in range(2)
            ]
        sums += pair
    return top, total * (1.0 / unit), sums


def combine_kernel(groups, parts_ref, out_ref):
    tiles = 2 * groups
    top, total, sums = merge(parts_ref, groups, LENDER_UNIT)
    coded = [encode_rows(jnp.concatenate(sums[2 * g : 2 * g + 2], axis=0)) for g in range(groups)]
    columns = [
        (top[:, c : c + 1], total[:, c : c + 1], coded[c // 2][0][c % 2 * 8 : c % 2 * 8 + 8])
        for c in range(tiles)
    ]
    stat = stat_tile(columns, OWNER_UNIT)
    for i in range(out_ref.shape[0]):
        for g in range(groups):
            out_ref[i, g * 16 : (g + 1) * 16, :] = coded[g][1]
        out_ref[i, tiles * 8 : tiles * 8 + 8, :] = stat


def finish_kernel(groups, parts_ref, token_ref, out_ref):
    top, total, sums = merge(parts_ref, groups, OWNER_UNIT)
    new = token_ref[0:8, :]
    best = jnp.maximum(top, new)
    carried = jnp.exp(top - best)
    own = jnp.exp(new - best)
    denominator = own + total * carried
    for g in range(groups):
        outs = []
        for row in range(2):
            c = g * 2 + row
            at = slice(c, c + 1)
            outs.append(
                (own[:, at] * token_ref[8 + c : 9 + c, :] + sums[c] * carried[:, at])
                / denominator[:, at]
            )
        for h in range(8):
            at = (g * 8 + h) * HEAD_SIZE
            out_ref[:, at : at + HEAD_SIZE] = jnp.concatenate(
                [outs[0][h : h + 1], outs[1][h : h + 1]], axis=0
            ).astype(bf16)


def shards(queries, fresh_key_value, key_value_pool, block_table, lengths):
    lenders = lax.axis_size("inst")
    pages = lax.axis_size("page")
    own_rows = queries.shape[0]
    slots, page_tok, width = key_value_pool.shape[1:]
    groups = width // HEAD_SIZE
    rows = groups * 16
    page_index = lax.axis_index("page").reshape(1).astype(jnp.int32)

    to_send = pl.pallas_call(
        functools.partial(send_kernel, slots, pages),
        out_shape=jax.ShapeDtypeStruct((lenders, rows + 8, HEAD_SIZE), bf16),
        in_specs=[pl.BlockSpec(memory_space=SMEM)] * 2 + vmem_specs(2),
        out_specs=pl.BlockSpec(memory_space=VMEM),
        name="send",
    )(page_index, lengths, queries, block_table)
    received = lax.all_to_all(to_send, "inst", 0, 0)

    keys, values = pl.pallas_call(
        token_major_kernel,
        out_shape=(
            jax.ShapeDtypeStruct((page_tok, slots, width), bf16),
            jax.ShapeDtypeStruct((page_tok, slots, width), bf16),
        ),
        in_specs=[pl.BlockSpec(memory_space=pl.ANY)],
        out_specs=(pl.BlockSpec(memory_space=VMEM), pl.BlockSpec(memory_space=pl.ANY)),
        scratch_shapes=[
            pltpu.VMEM(key_value_pool.shape, bf16),
            pltpu.VMEM((page_tok, slots, width), bf16),
            pltpu.SemaphoreType.DMA((2, PARTS)),
            pltpu.SemaphoreType.DMA((PARTS,)),
        ],
        cost_estimate=pl.CostEstimate(flops=10**9, bytes_accessed=2 * 4 * 2**20, transcendentals=0),
        compiler_params=pltpu.CompilerParams(vmem_limit_bytes=50 * 2**20),
        name="token_major",
    )(key_value_pool)

    partial, token = pl.pallas_call(
        attend_kernel,
        out_shape=(
            jax.ShapeDtypeStruct((lenders, rows + 8, HEAD_SIZE), jnp.int16),
            jax.ShapeDtypeStruct((16, HEAD_SIZE), f32),
        ),
        in_specs=vmem_specs(4) + [pl.BlockSpec(memory_space=pl.ANY)],
        out_specs=tuple(vmem_specs(2)),
        scratch_shapes=[
            pltpu.VMEM(values.shape, bf16),
            pltpu.VMEM((page_tok, groups * 8, slots), f32),
            pltpu.VMEM((page_tok, groups * 8, slots), f32),
            pltpu.SemaphoreType.DMA,
        ],
        compiler_params=pltpu.CompilerParams(vmem_limit_bytes=51 * 2**20),
        name="attend",
    )(received, keys, queries, fresh_key_value, values)
    parts = lax.all_to_all(partial, "inst", 0, 0)

    combined = pl.pallas_call(
        functools.partial(combine_kernel, groups),
        out_shape=jax.ShapeDtypeStruct((pages, rows + 8, HEAD_SIZE), jnp.int16),
        in_specs=vmem_specs(1),
        out_specs=pl.BlockSpec(memory_space=VMEM),
        compiler_params=pltpu.CompilerParams(vmem_limit_bytes=16 * 2**20),
        name="combine",
    )(parts)
    page_parts = lax.all_to_all(combined, "page", 0, 0)

    return pl.pallas_call(
        functools.partial(finish_kernel, groups),
        out_shape=jax.ShapeDtypeStruct(queries.shape, bf16),
        in_specs=vmem_specs(2),
        out_specs=pl.BlockSpec(memory_space=VMEM),
        compiler_params=pltpu.CompilerParams(vmem_limit_bytes=16 * 2**20),
        name="finish",
    )(page_parts, token)


def solution(mesh):
    return jax.shard_map(
        shards,
        mesh=mesh,
        in_specs=(
            P("inst", "head"),
            P(None, "inst", "head"),
            P(None, ("inst", "page"), None, "head"),
            P("inst", None),
            P("inst"),
        ),
        out_specs=P("inst", "head"),
        check_vma=False,
    )
```

```python
import functools
import math

import jax
import jax.numpy as jnp
from jax import lax
from jax.experimental import pallas as pl
from jax.experimental.pallas import tpu as pltpu
from jax.sharding import PartitionSpec as P

HEAD_SIZE = 128
LOWEST_SCORE = -1e30
SCALE = 1.0 / math.sqrt(HEAD_SIZE)
VMEM = pltpu.MemorySpace.VMEM
SMEM = pltpu.MemorySpace.SMEM
f32 = jnp.float32
bf16 = jnp.bfloat16


def nt_dot(a, b):
    return lax.dot_general(a, b, (((1,), (1,)), ((), ())), preferred_element_type=f32)


STEPS = 16.0
FULL = 32700.0
LOWEST_TOP = -32000.0
PART = 32767.0


def encode_rows(x):
    top = jnp.max(jnp.abs(x), axis=1, keepdims=True)
    k = jnp.ceil(jnp.log2(jnp.maximum(top, 2.0**-120)) * STEPS)
    code = jnp.round((x * jnp.exp2(k * (-1.0 / STEPS))) * FULL)
    return k, code.astype(jnp.int32).astype(jnp.int16)


def vmem_specs(n):
    return [pl.BlockSpec(memory_space=VMEM)] * n


def send_kernel(
    slots, pages, page_ref, lengths_ref, queries_ref, table_ref, out_hbm, out_ref, sems
):
    peers = out_hbm.shape[0]
    own_rows, most_pages = table_ref.shape
    heads = queries_ref.shape[1] // HEAD_SIZE
    page_tok = 16
    slot_bits = slots.bit_length() - 1
    page_bits = pages.bit_length() - 1
    sub = lax.broadcasted_iota(jnp.int32, (8, HEAD_SIZE), 0)
    pieces = []
    for g in range(heads // 8):
        pair = [jnp.zeros((8, HEAD_SIZE), f32)] * own_rows
        for head in range(8):
            at = (g * 8 + head) * HEAD_SIZE
            both = queries_ref[:, at : at + HEAD_SIZE].astype(f32)
            pair = [
                jnp.where(sub == head, both[row : row + 1, :], pair[row]) for row in range(own_rows)
            ]
        pieces += pair
    queries = jnp.concatenate(pieces, axis=0).astype(bf16)
    rows = own_rows * heads
    for peer in range(peers):
        out_ref[peer, 0:rows, :] = queries
    stores = [
        pltpu.make_async_copy(out_ref.at[:, at], out_hbm.at[:, at], sems.at[n])
        for n, at in enumerate((pl.ds(0, rows), pl.ds(rows, 8)))
    ]
    stores[0].start()
    column = lax.broadcasted_iota(jnp.int32, (1, most_pages), 1)
    lender_rows = lax.broadcasted_iota(jnp.int32, (peers, most_pages), 0)
    slot_rows = lax.broadcasted_iota(jnp.int32, (slots, most_pages), 0)
    fills = []
    for row in range(own_rows):
        entry = table_ref[row : row + 1, :]
        fill = jnp.clip(lengths_ref[row] - column * page_tok, 0, page_tok)
        here = ((entry >> slot_bits) & (pages - 1)) == page_ref[0]
        lender = jnp.where(here & (entry >= 0), entry >> (slot_bits + page_bits), -1)
        slot = entry & (slots - 1)
        a = jnp.where(lender_rows == lender, fill.astype(f32), 0.0).astype(bf16)
        b = jnp.where(slot_rows == slot, 1.0, 0.0).astype(bf16)
        fills.append(nt_dot(a, b))
    sub = lax.broadcasted_iota(jnp.int32, (8, slots), 0)
    for peer in range(peers):
        tile = jnp.zeros((8, slots), f32)
        for row in range(own_rows):
            tile = jnp.where(sub == row, fills[row][peer : peer + 1, :], tile)
        out_ref[peer, rows : rows + 8, :] = tile.astype(bf16)
    stores[1].start()
    for store in stores:
        store.wait()


def new_token(queries_ref, fresh_ref, token_ref):
    groups = fresh_ref.shape[2] // HEAD_SIZE
    sub = lax.broadcasted_iota(jnp.int32, (8, HEAD_SIZE), 0)
    lane = lax.broadcasted_iota(jnp.int32, (8, HEAD_SIZE), 1)
    fresh_k = fresh_ref[0].astype(f32)
    fresh_v = fresh_ref[1].astype(f32)
    scores = jnp.zeros((8, HEAD_SIZE), f32)
    values = jnp.zeros((8, HEAD_SIZE), f32)
    for g in range(groups):
        both = [
            queries_ref[:, (g * 8 + h) * HEAD_SIZE : (g * 8 + h + 1) * HEAD_SIZE].astype(f32)
            for h in range(8)
        ]
        for row in range(2):
            q = jnp.zeros((8, HEAD_SIZE), f32)
            for h in range(8):
                q = jnp.where(sub == h, both[h][row : row + 1, :], q)
            k = fresh_k[row : row + 1, g * HEAD_SIZE : (g + 1) * HEAD_SIZE]
            new = jnp.sum(q * k, axis=1, keepdims=True) * SCALE
            scores = jnp.where(lane == g * 2 + row, new, scores)
            v = fresh_v[row : row + 1, g * HEAD_SIZE : (g + 1) * HEAD_SIZE]
            values = jnp.where(sub == g * 2 + row, v, values)
    token_ref[0:8, :] = scores
    token_ref[8:16, :] = values


PARTS = 2


def token_major_kernel(
    pool_hbm, keys_ref, values_hbm, pool_ref, values_ref, load_sems, store_sems
):
    pages, page_tok, width = pool_hbm.shape[1:]
    chunk = pages // PARTS
    block = page_tok * 16
    loads = []
    stores = []
    for kind in (1, 0):
        for c in range(PARTS):
            at = pl.ds(c * chunk, chunk)
            loads.append(
                pltpu.make_async_copy(
                    pool_hbm.at[kind, at], pool_ref.at[kind, at], load_sems.at[kind, c]
                )
            )
            if kind == 1:
                stores.append(
                    pltpu.make_async_copy(
                        values_ref.at[:, at], values_hbm.at[:, at], store_sems.at[c]
                    )
                )
    for load in loads:
        load.start()
    i = lax.broadcasted_iota(jnp.int32, (block, block), 0)
    j = lax.broadcasted_iota(jnp.int32, (block, block), 1)
    perm = jnp.where((i % 16) * page_tok + i // 16 == j, 1.0, 0.0).astype(bf16)
    for kind in (1, 0):
        out_ref = values_ref if kind == 1 else keys_ref
        for c in range(PARTS):
            loads[(1 - kind) * PARTS + c].wait()
            for b in range(chunk // 16):
                first = c * chunk + b * 16
                rows = pool_ref[kind, first : first + 16].reshape(block, width)
                moved = jnp.dot(perm, rows, preferred_element_type=f32).astype(bf16)
                out_ref[:, first : first + 16, :] = moved.reshape(page_tok, 16, width)
            if kind == 1:
                stores[c].start()
    for store in stores:
        store.wait()


def attend_kernel(
    recv_ref,
    keys_ref,
    queries_ref,
    fresh_ref,
    values_hbm,
    out_ref,
    token_ref,
    values_ref,
    score_ref,
    weight_ref,
    sem,
):
    peers = recv_ref.shape[0]
    page_tok, slots, width = keys_ref.shape
    load = pltpu.make_async_copy(values_hbm, values_ref, sem)
    load.start()
    groups = width // HEAD_SIZE
    requests = 2 * peers
    heads = groups * 8
    rows = groups * 16
    sub8 = lax.broadcasted_iota(jnp.int32, (8, slots), 0)
    fill = jnp.zeros((8, slots), f32)
    code = jnp.zeros((8, slots), f32)
    for peer in range(peers):
        tile = recv_ref[peer, rows : rows + 8, :].astype(f32)
        fill = fill + tile
        code = code + jnp.where(tile > 0.0, (sub8 + (2 * peer + 1)).astype(f32), 0.0)
    fill = jnp.broadcast_to(jnp.sum(fill, axis=0, keepdims=True), (8, slots))
    owner = jnp.broadcast_to(jnp.sum(code, axis=0, keepdims=True), (8, slots))

    def score_step(t, carry):
        live = fill > jnp.asarray(t, f32)
        for g in range(groups):
            q = recv_ref[:, g * 16 : (g + 1) * 16, :].reshape(requests * 8, HEAD_SIZE)
            k = keys_ref[t, :, g * HEAD_SIZE : (g + 1) * HEAD_SIZE]
            s = nt_dot(q, k)
            picked = jnp.zeros((8, slots), f32)
            for r in range(requests):
                picked = jnp.where(owner == float(r + 1), s[r * 8 : (r + 1) * 8], picked)
            score_ref[t, g * 8 : (g + 1) * 8, :] = jnp.where(live, picked * SCALE, LOWEST_SCORE)
        return carry

    lax.fori_loop(0, page_tok, score_step, 0, unroll=8)

    new_token(queries_ref, fresh_ref, token_ref)
    owner_h = jnp.broadcast_to(owner[0:1], (heads, slots))
    fill_h = jnp.broadcast_to(fill[0:1], (heads, slots))
    page_max = score_ref[0]
    for t in range(1, page_tok):
        page_max = jnp.maximum(page_max, score_ref[t])
    maxima = []
    owner_max = jnp.zeros((heads, slots), f32)
    for r in range(requests):
        mine = owner_h == float(r + 1)
        top = jnp.max(jnp.where(mine, page_max, LOWEST_TOP), axis=1, keepdims=True)
        top = jnp.round(jnp.maximum(top, LOWEST_TOP))
        maxima.append(top)
        owner_max = jnp.where(mine, top, owner_max)
    factor = jnp.exp(page_max - owner_max)
    page_sum = jnp.zeros((heads, slots), f32)
    sub16 = lax.broadcasted_iota(jnp.int32, (16, slots), 0)
    owner_16 = jnp.broadcast_to(owner[0:1], (16, slots))
    for t in range(page_tok):
        w = jnp.where(fill_h > float(t), jnp.exp(score_ref[t] - page_max), 0.0)
        page_sum = page_sum + w
        scaled = w.astype(bf16).astype(f32) * factor
        high = scaled.astype(bf16).astype(f32)
        score_ref[t] = high
        weight_ref[t] = scaled - high
    load.wait()
    page_sum = page_sum * factor
    masks = [
        jnp.where(owner_16 == (2 * k + 1 + sub16 // 8).astype(f32), 1.0, 0.0).astype(bf16)
        for k in range(peers)
    ]
    totals = [
        jnp.sum(jnp.where(owner_h == float(r + 1), page_sum, 0.0), axis=1, keepdims=True)
        for r in range(requests)
    ]
    scales = []
    for g in range(groups):
        acc = jnp.zeros((requests * 8, HEAD_SIZE), f32)
        for t0 in range(0, page_tok, 2):
            v = values_ref[t0 : t0 + 2, :, g * HEAD_SIZE : (g + 1) * HEAD_SIZE].reshape(
                2 * slots, HEAD_SIZE
            )
            for ref in (score_ref, weight_ref):
                cols = []
                for t in (t0, t0 + 1):
                    w8 = ref[t, g * 8 : (g + 1) * 8, :]
                    w16 = jnp.concatenate([w8, w8], axis=0).astype(bf16)
                    cols.append(jnp.concatenate([w16 * m for m in masks], axis=0))
                acc = acc + jnp.dot(
                    jnp.concatenate(cols, axis=1), v, preferred_element_type=f32
                )
        k, code = encode_rows(acc)
        scales.append(k)
        out_ref[:, g * 16 : (g + 1) * 16, :] = code.reshape(peers, 16, HEAD_SIZE)
    for peer in range(peers):
        columns = []
        for g in range(groups):
            for row in range(2):
                r = 2 * peer + row
                at = slice(g * 8, (g + 1) * 8)
                columns.append((maxima[r][at], totals[r][at], scales[g][r * 8 : (r + 1) * 8]))
        out_ref[peer, rows : rows + 8, :] = stat_tile(columns, LENDER_UNIT)


LENDER_UNIT = 8.0
OWNER_UNIT = 1.0


def stat_tile(columns, unit):
    tiles = len(columns)
    lane = lax.broadcasted_iota(jnp.int32, (8, HEAD_SIZE), 1)
    top = jnp.zeros((8, HEAD_SIZE), f32)
    total = top
    scale = top
    for c, (m, l, k) in enumerate(columns):
        top = jnp.where(lane == c, m, top)
        total = jnp.where((lane == tiles + c) | (lane == 2 * tiles + c), l, total)
        scale = jnp.where(lane == 3 * tiles + c, k, scale)
    total = total * unit
    whole = jnp.floor(total)
    part = jnp.round((total - whole) * PART)
    tile = jnp.where(lane < tiles, top, jnp.where(lane < 2 * tiles, whole, part))
    tile = jnp.where(lane < 3 * tiles, tile, scale)
    return tile.astype(jnp.int32).astype(jnp.int16)


def merge(parts_ref, groups, unit):
    tiles = 2 * groups
    count = parts_ref.shape[0]
    stats = [
        parts_ref[i, tiles * 8 : tiles * 8 + 8, :].astype(jnp.int32).astype(f32)
        for i in range(count)
    ]
    top = stats[0]
    for s in stats[1:]:
        top = jnp.maximum(top, s)
    total = jnp.zeros_like(top)
    scales = []
    for s in stats:
        shifted = [pltpu.roll(s, HEAD_SIZE - n * tiles, axis=1) for n in (1, 2, 3)]
        e = jnp.exp(s - top)
        total = total + (shifted[0] + shifted[1] * (1.0 / PART)) * e
        scales.append(e * (jnp.exp2(shifted[2] * (1.0 / STEPS)) * (1.0 / FULL)))
    sums = []
    for g in range(groups):
        pair = [jnp.zeros((8, HEAD_SIZE), f32)] * 2
        for i in range(count):
            both = parts_ref[i, g * 16 : (g + 1) * 16, :].astype(jnp.int32).astype(f32)
            pair = [
                pair[n] + both[n * 8 : (n + 1) * 8] * scales[i][:, g * 2 + n : g * 2 + n + 1]
                for n in range(2)
            ]
        sums += pair
    return top, total * (1.0 / unit), sums


def combine_kernel(groups, parts_ref, out_ref):
    tiles = 2 * groups
    top, total, sums = merge(parts_ref, groups, LENDER_UNIT)
    coded = [encode_rows(jnp.concatenate(sums[2 * g : 2 * g + 2], axis=0)) for g in range(groups)]
    columns = [
        (top[:, c : c + 1], total[:, c : c + 1], coded[c // 2][0][c % 2 * 8 : c % 2 * 8 + 8])
        for c in range(tiles)
    ]
    stat = stat_tile(columns, OWNER_UNIT)
    for i in range(out_ref.shape[0]):
        for g in range(groups):
            out_ref[i, g * 16 : (g + 1) * 16, :] = coded[g][1]
        out_ref[i, tiles * 8 : tiles * 8 + 8, :] = stat


def finish_kernel(groups, parts_ref, token_ref, out_ref):
    top, total, sums = merge(parts_ref, groups, OWNER_UNIT)
    new = token_ref[0:8, :]
    best = jnp.maximum(top, new)
    carried = jnp.exp(top - best)
    own = jnp.exp(new - best)
    denominator = own + total * carried
    for g in range(groups):
        outs = []
        for row in range(2):
            c = g * 2 + row
            at = slice(c, c + 1)
            outs.append(
                (own[:, at] * token_ref[8 + c : 9 + c, :] + sums[c] * carried[:, at])
                / denominator[:, at]
            )
        for h in range(8):
            at = (g * 8 + h) * HEAD_SIZE
            out_ref[:, at : at + HEAD_SIZE] = jnp.concatenate(
                [outs[0][h : h + 1], outs[1][h : h + 1]], axis=0
            ).astype(bf16)


def shards(queries, fresh_key_value, key_value_pool, block_table, lengths):
    lenders = lax.axis_size("inst")
    pages = lax.axis_size("page")
    own_rows = queries.shape[0]
    slots, page_tok, width = key_value_pool.shape[1:]
    groups = width // HEAD_SIZE
    rows = groups * 16
    page_index = lax.axis_index("page").reshape(1).astype(jnp.int32)

    to_send = pl.pallas_call(
        functools.partial(send_kernel, slots, pages),
        out_shape=jax.ShapeDtypeStruct((lenders, rows + 8, HEAD_SIZE), bf16),
        in_specs=[pl.BlockSpec(memory_space=SMEM)] * 2 + vmem_specs(2),
        out_specs=pl.BlockSpec(memory_space=pl.ANY),
        scratch_shapes=[
            pltpu.VMEM((lenders, rows + 8, HEAD_SIZE), bf16),
            pltpu.SemaphoreType.DMA((2,)),
        ],
        name="send",
    )(page_index, lengths, queries, block_table)
    received = lax.all_to_all(to_send, "inst", 0, 0)

    keys, values = pl.pallas_call(
        token_major_kernel,
        out_shape=(
            jax.ShapeDtypeStruct((page_tok, slots, width), bf16),
            jax.ShapeDtypeStruct((page_tok, slots, width), bf16),
        ),
        in_specs=[pl.BlockSpec(memory_space=pl.ANY)],
        out_specs=(pl.BlockSpec(memory_space=VMEM), pl.BlockSpec(memory_space=pl.ANY)),
        scratch_shapes=[
            pltpu.VMEM(key_value_pool.shape, bf16),
            pltpu.VMEM((page_tok, slots, width), bf16),
            pltpu.SemaphoreType.DMA((2, PARTS)),
            pltpu.SemaphoreType.DMA((PARTS,)),
        ],
        cost_estimate=pl.CostEstimate(flops=10**9, bytes_accessed=2 * 4 * 2**20, transcendentals=0),
        compiler_params=pltpu.CompilerParams(vmem_limit_bytes=50 * 2**20),
        name="token_major",
    )(key_value_pool)

    partial, token = pl.pallas_call(
        attend_kernel,
        out_shape=(
            jax.ShapeDtypeStruct((lenders, rows + 8, HEAD_SIZE), jnp.int16),
            jax.ShapeDtypeStruct((16, HEAD_SIZE), f32),
        ),
        in_specs=vmem_specs(4) + [pl.BlockSpec(memory_space=pl.ANY)],
        out_specs=tuple(vmem_specs(2)),
        scratch_shapes=[
            pltpu.VMEM(values.shape, bf16),
            pltpu.VMEM((page_tok, groups * 8, slots), f32),
            pltpu.VMEM((page_tok, groups * 8, slots), f32),
            pltpu.SemaphoreType.DMA,
        ],
        compiler_params=pltpu.CompilerParams(vmem_limit_bytes=51 * 2**20),
        name="attend",
    )(received, keys, queries, fresh_key_value, values)
    parts = lax.all_to_all(partial, "inst", 0, 0)

    combined = pl.pallas_call(
        functools.partial(combine_kernel, groups),
        out_shape=jax.ShapeDtypeStruct((pages, rows + 8, HEAD_SIZE), jnp.int16),
        in_specs=vmem_specs(1),
        out_specs=pl.BlockSpec(memory_space=VMEM),
        compiler_params=pltpu.CompilerParams(vmem_limit_bytes=16 * 2**20),
        name="combine",
    )(parts)
    page_parts = lax.all_to_all(combined, "page", 0, 0)

    return pl.pallas_call(
        functools.partial(finish_kernel, groups),
        out_shape=jax.ShapeDtypeStruct(queries.shape, bf16),
        in_specs=vmem_specs(2),
        out_specs=pl.BlockSpec(memory_space=VMEM),
        compiler_params=pltpu.CompilerParams(vmem_limit_bytes=16 * 2**20),
        name="finish",
    )(page_parts, token)


def solution(mesh):
    return jax.shard_map(
        shards,
        mesh=mesh,
        in_specs=(
            P("inst", "head"),
            P(None, "inst", "head"),
            P(None, ("inst", "page"), None, "head"),
            P("inst", None),
            P("inst"),
        ),
        out_specs=P("inst", "head"),
        check_vma=False,
    )
```

```python
import functools
import math

import jax
import jax.numpy as jnp
from jax import lax
from jax.experimental import pallas as pl
from jax.experimental.pallas import tpu as pltpu
from jax.sharding import PartitionSpec as P

HEAD_SIZE = 128
LOWEST_SCORE = -1e30
SCALE = 1.0 / math.sqrt(HEAD_SIZE)
VMEM = pltpu.MemorySpace.VMEM
SMEM = pltpu.MemorySpace.SMEM
f32 = jnp.float32
bf16 = jnp.bfloat16


def nt_dot(a, b):
    return lax.dot_general(a, b, (((1,), (1,)), ((), ())), preferred_element_type=f32)


STEPS = 16.0
FULL = 32700.0
LOWEST_TOP = -32000.0
PART = 32767.0


def encode_rows(x):
    top = jnp.max(jnp.abs(x), axis=1, keepdims=True)
    k = jnp.ceil(jnp.log2(jnp.maximum(top, 2.0**-120)) * STEPS)
    code = jnp.round((x * jnp.exp2(k * (-1.0 / STEPS))) * FULL)
    return k, code.astype(jnp.int32).astype(jnp.int16)


def vmem_specs(n):
    return [pl.BlockSpec(memory_space=VMEM)] * n


def send_kernel(
    slots, pages, page_ref, lengths_ref, queries_ref, table_ref, out_hbm, out_ref, sems
):
    peers = out_hbm.shape[0]
    own_rows, most_pages = table_ref.shape
    heads = queries_ref.shape[1] // HEAD_SIZE
    page_tok = 16
    slot_bits = slots.bit_length() - 1
    page_bits = pages.bit_length() - 1
    sub = lax.broadcasted_iota(jnp.int32, (8, HEAD_SIZE), 0)
    pieces = []
    for g in range(heads // 8):
        pair = [jnp.zeros((8, HEAD_SIZE), f32)] * own_rows
        for head in range(8):
            at = (g * 8 + head) * HEAD_SIZE
            both = queries_ref[:, at : at + HEAD_SIZE].astype(f32)
            pair = [
                jnp.where(sub == head, both[row : row + 1, :], pair[row]) for row in range(own_rows)
            ]
        pieces += pair
    queries = jnp.concatenate(pieces, axis=0).astype(bf16)
    rows = own_rows * heads
    for peer in range(peers):
        out_ref[peer, 0:rows, :] = queries
    stores = [
        pltpu.make_async_copy(out_ref.at[:, at], out_hbm.at[:, at], sems.at[n])
        for n, at in enumerate((pl.ds(0, rows), pl.ds(rows, 8)))
    ]
    stores[0].start()
    column = lax.broadcasted_iota(jnp.int32, (1, most_pages), 1)
    lender_rows = lax.broadcasted_iota(jnp.int32, (peers, most_pages), 0)
    slot_rows = lax.broadcasted_iota(jnp.int32, (slots, most_pages), 0)
    fills = []
    for row in range(own_rows):
        entry = table_ref[row : row + 1, :]
        fill = jnp.clip(lengths_ref[row] - column * page_tok, 0, page_tok)
        here = ((entry >> slot_bits) & (pages - 1)) == page_ref[0]
        lender = jnp.where(here & (entry >= 0), entry >> (slot_bits + page_bits), -1)
        slot = entry & (slots - 1)
        a = jnp.where(lender_rows == lender, fill.astype(f32), 0.0).astype(bf16)
        b = jnp.where(slot_rows == slot, 1.0, 0.0).astype(bf16)
        fills.append(nt_dot(a, b))
    sub = lax.broadcasted_iota(jnp.int32, (8, slots), 0)
    for peer in range(peers):
        tile = jnp.zeros((8, slots), f32)
        for row in range(own_rows):
            tile = jnp.where(sub == row, fills[row][peer : peer + 1, :], tile)
        out_ref[peer, rows : rows + 8, :] = tile.astype(bf16)
    stores[1].start()
    for store in stores:
        store.wait()


def new_token(queries_ref, fresh_ref, token_ref):
    groups = fresh_ref.shape[2] // HEAD_SIZE
    sub = lax.broadcasted_iota(jnp.int32, (8, HEAD_SIZE), 0)
    lane = lax.broadcasted_iota(jnp.int32, (8, HEAD_SIZE), 1)
    fresh_k = fresh_ref[0].astype(f32)
    fresh_v = fresh_ref[1].astype(f32)
    scores = jnp.zeros((8, HEAD_SIZE), f32)
    values = jnp.zeros((8, HEAD_SIZE), f32)
    for g in range(groups):
        both = [
            queries_ref[:, (g * 8 + h) * HEAD_SIZE : (g * 8 + h + 1) * HEAD_SIZE].astype(f32)
            for h in range(8)
        ]
        for row in range(2):
            q = jnp.zeros((8, HEAD_SIZE), f32)
            for h in range(8):
                q = jnp.where(sub == h, both[h][row : row + 1, :], q)
            k = fresh_k[row : row + 1, g * HEAD_SIZE : (g + 1) * HEAD_SIZE]
            new = jnp.sum(q * k, axis=1, keepdims=True) * SCALE
            scores = jnp.where(lane == g * 2 + row, new, scores)
            v = fresh_v[row : row + 1, g * HEAD_SIZE : (g + 1) * HEAD_SIZE]
            values = jnp.where(sub == g * 2 + row, v, values)
    token_ref[0:8, :] = scores
    token_ref[8:16, :] = values


PARTS = 2


def token_major_kernel(
    pool_hbm, keys_ref, values_hbm, pool_ref, values_ref, load_sems, store_sems
):
    pages, page_tok, width = pool_hbm.shape[1:]
    chunk = pages // PARTS
    block = page_tok * 16
    loads = []
    stores = []
    for kind in (1, 0):
        for c in range(PARTS):
            at = pl.ds(c * chunk, chunk)
            loads.append(
                pltpu.make_async_copy(
                    pool_hbm.at[kind, at], pool_ref.at[kind, at], load_sems.at[kind, c]
                )
            )
            if kind == 1:
                stores.append(
                    pltpu.make_async_copy(
                        values_ref.at[:, at], values_hbm.at[:, at], store_sems.at[c]
                    )
                )
    for load in loads:
        load.start()
    i = lax.broadcasted_iota(jnp.int32, (block, block), 0)
    j = lax.broadcasted_iota(jnp.int32, (block, block), 1)
    perm = jnp.where((i % 16) * page_tok + i // 16 == j, 1.0, 0.0).astype(bf16)
    for kind in (1, 0):
        out_ref = values_ref if kind == 1 else keys_ref
        for c in range(PARTS):
            loads[(1 - kind) * PARTS + c].wait()
            for b in range(chunk // 16):
                first = c * chunk + b * 16
                rows = pool_ref[kind, first : first + 16].reshape(block, width)
                moved = jnp.dot(perm, rows, preferred_element_type=f32).astype(bf16)
                out_ref[:, first : first + 16, :] = moved.reshape(page_tok, 16, width)
            if kind == 1:
                stores[c].start()
    for store in stores:
        store.wait()


def attend_kernel(
    recv_ref,
    keys_ref,
    queries_ref,
    fresh_ref,
    values_hbm,
    out_ref,
    token_ref,
    values_ref,
    score_ref,
    weight_ref,
    sems,
):
    peers = recv_ref.shape[0]
    page_tok, slots, width = keys_ref.shape

    def load(i):
        at = pl.ds(i * (page_tok // 2), page_tok // 2)
        return pltpu.make_async_copy(values_hbm.at[at], values_ref.at[at], sems.at[i])

    def load_step(i, carry):
        load(i).start()
        return carry

    lax.fori_loop(0, 2, load_step, 0)
    groups = width // HEAD_SIZE
    requests = 2 * peers
    heads = groups * 8
    rows = groups * 16
    sub8 = lax.broadcasted_iota(jnp.int32, (8, slots), 0)
    fill = jnp.zeros((8, slots), f32)
    code = jnp.zeros((8, slots), f32)
    for peer in range(peers):
        tile = recv_ref[peer, rows : rows + 8, :].astype(f32)
        fill = fill + tile
        code = code + jnp.where(tile > 0.0, (sub8 + (2 * peer + 1)).astype(f32), 0.0)
    fill = jnp.broadcast_to(jnp.sum(fill, axis=0, keepdims=True), (8, slots))
    owner = jnp.broadcast_to(jnp.sum(code, axis=0, keepdims=True), (8, slots))

    def score_step(t, carry):
        live = fill > jnp.asarray(t, f32)
        for g in range(groups):
            q = recv_ref[:, g * 16 : (g + 1) * 16, :].reshape(requests * 8, HEAD_SIZE)
            k = keys_ref[t, :, g * HEAD_SIZE : (g + 1) * HEAD_SIZE]
            s = nt_dot(q, k)
            picked = jnp.zeros((8, slots), f32)
            for r in range(requests):
                picked = jnp.where(owner == float(r + 1), s[r * 8 : (r + 1) * 8], picked)
            score_ref[t, g * 8 : (g + 1) * 8, :] = jnp.where(live, picked * SCALE, LOWEST_SCORE)
        return carry

    lax.fori_loop(0, page_tok, score_step, 0, unroll=True)

    new_token(queries_ref, fresh_ref, token_ref)
    owner_h = jnp.broadcast_to(owner[0:1], (heads, slots))
    fill_h = jnp.broadcast_to(fill[0:1], (heads, slots))
    page_max = score_ref[0]
    for t in range(1, page_tok):
        page_max = jnp.maximum(page_max, score_ref[t])
    maxima = []
    owner_max = jnp.zeros((heads, slots), f32)
    for r in range(requests):
        mine = owner_h == float(r + 1)
        top = jnp.max(jnp.where(mine, page_max, LOWEST_TOP), axis=1, keepdims=True)
        top = jnp.round(jnp.maximum(top, LOWEST_TOP))
        maxima.append(top)
        owner_max = jnp.where(mine, top, owner_max)
    factor = jnp.exp(page_max - owner_max)
    page_sum = jnp.zeros((heads, slots), f32)
    sub16 = lax.broadcasted_iota(jnp.int32, (16, slots), 0)
    owner_16 = jnp.broadcast_to(owner[0:1], (16, slots))
    for t in range(page_tok):
        w = jnp.where(fill_h > float(t), jnp.exp(score_ref[t] - page_max), 0.0)
        page_sum = page_sum + w
        scaled = w.astype(bf16).astype(f32) * factor
        high = scaled.astype(bf16).astype(f32)
        score_ref[t] = high
        weight_ref[t] = scaled - high
    for i in range(2):
        load(i).wait()
    page_sum = page_sum * factor
    masks = [
        jnp.where(owner_16 == (2 * k + 1 + sub16 // 8).astype(f32), 1.0, 0.0).astype(bf16)
        for k in range(peers)
    ]
    totals = [
        jnp.sum(jnp.where(owner_h == float(r + 1), page_sum, 0.0), axis=1, keepdims=True)
        for r in range(requests)
    ]
    scales = []
    for g in range(groups):
        acc = jnp.zeros((requests * 8, HEAD_SIZE), f32)
        for t0 in range(0, page_tok, 2):
            v = values_ref[t0 : t0 + 2, :, g * HEAD_SIZE : (g + 1) * HEAD_SIZE].reshape(
                2 * slots, HEAD_SIZE
            )
            for ref in (score_ref, weight_ref):
                cols = []
                for t in (t0, t0 + 1):
                    w8 = ref[t, g * 8 : (g + 1) * 8, :]
                    w16 = jnp.concatenate([w8, w8], axis=0).astype(bf16)
                    cols.append(jnp.concatenate([w16 * m for m in masks], axis=0))
                acc = acc + jnp.dot(
                    jnp.concatenate(cols, axis=1), v, preferred_element_type=f32
                )
        k, code = encode_rows(acc)
        scales.append(k)
        out_ref[:, g * 16 : (g + 1) * 16, :] = code.reshape(peers, 16, HEAD_SIZE)
    for peer in range(peers):
        columns = []
        for g in range(groups):
            for row in range(2):
                r = 2 * peer + row
                at = slice(g * 8, (g + 1) * 8)
                columns.append((maxima[r][at], totals[r][at], scales[g][r * 8 : (r + 1) * 8]))
        out_ref[peer, rows : rows + 8, :] = stat_tile(columns, LENDER_UNIT)


LENDER_UNIT = 8.0
OWNER_UNIT = 1.0


def stat_tile(columns, unit):
    tiles = len(columns)
    lane = lax.broadcasted_iota(jnp.int32, (8, HEAD_SIZE), 1)
    top = jnp.zeros((8, HEAD_SIZE), f32)
    total = top
    scale = top
    for c, (m, l, k) in enumerate(columns):
        top = jnp.where(lane == c, m, top)
        total = jnp.where((lane == tiles + c) | (lane == 2 * tiles + c), l, total)
        scale = jnp.where(lane == 3 * tiles + c, k, scale)
    total = total * unit
    whole = jnp.floor(total)
    part = jnp.round((total - whole) * PART)
    tile = jnp.where(lane < tiles, top, jnp.where(lane < 2 * tiles, whole, part))
    tile = jnp.where(lane < 3 * tiles, tile, scale)
    return tile.astype(jnp.int32).astype(jnp.int16)


def merge(parts_ref, groups, unit):
    tiles = 2 * groups
    count = parts_ref.shape[0]
    stats = [
        parts_ref[i, tiles * 8 : tiles * 8 + 8, :].astype(jnp.int32).astype(f32)
        for i in range(count)
    ]
    top = stats[0]
    for s in stats[1:]:
        top = jnp.maximum(top, s)
    total = jnp.zeros_like(top)
    scales = []
    for s in stats:
        shifted = [pltpu.roll(s, HEAD_SIZE - n * tiles, axis=1) for n in (1, 2, 3)]
        e = jnp.exp(s - top)
        total = total + (shifted[0] + shifted[1] * (1.0 / PART)) * e
        scales.append(e * (jnp.exp2(shifted[2] * (1.0 / STEPS)) * (1.0 / FULL)))
    sums = []
    for g in range(groups):
        pair = [jnp.zeros((8, HEAD_SIZE), f32)] * 2
        for i in range(count):
            both = parts_ref[i, g * 16 : (g + 1) * 16, :].astype(jnp.int32).astype(f32)
            pair = [
                pair[n] + both[n * 8 : (n + 1) * 8] * scales[i][:, g * 2 + n : g * 2 + n + 1]
                for n in range(2)
            ]
        sums += pair
    return top, total * (1.0 / unit), sums


def combine_kernel(groups, parts_ref, out_ref):
    tiles = 2 * groups
    top, total, sums = merge(parts_ref, groups, LENDER_UNIT)
    coded = [encode_rows(jnp.concatenate(sums[2 * g : 2 * g + 2], axis=0)) for g in range(groups)]
    columns = [
        (top[:, c : c + 1], total[:, c : c + 1], coded[c // 2][0][c % 2 * 8 : c % 2 * 8 + 8])
        for c in range(tiles)
    ]
    stat = stat_tile(columns, OWNER_UNIT)
    for i in range(out_ref.shape[0]):
        for g in range(groups):
            out_ref[i, g * 16 : (g + 1) * 16, :] = coded[g][1]
        out_ref[i, tiles * 8 : tiles * 8 + 8, :] = stat


def finish_kernel(groups, parts_ref, token_ref, out_ref):
    top, total, sums = merge(parts_ref, groups, OWNER_UNIT)
    new = token_ref[0:8, :]
    best = jnp.maximum(top, new)
    carried = jnp.exp(top - best)
    own = jnp.exp(new - best)
    denominator = own + total * carried
    for g in range(groups):
        outs = []
        for row in range(2):
            c = g * 2 + row
            at = slice(c, c + 1)
            outs.append(
                (own[:, at] * token_ref[8 + c : 9 + c, :] + sums[c] * carried[:, at])
                / denominator[:, at]
            )
        for h in range(8):
            at = (g * 8 + h) * HEAD_SIZE
            out_ref[:, at : at + HEAD_SIZE] = jnp.concatenate(
                [outs[0][h : h + 1], outs[1][h : h + 1]], axis=0
            ).astype(bf16)


def shards(queries, fresh_key_value, key_value_pool, block_table, lengths):
    lenders = lax.axis_size("inst")
    pages = lax.axis_size("page")
    own_rows = queries.shape[0]
    slots, page_tok, width = key_value_pool.shape[1:]
    groups = width // HEAD_SIZE
    rows = groups * 16
    page_index = lax.axis_index("page").reshape(1).astype(jnp.int32)

    to_send = pl.pallas_call(
        functools.partial(send_kernel, slots, pages),
        out_shape=jax.ShapeDtypeStruct((lenders, rows + 8, HEAD_SIZE), bf16),
        in_specs=[pl.BlockSpec(memory_space=SMEM)] * 2 + vmem_specs(2),
        out_specs=pl.BlockSpec(memory_space=pl.ANY),
        scratch_shapes=[
            pltpu.VMEM((lenders, rows + 8, HEAD_SIZE), bf16),
            pltpu.SemaphoreType.DMA((2,)),
        ],
        name="send",
    )(page_index, lengths, queries, block_table)
    received = lax.all_to_all(to_send, "inst", 0, 0)

    keys, values = pl.pallas_call(
        token_major_kernel,
        out_shape=(
            jax.ShapeDtypeStruct((page_tok, slots, width), bf16),
            jax.ShapeDtypeStruct((page_tok, slots, width), bf16),
        ),
        in_specs=[pl.BlockSpec(memory_space=pl.ANY)],
        out_specs=(pl.BlockSpec(memory_space=VMEM), pl.BlockSpec(memory_space=pl.ANY)),
        scratch_shapes=[
            pltpu.VMEM(key_value_pool.shape, bf16),
            pltpu.VMEM((page_tok, slots, width), bf16),
            pltpu.SemaphoreType.DMA((2, PARTS)),
            pltpu.SemaphoreType.DMA((PARTS,)),
        ],
        cost_estimate=pl.CostEstimate(flops=10**9, bytes_accessed=2 * 4 * 2**20, transcendentals=0),
        compiler_params=pltpu.CompilerParams(vmem_limit_bytes=50 * 2**20),
        name="token_major",
    )(key_value_pool)

    partial, token = pl.pallas_call(
        attend_kernel,
        out_shape=(
            jax.ShapeDtypeStruct((lenders, rows + 8, HEAD_SIZE), jnp.int16),
            jax.ShapeDtypeStruct((16, HEAD_SIZE), f32),
        ),
        in_specs=vmem_specs(4) + [pl.BlockSpec(memory_space=pl.ANY)],
        out_specs=tuple(vmem_specs(2)),
        scratch_shapes=[
            pltpu.VMEM(values.shape, bf16),
            pltpu.VMEM((page_tok, groups * 8, slots), f32),
            pltpu.VMEM((page_tok, groups * 8, slots), f32),
            pltpu.SemaphoreType.DMA((2,)),
        ],
        compiler_params=pltpu.CompilerParams(vmem_limit_bytes=51 * 2**20),
        name="attend",
    )(received, keys, queries, fresh_key_value, values)
    parts = lax.all_to_all(partial, "inst", 0, 0)

    combined = pl.pallas_call(
        functools.partial(combine_kernel, groups),
        out_shape=jax.ShapeDtypeStruct((pages, rows + 8, HEAD_SIZE), jnp.int16),
        in_specs=vmem_specs(1),
        out_specs=pl.BlockSpec(memory_space=VMEM),
        compiler_params=pltpu.CompilerParams(vmem_limit_bytes=16 * 2**20),
        name="combine",
    )(parts)
    page_parts = lax.all_to_all(combined, "page", 0, 0)

    return pl.pallas_call(
        functools.partial(finish_kernel, groups),
        out_shape=jax.ShapeDtypeStruct(queries.shape, bf16),
        in_specs=vmem_specs(2),
        out_specs=pl.BlockSpec(memory_space=VMEM),
        compiler_params=pltpu.CompilerParams(vmem_limit_bytes=16 * 2**20),
        name="finish",
    )(page_parts, token)


def solution(mesh):
    return jax.shard_map(
        shards,
        mesh=mesh,
        in_specs=(
            P("inst", "head"),
            P(None, "inst", "head"),
            P(None, ("inst", "page"), None, "head"),
            P("inst", None),
            P("inst"),
        ),
        out_specs=P("inst", "head"),
        check_vma=False,
    )
```

```python
import functools
import math

import jax
import jax.numpy as jnp
from jax import lax
from jax.experimental import pallas as pl
from jax.experimental.pallas import tpu as pltpu
from jax.sharding import PartitionSpec as P

HEAD_SIZE = 128
LOWEST_SCORE = -1e30
SCALE = 1.0 / math.sqrt(HEAD_SIZE)
VMEM = pltpu.MemorySpace.VMEM
SMEM = pltpu.MemorySpace.SMEM
f32 = jnp.float32
bf16 = jnp.bfloat16


def nt_dot(a, b):
    return lax.dot_general(a, b, (((1,), (1,)), ((), ())), preferred_element_type=f32)


STEPS = 16.0
FULL = 32700.0
LOWEST_TOP = -32000.0
PART = 32767.0


def encode_rows(x):
    top = jnp.max(jnp.abs(x), axis=1, keepdims=True)
    k = jnp.ceil(jnp.log2(jnp.maximum(top, 2.0**-120)) * STEPS)
    code = jnp.round((x * jnp.exp2(k * (-1.0 / STEPS))) * FULL)
    return k, code.astype(jnp.int32).astype(jnp.int16)


def vmem_specs(n):
    return [pl.BlockSpec(memory_space=VMEM)] * n


def send_kernel(
    slots, pages, page_ref, lengths_ref, queries_ref, table_ref, out_hbm, out_ref, sems
):
    peers = out_hbm.shape[0]
    own_rows, most_pages = table_ref.shape
    heads = queries_ref.shape[1] // HEAD_SIZE
    page_tok = 16
    slot_bits = slots.bit_length() - 1
    page_bits = pages.bit_length() - 1
    sub = lax.broadcasted_iota(jnp.int32, (8, HEAD_SIZE), 0)
    pieces = []
    for g in range(heads // 8):
        pair = [jnp.zeros((8, HEAD_SIZE), f32)] * own_rows
        for head in range(8):
            at = (g * 8 + head) * HEAD_SIZE
            both = queries_ref[:, at : at + HEAD_SIZE].astype(f32)
            pair = [
                jnp.where(sub == head, both[row : row + 1, :], pair[row]) for row in range(own_rows)
            ]
        pieces += pair
    queries = jnp.concatenate(pieces, axis=0).astype(bf16)
    rows = own_rows * heads
    for peer in range(peers):
        out_ref[peer, 0:rows, :] = queries
    stores = [
        pltpu.make_async_copy(out_ref.at[:, at], out_hbm.at[:, at], sems.at[n])
        for n, at in enumerate((pl.ds(0, rows), pl.ds(rows, 8)))
    ]
    stores[0].start()
    column = lax.broadcasted_iota(jnp.int32, (1, most_pages), 1)
    lender_rows = lax.broadcasted_iota(jnp.int32, (peers, most_pages), 0)
    slot_rows = lax.broadcasted_iota(jnp.int32, (slots, most_pages), 0)
    fills = []
    for row in range(own_rows):
        entry = table_ref[row : row + 1, :]
        fill = jnp.clip(lengths_ref[row] - column * page_tok, 0, page_tok)
        here = ((entry >> slot_bits) & (pages - 1)) == page_ref[0]
        lender = jnp.where(here & (entry >= 0), entry >> (slot_bits + page_bits), -1)
        slot = entry & (slots - 1)
        a = jnp.where(lender_rows == lender, fill.astype(f32), 0.0).astype(bf16)
        b = jnp.where(slot_rows == slot, 1.0, 0.0).astype(bf16)
        fills.append(nt_dot(a, b))
    sub = lax.broadcasted_iota(jnp.int32, (8, slots), 0)
    for peer in range(peers):
        tile = jnp.zeros((8, slots), f32)
        for row in range(own_rows):
            tile = jnp.where(sub == row, fills[row][peer : peer + 1, :], tile)
        out_ref[peer, rows : rows + 8, :] = tile.astype(bf16)
    stores[1].start()
    for store in stores:
        store.wait()


def new_token(queries_ref, fresh_ref, token_ref):
    groups = fresh_ref.shape[2] // HEAD_SIZE
    sub = lax.broadcasted_iota(jnp.int32, (8, HEAD_SIZE), 0)
    lane = lax.broadcasted_iota(jnp.int32, (8, HEAD_SIZE), 1)
    fresh_k = fresh_ref[0].astype(f32)
    fresh_v = fresh_ref[1].astype(f32)
    scores = jnp.zeros((8, HEAD_SIZE), f32)
    values = jnp.zeros((8, HEAD_SIZE), f32)
    for g in range(groups):
        both = [
            queries_ref[:, (g * 8 + h) * HEAD_SIZE : (g * 8 + h + 1) * HEAD_SIZE].astype(f32)
            for h in range(8)
        ]
        for row in range(2):
            q = jnp.zeros((8, HEAD_SIZE), f32)
            for h in range(8):
                q = jnp.where(sub == h, both[h][row : row + 1, :], q)
            k = fresh_k[row : row + 1, g * HEAD_SIZE : (g + 1) * HEAD_SIZE]
            new = jnp.sum(q * k, axis=1, keepdims=True) * SCALE
            scores = jnp.where(lane == g * 2 + row, new, scores)
            v = fresh_v[row : row + 1, g * HEAD_SIZE : (g + 1) * HEAD_SIZE]
            values = jnp.where(sub == g * 2 + row, v, values)
    token_ref[0:8, :] = scores
    token_ref[8:16, :] = values


PARTS = 2


def token_major_kernel(
    pool_hbm, keys_ref, values_hbm, pool_ref, values_ref, load_sems, store_sems
):
    pages, page_tok, width = pool_hbm.shape[1:]
    chunk = pages // PARTS
    block = page_tok * 16
    loads = []
    stores = []
    for kind in (1, 0):
        for c in range(PARTS):
            at = pl.ds(c * chunk, chunk)
            loads.append(
                pltpu.make_async_copy(
                    pool_hbm.at[kind, at], pool_ref.at[kind, at], load_sems.at[kind, c]
                )
            )
            if kind == 1:
                stores.append(
                    pltpu.make_async_copy(
                        values_ref.at[:, at], values_hbm.at[:, at], store_sems.at[c]
                    )
                )
    for load in loads:
        load.start()
    i = lax.broadcasted_iota(jnp.int32, (block, block), 0)
    j = lax.broadcasted_iota(jnp.int32, (block, block), 1)
    perm = jnp.where((i % 16) * page_tok + i // 16 == j, 1.0, 0.0).astype(bf16)
    for kind in (1, 0):
        out_ref = values_ref if kind == 1 else keys_ref
        for c in range(PARTS):
            loads[(1 - kind) * PARTS + c].wait()
            for b in range(chunk // 16):
                first = c * chunk + b * 16
                rows = pool_ref[kind, first : first + 16].reshape(block, width)
                moved = jnp.dot(perm, rows, preferred_element_type=f32).astype(bf16)
                out_ref[:, first : first + 16, :] = moved.reshape(page_tok, 16, width)
            if kind == 1:
                stores[c].start()
    for store in stores:
        store.wait()


def attend_kernel(
    recv_ref,
    keys_ref,
    queries_ref,
    fresh_ref,
    values_hbm,
    out_ref,
    token_ref,
    values_ref,
    score_ref,
    weight_ref,
    sems,
):
    peers = recv_ref.shape[0]
    page_tok, slots, width = keys_ref.shape

    def load(i):
        at = pl.ds(i * (page_tok // 2), page_tok // 2)
        return pltpu.make_async_copy(values_hbm.at[at], values_ref.at[at], sems.at[i])

    def load_step(i, carry):
        load(i).start()
        return carry

    lax.fori_loop(0, 2, load_step, 0)
    groups = width // HEAD_SIZE
    requests = 2 * peers
    heads = groups * 8
    rows = groups * 16
    sub8 = lax.broadcasted_iota(jnp.int32, (8, slots), 0)
    fill = jnp.zeros((8, slots), f32)
    code = jnp.zeros((8, slots), f32)
    for peer in range(peers):
        tile = recv_ref[peer, rows : rows + 8, :].astype(f32)
        fill = fill + tile
        code = code + jnp.where(tile > 0.0, (sub8 + (2 * peer + 1)).astype(f32), 0.0)
    fill = jnp.broadcast_to(jnp.sum(fill, axis=0, keepdims=True), (8, slots))
    owner = jnp.broadcast_to(jnp.sum(code, axis=0, keepdims=True), (8, slots))

    def score_step(t, carry):
        live = fill > jnp.asarray(t, f32)
        for g in range(groups):
            q = recv_ref[:, g * 16 : (g + 1) * 16, :].reshape(requests * 8, HEAD_SIZE)
            k = keys_ref[t, :, g * HEAD_SIZE : (g + 1) * HEAD_SIZE]
            s = nt_dot(q, k)
            picked = jnp.zeros((8, slots), f32)
            for r in range(requests):
                picked = jnp.where(owner == float(r + 1), s[r * 8 : (r + 1) * 8], picked)
            score_ref[t, g * 8 : (g + 1) * 8, :] = jnp.where(live, picked * SCALE, LOWEST_SCORE)
        return carry

    lax.fori_loop(0, page_tok, score_step, 0, unroll=True)

    new_token(queries_ref, fresh_ref, token_ref)
    owner_h = jnp.broadcast_to(owner[0:1], (heads, slots))
    fill_h = jnp.broadcast_to(fill[0:1], (heads, slots))
    page_max = score_ref[0]
    for t in range(1, page_tok):
        page_max = jnp.maximum(page_max, score_ref[t])
    maxima = []
    owner_max = jnp.zeros((heads, slots), f32)
    for r in range(requests):
        mine = owner_h == float(r + 1)
        top = jnp.max(jnp.where(mine, page_max, LOWEST_TOP), axis=1, keepdims=True)
        top = jnp.round(jnp.maximum(top, LOWEST_TOP))
        maxima.append(top)
        owner_max = jnp.where(mine, top, owner_max)
    factor = jnp.exp(page_max - owner_max)
    page_sum = jnp.zeros((heads, slots), f32)
    sub16 = lax.broadcasted_iota(jnp.int32, (16, slots), 0)
    owner_16 = jnp.broadcast_to(owner[0:1], (16, slots))
    for t in range(page_tok):
        w = jnp.where(fill_h > float(t), jnp.exp(score_ref[t] - page_max), 0.0)
        page_sum = page_sum + w
        scaled = w.astype(bf16).astype(f32) * factor
        high = scaled.astype(bf16).astype(f32)
        score_ref[t] = high
        weight_ref[t] = scaled - high
    for i in range(2):
        load(i).wait()
    page_sum = page_sum * factor
    masks = [
        jnp.where(owner_16 == (2 * k + 1 + sub16 // 8).astype(f32), 1.0, 0.0).astype(bf16)
        for k in range(peers)
    ]
    totals = [
        jnp.sum(jnp.where(owner_h == float(r + 1), page_sum, 0.0), axis=1, keepdims=True)
        for r in range(requests)
    ]
    heads_of_stats = []
    for peer in range(peers):
        columns = []
        for g in range(groups):
            at = slice(g * 8, (g + 1) * 8)
            for r in (2 * peer, 2 * peer + 1):
                columns.append((maxima[r][at], totals[r][at]))
        heads_of_stats.append(stat_head(columns, LENDER_UNIT))
    scales = []
    for g in range(groups):
        acc = jnp.zeros((requests * 8, HEAD_SIZE), f32)
        for t0 in range(0, page_tok, 2):
            v = values_ref[t0 : t0 + 2, :, g * HEAD_SIZE : (g + 1) * HEAD_SIZE].reshape(
                2 * slots, HEAD_SIZE
            )
            for ref in (score_ref, weight_ref):
                cols = []
                for t in (t0, t0 + 1):
                    w8 = ref[t, g * 8 : (g + 1) * 8, :]
                    w16 = jnp.concatenate([w8, w8], axis=0).astype(bf16)
                    cols.append(jnp.concatenate([w16 * m for m in masks], axis=0))
                acc = acc + jnp.dot(
                    jnp.concatenate(cols, axis=1), v, preferred_element_type=f32
                )
        k, code = encode_rows(acc)
        scales.append(k)
        out_ref[:, g * 16 : (g + 1) * 16, :] = code.reshape(peers, 16, HEAD_SIZE)
    for peer in range(peers):
        columns = [
            scales[g][r * 8 : (r + 1) * 8]
            for g in range(groups)
            for r in (2 * peer, 2 * peer + 1)
        ]
        out_ref[peer, rows : rows + 8, :] = stat_tile(heads_of_stats[peer], columns)


LENDER_UNIT = 8.0
OWNER_UNIT = 1.0


def stat_head(columns, unit):
    tiles = len(columns)
    lane = lax.broadcasted_iota(jnp.int32, (8, HEAD_SIZE), 1)
    top = jnp.zeros((8, HEAD_SIZE), f32)
    total = top
    for c, (m, l) in enumerate(columns):
        top = jnp.where(lane == c, m, top)
        total = jnp.where((lane == tiles + c) | (lane == 2 * tiles + c), l, total)
    total = total * unit
    whole = jnp.floor(total)
    part = jnp.round((total - whole) * PART)
    return jnp.where(lane < tiles, top, jnp.where(lane < 2 * tiles, whole, part))


def stat_tile(tile, scales):
    lane = lax.broadcasted_iota(jnp.int32, (8, HEAD_SIZE), 1)
    for c, k in enumerate(scales):
        tile = jnp.where(lane == 3 * len(scales) + c, k, tile)
    return tile.astype(jnp.int32).astype(jnp.int16)


def merge(parts_ref, groups, unit):
    tiles = 2 * groups
    count = parts_ref.shape[0]
    stats = [
        parts_ref[i, tiles * 8 : tiles * 8 + 8, :].astype(jnp.int32).astype(f32)
        for i in range(count)
    ]
    top = stats[0]
    for s in stats[1:]:
        top = jnp.maximum(top, s)
    total = jnp.zeros_like(top)
    scales = []
    for s in stats:
        shifted = [pltpu.roll(s, HEAD_SIZE - n * tiles, axis=1) for n in (1, 2, 3)]
        e = jnp.exp(s - top)
        total = total + (shifted[0] + shifted[1] * (1.0 / PART)) * e
        scales.append(e * (jnp.exp2(shifted[2] * (1.0 / STEPS)) * (1.0 / FULL)))
    sums = []
    for g in range(groups):
        pair = [jnp.zeros((8, HEAD_SIZE), f32)] * 2
        for i in range(count):
            both = parts_ref[i, g * 16 : (g + 1) * 16, :].astype(jnp.int32).astype(f32)
            pair = [
                pair[n] + both[n * 8 : (n + 1) * 8] * scales[i][:, g * 2 + n : g * 2 + n + 1]
                for n in range(2)
            ]
        sums += pair
    return top, total * (1.0 / unit), sums


def combine_kernel(groups, parts_ref, out_ref):
    tiles = 2 * groups
    top, total, sums = merge(parts_ref, groups, LENDER_UNIT)
    coded = [encode_rows(jnp.concatenate(sums[2 * g : 2 * g + 2], axis=0)) for g in range(groups)]
    head = stat_head(
        [(top[:, c : c + 1], total[:, c : c + 1]) for c in range(tiles)], OWNER_UNIT
    )
    stat = stat_tile(
        head, [coded[c // 2][0][c % 2 * 8 : c % 2 * 8 + 8] for c in range(tiles)]
    )
    for i in range(out_ref.shape[0]):
        for g in range(groups):
            out_ref[i, g * 16 : (g + 1) * 16, :] = coded[g][1]
        out_ref[i, tiles * 8 : tiles * 8 + 8, :] = stat


def finish_kernel(groups, parts_ref, token_ref, out_ref):
    top, total, sums = merge(parts_ref, groups, OWNER_UNIT)
    new = token_ref[0:8, :]
    best = jnp.maximum(top, new)
    carried = jnp.exp(top - best)
    own = jnp.exp(new - best)
    denominator = own + total * carried
    for g in range(groups):
        outs = []
        for row in range(2):
            c = g * 2 + row
            at = slice(c, c + 1)
            outs.append(
                (own[:, at] * token_ref[8 + c : 9 + c, :] + sums[c] * carried[:, at])
                / denominator[:, at]
            )
        for h in range(8):
            at = (g * 8 + h) * HEAD_SIZE
            out_ref[:, at : at + HEAD_SIZE] = jnp.concatenate(
                [outs[0][h : h + 1], outs[1][h : h + 1]], axis=0
            ).astype(bf16)


def shards(queries, fresh_key_value, key_value_pool, block_table, lengths):
    lenders = lax.axis_size("inst")
    pages = lax.axis_size("page")
    own_rows = queries.shape[0]
    slots, page_tok, width = key_value_pool.shape[1:]
    groups = width // HEAD_SIZE
    rows = groups * 16
    page_index = lax.axis_index("page").reshape(1).astype(jnp.int32)

    to_send = pl.pallas_call(
        functools.partial(send_kernel, slots, pages),
        out_shape=jax.ShapeDtypeStruct((lenders, rows + 8, HEAD_SIZE), bf16),
        in_specs=[pl.BlockSpec(memory_space=SMEM)] * 2 + vmem_specs(2),
        out_specs=pl.BlockSpec(memory_space=pl.ANY),
        scratch_shapes=[
            pltpu.VMEM((lenders, rows + 8, HEAD_SIZE), bf16),
            pltpu.SemaphoreType.DMA((2,)),
        ],
        name="send",
    )(page_index, lengths, queries, block_table)
    received = lax.all_to_all(to_send, "inst", 0, 0)

    keys, values = pl.pallas_call(
        token_major_kernel,
        out_shape=(
            jax.ShapeDtypeStruct((page_tok, slots, width), bf16),
            jax.ShapeDtypeStruct((page_tok, slots, width), bf16),
        ),
        in_specs=[pl.BlockSpec(memory_space=pl.ANY)],
        out_specs=(pl.BlockSpec(memory_space=VMEM), pl.BlockSpec(memory_space=pl.ANY)),
        scratch_shapes=[
            pltpu.VMEM(key_value_pool.shape, bf16),
            pltpu.VMEM((page_tok, slots, width), bf16),
            pltpu.SemaphoreType.DMA((2, PARTS)),
            pltpu.SemaphoreType.DMA((PARTS,)),
        ],
        cost_estimate=pl.CostEstimate(flops=10**9, bytes_accessed=2 * 4 * 2**20, transcendentals=0),
        compiler_params=pltpu.CompilerParams(vmem_limit_bytes=50 * 2**20),
        name="token_major",
    )(key_value_pool)

    partial, token = pl.pallas_call(
        attend_kernel,
        out_shape=(
            jax.ShapeDtypeStruct((lenders, rows + 8, HEAD_SIZE), jnp.int16),
            jax.ShapeDtypeStruct((16, HEAD_SIZE), f32),
        ),
        in_specs=vmem_specs(4) + [pl.BlockSpec(memory_space=pl.ANY)],
        out_specs=tuple(vmem_specs(2)),
        scratch_shapes=[
            pltpu.VMEM(values.shape, bf16),
            pltpu.VMEM((page_tok, groups * 8, slots), f32),
            pltpu.VMEM((page_tok, groups * 8, slots), f32),
            pltpu.SemaphoreType.DMA((2,)),
        ],
        compiler_params=pltpu.CompilerParams(vmem_limit_bytes=51 * 2**20),
        name="attend",
    )(received, keys, queries, fresh_key_value, values)
    parts = lax.all_to_all(partial, "inst", 0, 0)

    combined = pl.pallas_call(
        functools.partial(combine_kernel, groups),
        out_shape=jax.ShapeDtypeStruct((pages, rows + 8, HEAD_SIZE), jnp.int16),
        in_specs=vmem_specs(1),
        out_specs=pl.BlockSpec(memory_space=VMEM),
        compiler_params=pltpu.CompilerParams(vmem_limit_bytes=16 * 2**20),
        name="combine",
    )(parts)
    page_parts = lax.all_to_all(combined, "page", 0, 0)

    return pl.pallas_call(
        functools.partial(finish_kernel, groups),
        out_shape=jax.ShapeDtypeStruct(queries.shape, bf16),
        in_specs=vmem_specs(2),
        out_specs=pl.BlockSpec(memory_space=VMEM),
        compiler_params=pltpu.CompilerParams(vmem_limit_bytes=16 * 2**20),
        name="finish",
    )(page_parts, token)


def solution(mesh):
    return jax.shard_map(
        shards,
        mesh=mesh,
        in_specs=(
            P("inst", "head"),
            P(None, "inst", "head"),
            P(None, ("inst", "page"), None, "head"),
            P("inst", None),
            P("inst"),
        ),
        out_specs=P("inst", "head"),
        check_vma=False,
    )
```

```python
import functools
import math

import jax
import jax.numpy as jnp
from jax import lax
from jax.experimental import pallas as pl
from jax.experimental.pallas import tpu as pltpu
from jax.sharding import PartitionSpec as P

HEAD_SIZE = 128
LOWEST_SCORE = -1e30
SCALE = 1.0 / math.sqrt(HEAD_SIZE)
VMEM = pltpu.MemorySpace.VMEM
SMEM = pltpu.MemorySpace.SMEM
f32 = jnp.float32
bf16 = jnp.bfloat16


def nt_dot(a, b):
    return lax.dot_general(a, b, (((1,), (1,)), ((), ())), preferred_element_type=f32)


STEPS = 16.0
FULL = 32700.0
LOWEST_TOP = -32000.0
PART = 32767.0


def encode_rows(x):
    top = jnp.max(jnp.abs(x), axis=1, keepdims=True)
    k = jnp.ceil(jnp.log2(jnp.maximum(top, 2.0**-120)) * STEPS)
    code = jnp.round((x * jnp.exp2(k * (-1.0 / STEPS))) * FULL)
    return k, code.astype(jnp.int32).astype(jnp.int16)


def vmem_specs(n):
    return [pl.BlockSpec(memory_space=VMEM)] * n


def send_kernel(
    slots, pages, lengths_ref, queries_ref, table_ref, out_hbm, out_ref, sems
):
    peers = out_hbm.shape[0]
    own_rows, most_pages = table_ref.shape
    heads = queries_ref.shape[1] // HEAD_SIZE
    page_tok = 16
    slot_bits = slots.bit_length() - 1
    page_bits = pages.bit_length() - 1
    sub = lax.broadcasted_iota(jnp.int32, (8, HEAD_SIZE), 0)
    pieces = []
    for g in range(heads // 8):
        pair = [jnp.zeros((8, HEAD_SIZE), f32)] * own_rows
        for head in range(8):
            at = (g * 8 + head) * HEAD_SIZE
            both = queries_ref[:, at : at + HEAD_SIZE].astype(f32)
            pair = [
                jnp.where(sub == head, both[row : row + 1, :], pair[row]) for row in range(own_rows)
            ]
        pieces += pair
    queries = jnp.concatenate(pieces, axis=0).astype(bf16)
    rows = own_rows * heads
    for peer in range(peers):
        out_ref[peer, 0:rows, :] = queries
    stores = [
        pltpu.make_async_copy(out_ref.at[:, at], out_hbm.at[:, at], sems.at[n])
        for n, at in enumerate((pl.ds(0, rows), pl.ds(rows, 8)))
    ]
    stores[0].start()
    column = lax.broadcasted_iota(jnp.int32, (1, most_pages), 1)
    lender_rows = lax.broadcasted_iota(jnp.int32, (peers, most_pages), 0)
    slot_rows = lax.broadcasted_iota(jnp.int32, (slots, most_pages), 0)
    fills = []
    for row in range(own_rows):
        entry = table_ref[row : row + 1, :]
        fill = jnp.clip(lengths_ref[row] - column * page_tok, 0, page_tok)
        here = ((entry >> slot_bits) & (pages - 1)) == lax.axis_index("page")
        lender = jnp.where(here & (entry >= 0), entry >> (slot_bits + page_bits), -1)
        slot = entry & (slots - 1)
        a = jnp.where(lender_rows == lender, fill.astype(f32), 0.0).astype(bf16)
        b = jnp.where(slot_rows == slot, 1.0, 0.0).astype(bf16)
        fills.append(nt_dot(a, b))
    sub = lax.broadcasted_iota(jnp.int32, (8, slots), 0)
    for peer in range(peers):
        tile = jnp.zeros((8, slots), f32)
        for row in range(own_rows):
            tile = jnp.where(sub == row, fills[row][peer : peer + 1, :], tile)
        out_ref[peer, rows : rows + 8, :] = tile.astype(bf16)
    stores[1].start()
    for store in stores:
        store.wait()


def new_token(queries_ref, fresh_ref, token_ref):
    groups = fresh_ref.shape[2] // HEAD_SIZE
    sub = lax.broadcasted_iota(jnp.int32, (8, HEAD_SIZE), 0)
    lane = lax.broadcasted_iota(jnp.int32, (8, HEAD_SIZE), 1)
    fresh_k = fresh_ref[0].astype(f32)
    fresh_v = fresh_ref[1].astype(f32)
    scores = jnp.zeros((8, HEAD_SIZE), f32)
    values = jnp.zeros((8, HEAD_SIZE), f32)
    for g in range(groups):
        both = [
            queries_ref[:, (g * 8 + h) * HEAD_SIZE : (g * 8 + h + 1) * HEAD_SIZE].astype(f32)
            for h in range(8)
        ]
        for row in range(2):
            q = jnp.zeros((8, HEAD_SIZE), f32)
            for h in range(8):
                q = jnp.where(sub == h, both[h][row : row + 1, :], q)
            k = fresh_k[row : row + 1, g * HEAD_SIZE : (g + 1) * HEAD_SIZE]
            new = jnp.sum(q * k, axis=1, keepdims=True) * SCALE
            scores = jnp.where(lane == g * 2 + row, new, scores)
            v = fresh_v[row : row + 1, g * HEAD_SIZE : (g + 1) * HEAD_SIZE]
            values = jnp.where(sub == g * 2 + row, v, values)
    token_ref[0:8, :] = scores
    token_ref[8:16, :] = values


PARTS = 2


def token_major_kernel(
    pool_hbm, keys_ref, values_hbm, pool_ref, values_ref, load_sems, store_sems
):
    pages, page_tok, width = pool_hbm.shape[1:]
    chunk = pages // PARTS
    block = page_tok * 16
    loads = []
    stores = []
    for kind in (1, 0):
        for c in range(PARTS):
            at = pl.ds(c * chunk, chunk)
            loads.append(
                pltpu.make_async_copy(
                    pool_hbm.at[kind, at], pool_ref.at[kind, at], load_sems.at[kind, c]
                )
            )
            if kind == 1:
                stores.append(
                    pltpu.make_async_copy(
                        values_ref.at[:, at], values_hbm.at[:, at], store_sems.at[c]
                    )
                )
    for load in loads:
        load.start()
    i = lax.broadcasted_iota(jnp.int32, (block, block), 0)
    j = lax.broadcasted_iota(jnp.int32, (block, block), 1)
    perm = jnp.where((i % 16) * page_tok + i // 16 == j, 1.0, 0.0).astype(bf16)
    for kind in (1, 0):
        out_ref = values_ref if kind == 1 else keys_ref
        for c in range(PARTS):
            loads[(1 - kind) * PARTS + c].wait()
            for b in range(chunk // 16):
                first = c * chunk + b * 16
                rows = pool_ref[kind, first : first + 16].reshape(block, width)
                moved = jnp.dot(perm, rows, preferred_element_type=f32).astype(bf16)
                out_ref[:, first : first + 16, :] = moved.reshape(page_tok, 16, width)
            if kind == 1:
                stores[c].start()
    for store in stores:
        store.wait()


def attend_kernel(
    recv_ref,
    keys_ref,
    queries_ref,
    fresh_ref,
    values_hbm,
    out_ref,
    token_ref,
    values_ref,
    score_ref,
    weight_ref,
    sems,
):
    peers = recv_ref.shape[0]
    page_tok, slots, width = keys_ref.shape

    def load(i):
        at = pl.ds(i * (page_tok // 2), page_tok // 2)
        return pltpu.make_async_copy(values_hbm.at[at], values_ref.at[at], sems.at[i])

    def load_step(i, carry):
        load(i).start()
        return carry

    lax.fori_loop(0, 2, load_step, 0)
    groups = width // HEAD_SIZE
    requests = 2 * peers
    heads = groups * 8
    rows = groups * 16
    sub8 = lax.broadcasted_iota(jnp.int32, (8, slots), 0)
    fill = jnp.zeros((8, slots), f32)
    code = jnp.zeros((8, slots), f32)
    for peer in range(peers):
        tile = recv_ref[peer, rows : rows + 8, :].astype(f32)
        fill = fill + tile
        code = code + jnp.where(tile > 0.0, (sub8 + (2 * peer + 1)).astype(f32), 0.0)
    fill = jnp.broadcast_to(jnp.sum(fill, axis=0, keepdims=True), (8, slots))
    owner = jnp.broadcast_to(jnp.sum(code, axis=0, keepdims=True), (8, slots))

    def score_step(t, carry):
        live = fill > jnp.asarray(t, f32)
        for g in range(groups):
            q = recv_ref[:, g * 16 : (g + 1) * 16, :].reshape(requests * 8, HEAD_SIZE)
            k = keys_ref[t, :, g * HEAD_SIZE : (g + 1) * HEAD_SIZE]
            s = nt_dot(q, k)
            picked = jnp.zeros((8, slots), f32)
            for r in range(requests):
                picked = jnp.where(owner == float(r + 1), s[r * 8 : (r + 1) * 8], picked)
            score_ref[t, g * 8 : (g + 1) * 8, :] = jnp.where(live, picked * SCALE, LOWEST_SCORE)
        return carry

    lax.fori_loop(0, page_tok, score_step, 0, unroll=True)

    new_token(queries_ref, fresh_ref, token_ref)
    owner_h = jnp.broadcast_to(owner[0:1], (heads, slots))
    fill_h = jnp.broadcast_to(fill[0:1], (heads, slots))
    page_max = score_ref[0]
    for t in range(1, page_tok):
        page_max = jnp.maximum(page_max, score_ref[t])
    maxima = []
    owner_max = jnp.zeros((heads, slots), f32)
    for r in range(requests):
        mine = owner_h == float(r + 1)
        top = jnp.max(jnp.where(mine, page_max, LOWEST_TOP), axis=1, keepdims=True)
        top = jnp.round(jnp.maximum(top, LOWEST_TOP))
        maxima.append(top)
        owner_max = jnp.where(mine, top, owner_max)
    factor = jnp.exp(page_max - owner_max)
    page_sum = jnp.zeros((heads, slots), f32)
    sub16 = lax.broadcasted_iota(jnp.int32, (16, slots), 0)
    owner_16 = jnp.broadcast_to(owner[0:1], (16, slots))
    for t in range(page_tok):
        w = jnp.where(fill_h > float(t), jnp.exp(score_ref[t] - page_max), 0.0)
        page_sum = page_sum + w
        scaled = w.astype(bf16).astype(f32) * factor
        high = scaled.astype(bf16).astype(f32)
        score_ref[t] = high
        weight_ref[t] = scaled - high
    for i in range(2):
        load(i).wait()
    page_sum = page_sum * factor
    masks = [
        jnp.where(owner_16 == (2 * k + 1 + sub16 // 8).astype(f32), 1.0, 0.0).astype(bf16)
        for k in range(peers)
    ]
    totals = [
        jnp.sum(jnp.where(owner_h == float(r + 1), page_sum, 0.0), axis=1, keepdims=True)
        for r in range(requests)
    ]
    scales = []
    for g in range(groups):
        acc = jnp.zeros((requests * 8, HEAD_SIZE), f32)
        for t0 in range(0, page_tok, 2):
            v = values_ref[t0 : t0 + 2, :, g * HEAD_SIZE : (g + 1) * HEAD_SIZE].reshape(
                2 * slots, HEAD_SIZE
            )
            for ref in (score_ref, weight_ref):
                cols = []
                for t in (t0, t0 + 1):
                    w8 = ref[t, g * 8 : (g + 1) * 8, :]
                    w16 = jnp.concatenate([w8, w8], axis=0).astype(bf16)
                    cols.append(jnp.concatenate([w16 * m for m in masks], axis=0))
                acc = acc + jnp.dot(
                    jnp.concatenate(cols, axis=1), v, preferred_element_type=f32
                )
        k, code = encode_rows(acc)
        scales.append(k)
        out_ref[:, g * 16 : (g + 1) * 16, :] = code.reshape(peers, 16, HEAD_SIZE)
    for peer in range(peers):
        columns = []
        for g in range(groups):
            for row in range(2):
                r = 2 * peer + row
                at = slice(g * 8, (g + 1) * 8)
                columns.append((maxima[r][at], totals[r][at], scales[g][r * 8 : (r + 1) * 8]))
        out_ref[peer, rows : rows + 8, :] = stat_tile(columns, LENDER_UNIT)


LENDER_UNIT = 8.0
OWNER_UNIT = 1.0


def stat_tile(columns, unit):
    tiles = len(columns)
    lane = lax.broadcasted_iota(jnp.int32, (8, HEAD_SIZE), 1)
    top = jnp.zeros((8, HEAD_SIZE), f32)
    total = top
    scale = top
    for c, (m, l, k) in enumerate(columns):
        top = jnp.where(lane == c, m, top)
        total = jnp.where((lane == tiles + c) | (lane == 2 * tiles + c), l, total)
        scale = jnp.where(lane == 3 * tiles + c, k, scale)
    total = total * unit
    whole = jnp.floor(total)
    part = jnp.round((total - whole) * PART)
    tile = jnp.where(lane < tiles, top, jnp.where(lane < 2 * tiles, whole, part))
    tile = jnp.where(lane < 3 * tiles, tile, scale)
    return tile.astype(jnp.int32).astype(jnp.int16)


def merge(parts_ref, groups, unit):
    tiles = 2 * groups
    count = parts_ref.shape[0]
    stats = [
        parts_ref[i, tiles * 8 : tiles * 8 + 8, :].astype(jnp.int32).astype(f32)
        for i in range(count)
    ]
    top = stats[0]
    for s in stats[1:]:
        top = jnp.maximum(top, s)
    total = jnp.zeros_like(top)
    scales = []
    for s in stats:
        shifted = [pltpu.roll(s, HEAD_SIZE - n * tiles, axis=1) for n in (1, 2, 3)]
        e = jnp.exp(s - top)
        total = total + (shifted[0] + shifted[1] * (1.0 / PART)) * e
        scales.append(e * (jnp.exp2(shifted[2] * (1.0 / STEPS)) * (1.0 / FULL)))
    sums = []
    for g in range(groups):
        pair = [jnp.zeros((8, HEAD_SIZE), f32)] * 2
        for i in range(count):
            both = parts_ref[i, g * 16 : (g + 1) * 16, :].astype(jnp.int32).astype(f32)
            pair = [
                pair[n] + both[n * 8 : (n + 1) * 8] * scales[i][:, g * 2 + n : g * 2 + n + 1]
                for n in range(2)
            ]
        sums += pair
    return top, total * (1.0 / unit), sums


def combine_kernel(groups, parts_ref, out_ref):
    tiles = 2 * groups
    top, total, sums = merge(parts_ref, groups, LENDER_UNIT)
    coded = [encode_rows(jnp.concatenate(sums[2 * g : 2 * g + 2], axis=0)) for g in range(groups)]
    columns = [
        (top[:, c : c + 1], total[:, c : c + 1], coded[c // 2][0][c % 2 * 8 : c % 2 * 8 + 8])
        for c in range(tiles)
    ]
    stat = stat_tile(columns, OWNER_UNIT)
    for i in range(out_ref.shape[0]):
        for g in range(groups):
            out_ref[i, g * 16 : (g + 1) * 16, :] = coded[g][1]
        out_ref[i, tiles * 8 : tiles * 8 + 8, :] = stat


def finish_kernel(groups, parts_ref, token_ref, out_ref):
    top, total, sums = merge(parts_ref, groups, OWNER_UNIT)
    new = token_ref[0:8, :]
    best = jnp.maximum(top, new)
    carried = jnp.exp(top - best)
    own = jnp.exp(new - best)
    denominator = own + total * carried
    for g in range(groups):
        outs = []
        for row in range(2):
            c = g * 2 + row
            at = slice(c, c + 1)
            outs.append(
                (own[:, at] * token_ref[8 + c : 9 + c, :] + sums[c] * carried[:, at])
                / denominator[:, at]
            )
        for h in range(8):
            at = (g * 8 + h) * HEAD_SIZE
            out_ref[:, at : at + HEAD_SIZE] = jnp.concatenate(
                [outs[0][h : h + 1], outs[1][h : h + 1]], axis=0
            ).astype(bf16)


def shards(queries, fresh_key_value, key_value_pool, block_table, lengths):
    lenders = lax.axis_size("inst")
    pages = lax.axis_size("page")
    own_rows = queries.shape[0]
    slots, page_tok, width = key_value_pool.shape[1:]
    groups = width // HEAD_SIZE
    rows = groups * 16

    to_send = pl.pallas_call(
        functools.partial(send_kernel, slots, pages),
        out_shape=jax.ShapeDtypeStruct((lenders, rows + 8, HEAD_SIZE), bf16),
        in_specs=[pl.BlockSpec(memory_space=SMEM)] + vmem_specs(2),
        out_specs=pl.BlockSpec(memory_space=pl.ANY),
        scratch_shapes=[
            pltpu.VMEM((lenders, rows + 8, HEAD_SIZE), bf16),
            pltpu.SemaphoreType.DMA((2,)),
        ],
        name="send",
    )(lengths, queries, block_table)
    received = lax.all_to_all(to_send, "inst", 0, 0)

    keys, values = pl.pallas_call(
        token_major_kernel,
        out_shape=(
            jax.ShapeDtypeStruct((page_tok, slots, width), bf16),
            jax.ShapeDtypeStruct((page_tok, slots, width), bf16),
        ),
        in_specs=[pl.BlockSpec(memory_space=pl.ANY)],
        out_specs=(pl.BlockSpec(memory_space=VMEM), pl.BlockSpec(memory_space=pl.ANY)),
        scratch_shapes=[
            pltpu.VMEM(key_value_pool.shape, bf16),
            pltpu.VMEM((page_tok, slots, width), bf16),
            pltpu.SemaphoreType.DMA((2, PARTS)),
            pltpu.SemaphoreType.DMA((PARTS,)),
        ],
        cost_estimate=pl.CostEstimate(flops=10**9, bytes_accessed=2 * 4 * 2**20, transcendentals=0),
        compiler_params=pltpu.CompilerParams(vmem_limit_bytes=50 * 2**20),
        name="token_major",
    )(key_value_pool)

    partial, token = pl.pallas_call(
        attend_kernel,
        out_shape=(
            jax.ShapeDtypeStruct((lenders, rows + 8, HEAD_SIZE), jnp.int16),
            jax.ShapeDtypeStruct((16, HEAD_SIZE), f32),
        ),
        in_specs=vmem_specs(4) + [pl.BlockSpec(memory_space=pl.ANY)],
        out_specs=tuple(vmem_specs(2)),
        scratch_shapes=[
            pltpu.VMEM(values.shape, bf16),
            pltpu.VMEM((page_tok, groups * 8, slots), f32),
            pltpu.VMEM((page_tok, groups * 8, slots), f32),
            pltpu.SemaphoreType.DMA((2,)),
        ],
        compiler_params=pltpu.CompilerParams(vmem_limit_bytes=51 * 2**20),
        name="attend",
    )(received, keys, queries, fresh_key_value, values)
    parts = lax.all_to_all(partial, "inst", 0, 0)

    combined = pl.pallas_call(
        functools.partial(combine_kernel, groups),
        out_shape=jax.ShapeDtypeStruct((pages, rows + 8, HEAD_SIZE), jnp.int16),
        in_specs=vmem_specs(1),
        out_specs=pl.BlockSpec(memory_space=VMEM),
        compiler_params=pltpu.CompilerParams(vmem_limit_bytes=16 * 2**20),
        name="combine",
    )(parts)
    page_parts = lax.all_to_all(combined, "page", 0, 0)

    return pl.pallas_call(
        functools.partial(finish_kernel, groups),
        out_shape=jax.ShapeDtypeStruct(queries.shape, bf16),
        in_specs=vmem_specs(2),
        out_specs=pl.BlockSpec(memory_space=VMEM),
        compiler_params=pltpu.CompilerParams(vmem_limit_bytes=16 * 2**20),
        name="finish",
    )(page_parts, token)


def solution(mesh):
    return jax.shard_map(
        shards,
        mesh=mesh,
        in_specs=(
            P("inst", "head"),
            P(None, "inst", "head"),
            P(None, ("inst", "page"), None, "head"),
            P("inst", None),
            P("inst"),
        ),
        out_specs=P("inst", "head"),
        check_vma=False,
    )
```
